32 devices in a mesh: rows: 16 (over z, x, core), seq: 2 (over y).
Axes of the slice: x: 2, y: 2, z: 4, core: 2. Of those that a mesh axis runs over, the one named last changes fastest.
Arguments:
- tokens: bfloat16 [64, 512, 768], P('rows', 'seq'), may hold values from -6 to 6
- lengths: int32 [64], P('rows'), may hold values from 42 to 512, as said below
- key_mask: int32 [64, 512], P('rows'), may hold values from 0 to 1, as said below
- cotangent: bfloat16 [64, 256, 768], P('rows', 'seq'), may hold values from -6 to 6
- w_qkv: bfloat16 [2, 3, 768, 768], replicated, may hold values from -0.21875 to 0.21875
- w_out: bfloat16 [2, 768, 768], replicated, may hold values from -0.75 to 0.75
- w_pos: bfloat16 [2, 768, 768], replicated, may hold values from -0.21875 to 0.21875
- w_up: bfloat16 [2, 768, 3072], replicated, may hold values from -0.21875 to 0.21875
- w_down: bfloat16 [2, 3072, 768], replicated, may hold values from -0.109375 to 0.109375
- attn_bias: float32 [2, 2, 768], replicated, may hold values from -3 to 3
- up_bias: float32 [2, 3072], replicated, may hold values from -3 to 3
- norm_gain: float32 [2, 2, 768], replicated, may hold values from 0.5 to 1.5
- norm_bias: float32 [2, 2, 768], replicated, may hold values from -2 to 2
- out_bias: float32 [2, 2, 768], replicated, may hold values from -3 to 3
Outputs:
- layer_out: bfloat16 [64, 256, 768], P('rows', 'seq')
- tokens_grad: float32 [64, 512, 768], P('rows', 'seq')
- grad_w_qkv: float32 [2, 3, 768, 768], P(None, None, 'rows')
- grad_w_out: float32 [2, 768, 768], P(None, 'rows')
- grad_w_pos: float32 [2, 768, 768], P(None, 'rows')
- grad_w_up: float32 [2, 768, 3072], P(None, 'rows')
- grad_w_down: float32 [2, 3072, 768], P(None, 'rows')
- grad_attn_bias: float32 [2, 2, 768], P(None, None, 'rows')
- grad_up_bias: float32 [2, 3072], P(None, 'rows')
- grad_norm_gain: float32 [2, 2, 768], P(None, None, 'rows')
- grad_norm_bias: float32 [2, 2, 768], P(None, None, 'rows')
- grad_out_bias: float32 [2, 2, 768], P(None, None, 'rows')
The draws below stay inside these ranges and needn't reach their ends.
Inputs may be any that keep to these rules, and one draw needn't show every extreme that they name: `lengths`: among the 4 sequences of one index of rows, one has length 512. `key_mask`: position 0 of every sequence is 1.
All inputs are finite; a program needn't handle non-finite values.
Results may differ from the reference program's by a relative error of at most 0.025.
Values may be sent and summed in bfloat16 or wider, within the bound.
A program may use at most 320 MiB of HBM per device.

```python
import jax
import jax.numpy as jnp
from jax import lax

D = 768
HEADS = 12
HEAD_DIM = 64
FF = 3072
SEQ_LEN = 512
SEQ_DEV = 4
SEQS = 64


def draw_lengths(key, part):
    shortest = max(2, SEQ_LEN // 12)
    base_len = jax.random.randint(jax.random.fold_in(key, 11), (SEQS,), shortest, SEQ_LEN + 1)
    chosen = jax.random.randint(jax.random.fold_in(key, 12), (SEQS // SEQ_DEV, 1), 0, SEQ_DEV)
    full_row = jnp.arange(SEQ_DEV, dtype=jnp.int32)[None, :] == chosen
    return jnp.where(full_row.reshape(SEQS), SEQ_LEN, base_len).astype(jnp.int32)


def draw_key_mask(key, part):
    coins = jax.random.randint(jax.random.fold_in(key, 21), (SEQS, SEQ_LEN), 0, 8)
    kept_mask = jnp.where(coins < 7, 1, 0).astype(jnp.int32)
    return kept_mask.at[:, 0].set(1)


def levels(key, shape, pieces, least, high):
    level = 1.0
    for axis_at, blocks in pieces:
        steps = jax.random.uniform(jax.random.fold_in(jax.random.fold_in(key, 6), axis_at), (blocks,), jnp.float32, least / len(pieces), high / len(pieces))
        level = level * jnp.repeat(jnp.exp(steps), shape[axis_at] // blocks).reshape((-1,) + (1,) * (len(shape) - 1 - axis_at))
    return level


def noise(own_key, dims, spread, reach, shards=(), kind=jnp.bfloat16):
    array = jax.random.normal(own_key, dims, jnp.float32) * spread
    if len(shards) > 0:
        array = levels(own_key, dims, shards, -0.22, 0.18) * array
    return jnp.clip(array, min=-reach, max=reach).astype(kind)


def setup_inputs(seed: int = 0) -> dict:
    keys = jax.random.split(jax.random.key(seed), 15)
    return {
        "tokens": noise(keys[0], (SEQS, SEQ_LEN, D), 1.0, 6.0, ((0, 16), (1, 2))),
        "lengths": draw_lengths(jax.random.fold_in(keys[14], 71), 0),
        "key_mask": draw_key_mask(jax.random.fold_in(keys[14], 71), 0),
        "cotangent": noise(keys[3], (SEQS, SEQ_LEN // 2, D), 1.0, 6.0, ((0, 16), (1, 2))),
        "w_qkv": noise(keys[4], (2, 3, D, D), D ** -0.5, 0.21875),
        "w_out": noise(keys[5], (2, D, D), (D // 12) ** -0.5, 0.75),
        "w_pos": noise(keys[6], (2, D, D), D ** -0.5, 0.21875),
        "w_up": noise(keys[7], (2, D, FF), D ** -0.5, 0.21875),
        "w_down": noise(keys[8], (2, FF, D), FF ** -0.5, 0.109375),
        "attn_bias": noise(keys[9], (2, 2, D), 0.5, 3.0, (), jnp.float32),
        "up_bias": noise(keys[10], (2, FF), 0.5, 3.0, (), jnp.float32),
        "norm_gain": jnp.clip(1.0 + 0.1 * jax.random.normal(keys[11], (2, 2, D), jnp.float32), 0.5, 1.5),
        "norm_bias": noise(keys[12], (2, 2, D), 0.3, 2.0, (), jnp.float32),
        "out_bias": noise(keys[13], (2, 2, D), 0.5, 3.0, (), jnp.float32),
    }


epsilon = 1e-06
masked_score = -1000000000.0
highest = lax.Precision.HIGHEST

@jax.custom_vjp
def low(v):
    return lax.optimization_barrier(v.astype(jnp.bfloat16)).astype(jnp.float32)

@jax.custom_vjp
def low_back(v):
    return v

def low_keep(v):
    return (low(v), None)

def low_pass(kept, grad):
    return (grad,)

def back_keep(v):
    return (v, None)

def back_low(kept, grad):
    return (low(grad),)
low.defvjp(low_keep, low_pass)
low_back.defvjp(back_keep, back_low)

def sinusoid(distance):
    half_width = D // 2
    frequency = 10000.0 ** (-jnp.arange(half_width, dtype=jnp.float32) / half_width)
    angles = distance.astype(jnp.float32)[:, None] * frequency[None, :]
    return jnp.concatenate([jnp.sin(angles), jnp.cos(angles)], axis=1)

def layer_norm(values, scale_gain, shift_bias):
    center = values - lax.optimization_barrier(jnp.mean(values, axis=-1, keepdims=True))
    variance = lax.optimization_barrier(jnp.mean(center * center, axis=-1, keepdims=True))
    return center * lax.rsqrt(variance + epsilon) * scale_gain + shift_bias

def attention_layer(residual, query_in, key_in, key_valid, stride, dist_unit, weights, layer_id):
    w_qkv, w_out, w_pos, w_up, w_down, attn_bias, up_bias, norm_gain, norm_bias, out_bias = weights
    seq_sets, query_len, model_width = query_in.shape
    key_len = key_in.shape[1]
    queries = low_back(jnp.matmul(query_in, w_qkv[layer_id, 0], precision=highest))
    keys_low = low(low_back(jnp.matmul(key_in, w_qkv[layer_id, 1], precision=highest)))
    values_low = low(low_back(jnp.matmul(key_in, w_qkv[layer_id, 2], precision=highest)))
    query_w = low(queries + attn_bias[layer_id, 0])
    query_r = low(queries + attn_bias[layer_id, 1])
    top_dist = stride * (query_len - 1)
    table_len = top_dist + key_len
    distance = (top_dist - jnp.arange(table_len, dtype=jnp.int32)) * dist_unit
    encoding = low(sinusoid(distance))
    pos_table = low(jnp.matmul(encoding, w_pos[layer_id], precision=highest))
    head_q = query_w.reshape(seq_sets, query_len, HEADS, HEAD_DIM)
    head_r = query_r.reshape(seq_sets, query_len, HEADS, HEAD_DIM)
    head_k = keys_low.reshape(seq_sets, key_len, HEADS, HEAD_DIM)
    head_v = values_low.reshape(seq_sets, key_len, HEADS, HEAD_DIM)
    table_heads = pos_table.reshape(table_len, HEADS, HEAD_DIM)
    content = jnp.einsum('bihc,bjhc->bhij', head_q, head_k, precision=highest)
    relative = jnp.einsum('bihc,rhc->bhir', head_r, table_heads, precision=highest)
    row_ids = jnp.arange(query_len, dtype=jnp.int32)[:, None]
    col_ids = jnp.arange(key_len, dtype=jnp.int32)[None, :]
    table_index = stride * (query_len - 1 - row_ids) + col_ids
    position = relative[:, :, row_ids, table_index]
    scores = low_back((content + position) * HEAD_DIM ** (-0.5))
    scores = jnp.where(key_valid[:, None, None, :] > 0, scores, masked_score)
    top_score = lax.optimization_barrier(jnp.max(scores, axis=-1, keepdims=True))
    exp_terms = jnp.exp(scores - top_score)
    attn_prob = low(exp_terms / lax.optimization_barrier(jnp.sum(exp_terms, axis=-1, keepdims=True)))
    mixed_heads = jnp.einsum('bhij,bjhc->bihc', attn_prob, head_v, precision=highest).reshape(seq_sets, query_len, model_width)
    mixed_low = low(low_back(mixed_heads))
    branch = low_back(jnp.matmul(mixed_low, w_out[layer_id], precision=highest) + out_bias[layer_id, 0])
    hidden = layer_norm(residual + branch, norm_gain[layer_id, 0], norm_bias[layer_id, 0])
    hidden_low = low(hidden)
    pre_act = low_back(jnp.matmul(hidden_low, w_up[layer_id], precision=highest) + up_bias[layer_id])
    act_low = low(jax.nn.gelu(pre_act, approximate=True))
    ffn_out = low_back(jnp.matmul(act_low, w_down[layer_id], precision=highest) + out_bias[layer_id, 1])
    return layer_norm(hidden + ffn_out, norm_gain[layer_id, 1], norm_bias[layer_id, 1])

def forward(token_values, valid_group, pooled_group, weight_set):
    seq_sets = token_values.shape[0]
    shifted = jnp.concatenate([token_values[:, :1], token_values[:, :-1]], axis=1)
    pooled = lax.optimization_barrier(jnp.mean(shifted.reshape(seq_sets, SEQ_LEN // 2, 2, D), axis=2))
    first_out = attention_layer(pooled, low(pooled), token_values, valid_group, 2, 1, weight_set, 0)
    first_low = low(first_out)
    return attention_layer(first_out, first_low, first_low, pooled_group, 1, 2, weight_set, 1)

def reference(tokens, lengths, key_mask, cotangent, w_qkv, w_out, w_pos, w_up, w_down, attn_bias, up_bias, norm_gain, norm_bias, out_bias):
    weights = (w_qkv.astype(jnp.float32), w_out.astype(jnp.float32), w_pos.astype(jnp.float32), w_up.astype(jnp.float32), w_down.astype(jnp.float32), attn_bias.astype(jnp.float32), up_bias.astype(jnp.float32), norm_gain.astype(jnp.float32), norm_bias.astype(jnp.float32), out_bias.astype(jnp.float32))
    places = jnp.arange(SEQ_LEN, dtype=jnp.int32)[None, :]
    key_valid = jnp.where(places < lengths[:, None], key_mask, 0)
    shifted_valid = jnp.concatenate([key_valid[:, :1], key_valid[:, :-1]], axis=1)
    pooled_valid = lax.optimization_barrier(jnp.max(shifted_valid.reshape(SEQS, SEQ_LEN // 2, 2), axis=2))
    groups = SEQS // SEQ_DEV
    stacked = (tokens.reshape(groups, SEQ_DEV, SEQ_LEN, D), key_valid.reshape(groups, SEQ_DEV, SEQ_LEN), pooled_valid.reshape(groups, SEQ_DEV, SEQ_LEN // 2), cotangent.reshape(groups, SEQ_DEV, SEQ_LEN // 2, D))

    def one_group(running, inputs):
        token_group, valid_group, pooled_group, cot_group = inputs

        def closure(token_values, weight_set):
            return forward(token_values, valid_group, pooled_group, weight_set)
        result, pullback = jax.vjp(closure, token_group.astype(jnp.float32), weights)
        token_grad, weight_grads = pullback(cot_group.astype(jnp.float32))
        running = jax.tree.map(jnp.add, running, weight_grads)
        return (running, (result.astype(jnp.bfloat16), token_grad))
    start_sums = jax.tree.map(jnp.zeros_like, weights)
    grad_sums, (outputs, token_grads) = lax.scan(one_group, start_sums, stacked)
    return (outputs.reshape(SEQS, SEQ_LEN // 2, D), token_grads.reshape(SEQS, SEQ_LEN, D), grad_sums[0], grad_sums[1], grad_sums[2], grad_sums[3], grad_sums[4], grad_sums[5], grad_sums[6], grad_sums[7], grad_sums[8], grad_sums[9])
```

```python
import functools

import jax
import jax.numpy as jnp
from jax import lax
from jax.experimental import pallas as pl
from jax.experimental.pallas import tpu as pltpu
from jax.sharding import PartitionSpec as P

D = 768
HEADS = 12
HEAD_DIM = 64
FF = 3072
PANELS = FF // D
HALF = D // 2
EPS = 1e-06
MASKED = -1000000000.0
SCALE = HEAD_DIM ** (-0.5)
BF = jnp.bfloat16
F32 = jnp.float32
MIB = 1 << 20

SHARDS = 16
UP_ROWS = PANELS * D // SHARDS
ROW = D // SHARDS


def mm(a, b):
    return lax.dot_general(a, b, (((1,), (0,)), ((), ())), preferred_element_type=F32)


def mm_nt(a, b):
    return lax.dot_general(a, b, (((1,), (1,)), ((), ())), preferred_element_type=F32)


def mm_tn(a, b):
    return lax.dot_general(a, b, (((0,), (0,)), ((), ())), preferred_element_type=F32)


def ln_fwd(z):
    center = z - jnp.mean(z, axis=-1, keepdims=True)
    var = jnp.mean(center * center, axis=-1, keepdims=True)
    rstd = lax.rsqrt(var + EPS)
    return center * rstd, rstd


def ln_bwd(dy, xhat, rstd, gain):
    dx = dy * gain
    m1 = jnp.mean(dx, axis=-1, keepdims=True)
    m2 = jnp.mean(dx * xhat, axis=-1, keepdims=True)
    return rstd * (dx - m1 - xhat * m2)


GELU_K = 0.7978845608028654
GELU_C = 0.044715


def gelu_and_slope(z):
    z2 = z * z
    t = jnp.tanh(GELU_K * z * (1.0 + GELU_C * z2))
    half = 0.5 * (1.0 + t)
    slope = half + 0.5 * z * (1.0 - t * t) * (GELU_K * (1.0 + 3.0 * GELU_C * z2))
    return z * half, slope


def split_hi_lo(x):
    hi = x.astype(BF)
    return hi, (x - hi.astype(F32)).astype(BF)


def cost(flops, nbytes, trans=0):
    return pl.CostEstimate(flops=int(flops), bytes_accessed=int(nbytes), transcendentals=int(trans))


def params(limit=56, **kw):
    return pltpu.CompilerParams(vmem_limit_bytes=limit * MIB, **kw)


def full_spec(shape, memory_space=pltpu.VMEM):
    return pl.BlockSpec(memory_space=memory_space)


ANY = pl.BlockSpec(memory_space=pl.ANY)
VM = pl.BlockSpec(memory_space=pltpu.VMEM)
SM = pl.BlockSpec(memory_space=pltpu.SMEM)


def sds(shape, dtype):
    return jax.ShapeDtypeStruct(shape, dtype)


def pool_matrix(rows, cols):
    k = lax.broadcasted_iota(jnp.int32, (rows, cols), 0)
    t = lax.broadcasted_iota(jnp.int32, (rows, cols), 1)
    both = jnp.where((t == 2 * k) | (t == 2 * k - 1), 0.5, 0.0)
    return jnp.where((k == 0) & (t == 0), 1.0, both).astype(BF)


def pool_matrix_t(rows, cols):
    t = lax.broadcasted_iota(jnp.int32, (rows, cols), 0)
    k = lax.broadcasted_iota(jnp.int32, (rows, cols), 1)
    both = jnp.where((t == 2 * k) | (t == 2 * k - 1), 0.5, 0.0)
    return jnp.where((k == 0) & (t == 0), 1.0, both).astype(BF)


def proj0_kernel(tok_ref, w_ref, bias_ref, pooled_ref, low_ref, qw_ref, qr_ref, k_ref, v_ref):
    tok = tok_ref[0]
    length = tok.shape[0]
    pooled = mm(pool_matrix(length // 2, length), tok)
    low = pooled.astype(BF)
    pooled_ref[0] = pooled
    low_ref[0] = low
    q = mm(low, w_ref[0, 0])
    qw_ref[0] = (q + bias_ref[0, 0:1, :]).astype(BF)
    qr_ref[0] = (q + bias_ref[0, 1:2, :]).astype(BF)
    k_ref[0] = mm(tok, w_ref[0, 1]).astype(BF)
    v_ref[0] = mm(tok, w_ref[0, 2]).astype(BF)


def proj0(tokens, w_qkv, attn_bias):
    s, length, _ = tokens.shape
    q = length // 2
    seq = lambda i: (i, 0, 0)
    return pl.pallas_call(
        proj0_kernel,
        grid=(s,),
        in_specs=[
            pl.BlockSpec((1, length, D), seq),
            pl.BlockSpec((1, 3, D, D), lambda i: (0, 0, 0, 0)),
            pl.BlockSpec((1, 2, D), lambda i: (0, 0, 0)),
        ],
        out_specs=[pl.BlockSpec((1, q, D), seq)] * 4 + [pl.BlockSpec((1, length, D), seq)] * 2,
        out_shape=[
            sds((s, q, D), F32),
            sds((s, q, D), BF),
            sds((s, q, D), BF),
            sds((s, q, D), BF),
            sds((s, length, D), BF),
            sds((s, length, D), BF),
        ],
        compiler_params=params(),
        cost_estimate=cost(2 * s * length * D * D * 3, 16 * MIB),
        name="proj0",
    )(tokens, w_qkv, attn_bias)


def head_masks():
    lane = lax.broadcasted_iota(jnp.int32, (1, 128), 1)
    first = jnp.where(lane < HEAD_DIM, 1.0, 0.0)
    return first.astype(BF), (1.0 - first).astype(BF)


def both_heads(x, masks):
    return jnp.concatenate([x * masks[0], x * masks[1]], axis=0)


QB = 128


def attn_fwd_kernel(stride, valid_ref, qw_ref, qr_ref, k_ref, v_ref, tab_ref, mixed_ref, p_ref):
    masks = head_masks()
    lane = lax.broadcasted_iota(jnp.int32, (1, 128), 1)
    keys = k_ref.shape[1]
    queries = qw_ref.shape[1]
    width = stride * QB + keys
    valid = valid_ref[0] > 0
    k = k_ref[0]
    v = v_ref[0]
    for b in range(queries // QB):
        rows = slice(b * QB, (b + 1) * QB)
        t0 = stride * (queries - QB - b * QB)
        content = mm_nt(both_heads(qw_ref[0, rows, :], masks), k)
        relative = mm_nt(both_heads(qr_ref[0, rows, :], masks), tab_ref[t0 : t0 + width, :])
        outs = []
        for h in range(2):
            part = slice(h * QB, (h + 1) * QB)
            rolled = pltpu.roll(
                relative[part], width - stride * (QB - 1), 1, stride=stride, stride_axis=0
            )
            scores = (content[part] + rolled[:, :keys]) * SCALE
            scores = jnp.where(valid, scores, MASKED)
            terms = jnp.exp(scores - jnp.max(scores, axis=-1, keepdims=True))
            prob = (terms * (1.0 / jnp.sum(terms, axis=-1, keepdims=True))).astype(BF)
            p_ref[0, h, rows, :] = prob
            outs.append(mm(prob, v))
        mixed_ref[0, rows, :] = jnp.where(lane < HEAD_DIM, outs[0], outs[1]).astype(BF)


def attn_fwd(stride, valid, qw, qr, k, v, tab):
    s, queries, _ = qw.shape
    keys = k.shape[1]
    table = tab.shape[0]
    pair = lambda i, j: (i, 0, j)
    return pl.pallas_call(
        functools.partial(attn_fwd_kernel, stride),
        grid=(s, HEADS // 2),
        in_specs=[
            pl.BlockSpec((1, 1, keys), lambda i, j: (i, 0, 0)),
            pl.BlockSpec((1, queries, 128), pair),
            pl.BlockSpec((1, queries, 128), pair),
            pl.BlockSpec((1, keys, 128), pair),
            pl.BlockSpec((1, keys, 128), pair),
            pl.BlockSpec((table, 128), lambda i, j: (0, j)),
        ],
        out_specs=[
            pl.BlockSpec((1, queries, 128), pair),
            pl.BlockSpec((1, 2, queries, keys), lambda i, j: (i, j, 0, 0)),
        ],
        out_shape=[sds((s, queries, D), BF), sds((s, HEADS, queries, keys), BF)],
        compiler_params=params(),
        cost_estimate=cost(2 * s * HEADS * queries * keys * 64 * 4, 12 * MIB, s * HEADS * queries * keys),
        name="attn_fwd_%d" % stride,
    )(valid, qw, qr, k, v, tab)


def attn_bwd_kernel(
    stride, p_ref, qw_ref, qr_ref, k_ref, v_ref, tab_ref, dm_ref, dq_ref, dk_ref, dv_ref, dtab_ref, dbias_ref
):
    masks = head_masks()
    lane = lax.broadcasted_iota(jnp.int32, (1, 128), 1)
    first = lane < HEAD_DIM
    keys = k_ref.shape[1]
    queries = qw_ref.shape[1]
    width = stride * QB + keys
    flip_i = lax.broadcasted_iota(jnp.int32, (QB, QB), 0)
    flip_j = lax.broadcasted_iota(jnp.int32, (QB, QB), 1)
    flip = jnp.where(flip_i + flip_j == QB - 1, 1.0, 0.0).astype(BF)

    @pl.when(pl.program_id(1) == 0)
    def _():
        dtab_ref[...] = jnp.zeros_like(dtab_ref)
        dbias_ref[...] = jnp.zeros_like(dbias_ref)

    k = k_ref[0]
    v = v_ref[0]
    sum_w = jnp.zeros((1, 128), F32)
    sum_r = jnp.zeros((1, 128), F32)
    dk = jnp.zeros((keys, 128), F32)
    dv = jnp.zeros((keys, 128), F32)
    for b in range(queries // QB):
        rows = slice(b * QB, (b + 1) * QB)
        t0 = stride * (queries - QB - b * QB)
        dm2 = both_heads(dm_ref[0, rows, :], masks)
        qw2 = both_heads(qw_ref[0, rows, :], masks)
        prob = jnp.concatenate([p_ref[0, 0, rows, :], p_ref[0, 1, rows, :]], axis=0)
        dprob = mm_nt(dm2, v)
        wide = prob.astype(F32)
        inner = jnp.sum(dprob * wide, axis=-1, keepdims=True)
        ds = (wide * (dprob - inner)).astype(BF)
        dv = dv + mm_tn(prob, dm2)
        dk = dk + mm_tn(ds, qw2)
        dqw2 = mm(ds, k)
        dqw = jnp.where(first, dqw2[:QB], dqw2[QB:]) * SCALE
        qr_rev = mm(flip, qr_ref[0, rows, :]).astype(BF)
        tab = tab_ref[t0 : t0 + width, :]
        rels = []
        for h in range(2):
            rev = mm(flip, ds[h * QB : (h + 1) * QB])
            padded = jnp.concatenate([rev, jnp.zeros((QB, width - keys), F32)], axis=1)
            rels.append(pltpu.roll(padded, 0, 1, stride=stride, stride_axis=0).astype(BF))
        rel2 = jnp.concatenate(rels, axis=0)
        dtab_ref[t0 : t0 + width, :] += mm_tn(rel2, both_heads(qr_rev, masks)) * SCALE
        dqr2 = mm(rel2, tab)
        dqr_rev = jnp.where(first, dqr2[:QB], dqr2[QB:])
        hi, lo = split_hi_lo(dqr_rev)
        dqr = (mm(flip, hi) + mm(flip, lo)) * SCALE
        dq_ref[0, rows, :] = (dqw + dqr).astype(BF)
        sum_w = sum_w + jnp.sum(dqw, axis=0, keepdims=True)
        sum_r = sum_r + jnp.sum(dqr, axis=0, keepdims=True)
    dk_ref[0] = (dk * SCALE).astype(BF)
    dv_ref[0] = dv.astype(BF)
    dbias_ref[0:1, :] += sum_w
    dbias_ref[1:2, :] += sum_r


def attn_bwd(stride, p, qw, qr, k, v, tab, dmixed):
    s, queries, _ = qw.shape
    keys = k.shape[1]
    table = tab.shape[0]
    pair = lambda j, i: (i, 0, j)
    return pl.pallas_call(
        functools.partial(attn_bwd_kernel, stride),
        grid=(HEADS // 2, s),
        in_specs=[
            pl.BlockSpec((1, 2, queries, keys), lambda j, i: (i, j, 0, 0)),
            pl.BlockSpec((1, queries, 128), pair),
            pl.BlockSpec((1, queries, 128), pair),
            pl.BlockSpec((1, keys, 128), pair),
            pl.BlockSpec((1, keys, 128), pair),
            pl.BlockSpec((table, 128), lambda j, i: (0, j)),
            pl.BlockSpec((1, queries, 128), pair),
        ],
        out_specs=[
            pl.BlockSpec((1, queries, 128), pair),
            pl.BlockSpec((1, keys, 128), pair),
            pl.BlockSpec((1, keys, 128), pair),
            pl.BlockSpec((table, 128), lambda j, i: (0, j)),
            pl.BlockSpec((8, 128), lambda j, i: (0, j)),
        ],
        out_shape=[
            sds((s, queries, D), BF),
            sds((s, keys, D), BF),
            sds((s, keys, D), BF),
            sds((table, D), F32),
            sds((8, D), F32),
        ],
        compiler_params=params(),
        cost_estimate=cost(2 * s * HEADS * queries * keys * 64 * 9, 16 * MIB),
        name="attn_bwd_%d" % stride,
    )(p, qw, qr, k, v, tab, dmixed)


def ffn_fwd_kernel(
    mixed_ref, resid_ref, wout_ref, wup_ref, wdown_ref, wqkv_ref, abias_ref, upb_ref, gain_ref, nbias_ref, obias_ref,
    hid_ref, x1_ref, r1_ref, act_ref, slope_ref, x2_ref, r2_ref, out_ref, low_ref, qw_ref, qr_ref, k_ref, v_ref,
):
    pre_norm = resid_ref[...] + (mm(mixed_ref[...], wout_ref[0]) + obias_ref[0, 0:1, :])
    x1, r1 = ln_fwd(pre_norm)
    x1_ref[...] = x1
    r1_ref[...] = jnp.broadcast_to(r1, r1_ref.shape)
    hidden = x1 * gain_ref[0, 0:1, :] + nbias_ref[0, 0:1, :]
    low = hidden.astype(BF)
    hid_ref[...] = low
    total = jnp.zeros_like(hidden)
    for c in range(PANELS):
        cols = slice(c * D, (c + 1) * D)
        act, slope = gelu_and_slope(mm(low, wup_ref[0, :, cols]) + upb_ref[0:1, cols])
        act = act.astype(BF)
        act_ref[:, cols] = act
        slope_ref[:, cols] = slope.astype(BF)
        total = total + mm(act, wdown_ref[0, cols, :])
    x2, r2 = ln_fwd(hidden + (total + obias_ref[0, 1:2, :]))
    x2_ref[...] = x2
    r2_ref[...] = jnp.broadcast_to(r2, r2_ref.shape)
    out = x2 * gain_ref[0, 1:2, :] + nbias_ref[0, 1:2, :]
    out_ref[...] = out
    olow = out.astype(BF)
    low_ref[...] = olow
    q = mm(olow, wqkv_ref[0, 0])
    qw_ref[...] = (q + abias_ref[0, 0:1, :]).astype(BF)
    qr_ref[...] = (q + abias_ref[0, 1:2, :]).astype(BF)
    k_ref[...] = mm(olow, wqkv_ref[0, 1]).astype(BF)
    v_ref[...] = mm(olow, wqkv_ref[0, 2]).astype(BF)


def ffn_fwd(mixed, resid, w_out, w_up, w_down, w_qkv, attn_bias, up_bias, gain, nbias, obias):
    rows = mixed.shape[0]
    blk = min(256, rows)
    row = lambda i: (i, 0)
    one = lambda l: (lambda i: (l, 0, 0))
    single = dict(pipeline_mode=pl.Buffered(1))
    wide = lambda n: pl.BlockSpec((blk, n), row)
    return pl.pallas_call(
        ffn_fwd_kernel,
        grid=(rows // blk,),
        in_specs=[
            wide(D),
            wide(D),
            pl.BlockSpec((1, D, D), one(0), **single),
            pl.BlockSpec((1, D, FF), one(0), **single),
            pl.BlockSpec((1, FF, D), one(0), **single),
            pl.BlockSpec((1, 3, D, D), lambda i: (1, 0, 0, 0), **single),
            pl.BlockSpec((1, 2, D), one(1)),
            pl.BlockSpec((2, FF), lambda i: (0, 0)),
            pl.BlockSpec((1, 2, D), one(0)),
            pl.BlockSpec((1, 2, D), one(0)),
            pl.BlockSpec((1, 2, D), one(0)),
        ],
        out_specs=[wide(D), wide(D), wide(128), wide(FF), wide(FF), wide(D), wide(128)] + [wide(D)] * 6,
        out_shape=[
            sds((rows, D), BF),
            sds((rows, D), F32),
            sds((rows, 128), F32),
            sds((rows, FF), BF),
            sds((rows, FF), BF),
            sds((rows, D), F32),
            sds((rows, 128), F32),
            sds((rows, D), F32),
            sds((rows, D), BF),
            sds((rows, D), BF),
            sds((rows, D), BF),
            sds((rows, D), BF),
            sds((rows, D), BF),
        ],
        compiler_params=params(),
        cost_estimate=cost(2 * rows * D * D * 12, 34 * MIB, rows * FF),
        name="ffn_fwd",
    )(mixed, resid, w_out, w_up, w_down, w_qkv, attn_bias, up_bias, gain, nbias, obias)


def bases(info_ref, rows_each):
    me, side = info_ref[0], info_ref[1]
    order_x, order_s = {}, {}
    for r in range(SHARDS):
        rel = jnp.bitwise_xor(me, r)
        b0 = jnp.bitwise_and(rel, 1)
        b1 = jnp.bitwise_and(jnp.right_shift(rel, 1), 1)
        b2 = jnp.bitwise_and(jnp.right_shift(rel, 2), 1)
        b3 = jnp.bitwise_and(jnp.right_shift(rel, 3), 1)
        for half in range(2):
            s = jnp.bitwise_xor(side, half)
            tail = b2 * 2 + b3
            order_x[r, half] = (((b0 * 2 + b1) * 2 + s) * 4 + tail) * rows_each
            order_s[r, half] = (((b0 * 2 + s) * 2 + b1) * 4 + tail) * rows_each
    return order_x, order_s


def put(buf_ref, base, offset, tile, shards, rows):
    low = tile.astype(BF)
    for n, r in enumerate(shards):
        for half in range(2):
            start = pl.multiple_of(base[r, half] + offset, 16)
            buf_ref[pl.ds(start, rows), :] = low[n * rows : (n + 1) * rows, half * HALF : (half + 1) * HALF]


def ship(buf_ref, keep_ref, send_ref, sems):
    n = keep_ref.shape[0]
    copies = [
        pltpu.make_async_copy(buf_ref.at[pl.ds(n, n)], send_ref, sems.at[0]),
        pltpu.make_async_copy(buf_ref.at[pl.ds(0, n)], keep_ref, sems.at[1]),
    ]
    for copy in copies:
        copy.start()
    return copies


def ffn_back(
    info_ref, dy, x2, r2, gain2, gain1, wout_ref, wup, wdown, act, slope, hid_ref, x1, r1, mixed_ref,
    small_ref, upg_ref, dmixed_ref, dbranch_ref, dres_ref, dpost_ref, dhid_ref, buf_a, buf_b, outs, sems,
):
    small_ref[...] = jnp.zeros_like(small_ref)
    dpost = ln_bwd(dy, x2, r2, gain2)
    small_ref[1:2, :] = jnp.sum(dy * x2, axis=0, keepdims=True)
    small_ref[3:4, :] = jnp.sum(dy, axis=0, keepdims=True)
    dffn = dpost.astype(BF)
    small_ref[5:6, :] = jnp.sum(dffn.astype(F32), axis=0, keepdims=True)
    dpost_ref[...] = dffn
    dhid_ref[...] = dpost
    order_x, order_s = bases(info_ref, UP_ROWS)
    for c in range(PANELS):
        cols = slice(c * D, (c + 1) * D)
        dffn = dpost_ref[...]
        dact = mm_nt(dffn, wdown[cols, :])
        put(buf_b, order_s, 0, mm_tn(act[:, cols], dffn), range(4 * c, 4 * c + 4), UP_ROWS)
        dpre = (dact * slope[:, cols].astype(F32)).astype(BF)
        upg_ref[:, cols] = jnp.broadcast_to(jnp.sum(dpre.astype(F32), axis=0, keepdims=True), (8, D))
        dhid_ref[...] += mm_nt(dpre, wup[:, cols])
        put(buf_a, order_x, c * ROW, mm_tn(hid_ref[...], dpre), range(SHARDS), ROW)
    copies = ship(buf_a, outs[0], outs[1], [sems.at[0], sems.at[1]]) if False else None
    n = outs[0].shape[0]
    copies = [
        pltpu.make_async_copy(buf_a.at[pl.ds(n, n)], outs[1], sems.at[0]),
        pltpu.make_async_copy(buf_b.at[pl.ds(n, n)], outs[3], sems.at[1]),
        pltpu.make_async_copy(buf_a.at[pl.ds(0, n)], outs[0], sems.at[2]),
        pltpu.make_async_copy(buf_b.at[pl.ds(0, n)], outs[2], sems.at[3]),
    ]
    for copy in copies:
        copy.start()
    dhid = dhid_ref[...]
    xh = x1()
    small_ref[0:1, :] = jnp.sum(dhid * xh, axis=0, keepdims=True)
    small_ref[2:3, :] = jnp.sum(dhid, axis=0, keepdims=True)
    dres = ln_bwd(dhid, xh, r1(), gain1)
    dres_ref[...] = dres
    dbranch = dres.astype(BF)
    dbranch_ref[...] = dbranch
    small_ref[4:5, :] = jnp.sum(dbranch.astype(F32), axis=0, keepdims=True)
    dmixed_ref[...] = mm_nt(dbranch, wout_ref[0]).astype(BF)
    for copy in copies:
        copy.wait()


def ffn_last_kernel(
    info_ref, mixed_ref, resid_ref, cot_ref, wout_ref, wup_hbm, wdown_hbm, upb_ref, gain_ref, nbias_ref, obias_ref,
    lout_ref, dmixed_ref, dbranch_ref, dres_ref, small_ref, upg_ref, ka, sa, kb, sb,
    wup, wdown, act, slope, hid, x1s, dffn_s, dhid_s, buf_a, buf_b, sems,
):
    cp_up = pltpu.make_async_copy(wup_hbm.at[1], wup, sems.at[4])
    cp_down = pltpu.make_async_copy(wdown_hbm.at[1], wdown, sems.at[5])
    cp_up.start()
    cp_down.start()
    pre_norm = resid_ref[...] + (mm(mixed_ref[...], wout_ref[0]) + obias_ref[0, 0:1, :])
    x1, r1 = ln_fwd(pre_norm)
    x1s[...] = x1
    hidden = x1 * gain_ref[0, 0:1, :] + nbias_ref[0, 0:1, :]
    hid[...] = hidden.astype(BF)
    dhid_s[...] = hidden + obias_ref[0, 1:2, :]
    cp_up.wait()
    cp_down.wait()
    for c in range(PANELS):
        cols = slice(c * D, (c + 1) * D)
        a, s = gelu_and_slope(mm(hid[...], wup[:, cols]) + upb_ref[1:2, cols])
        a = a.astype(BF)
        act[:, cols] = a
        slope[:, cols] = s.astype(BF)
        dhid_s[...] += mm(a, wdown[cols, :])
    x2, r2 = ln_fwd(dhid_s[...])
    lout_ref[...] = (x2 * gain_ref[0, 1:2, :] + nbias_ref[0, 1:2, :]).astype(BF)
    dy = cot_ref[...].astype(F32)
    ffn_back(
        info_ref, dy, x2, r2, gain_ref[0, 1:2, :], gain_ref[0, 0:1, :], wout_ref, wup, wdown, act, slope, hid,
        lambda: x1s[...], lambda: r1, mixed_ref, small_ref, upg_ref, dmixed_ref, dbranch_ref, dres_ref, dffn_s, dhid_s,
        buf_a, buf_b, (ka, sa, kb, sb), sems,
    )


BUF_ROWS = 2 * SHARDS * UP_ROWS


def ffn_last(info, mixed, resid, cot, w_out, w_up, w_down, up_bias, gain, nbias, obias):
    rows = mixed.shape[0]
    layer = lambda: pl.BlockSpec((1, 2, D), lambda i, n: (1, 0, 0))
    whole = pl.BlockSpec((rows, D), lambda i, n: (0, 0))
    return pl.pallas_call(
        ffn_last_kernel,
        grid_spec=pltpu.PrefetchScalarGridSpec(
            num_scalar_prefetch=1,
            grid=(1,),
            in_specs=[
                whole, whole, whole,
                pl.BlockSpec((1, D, D), lambda i, n: (1, 0, 0)),
                ANY, ANY,
                pl.BlockSpec((2, FF), lambda i, n: (0, 0)),
                layer(), layer(), layer(),
            ],
            out_specs=[whole, whole, whole, whole,
                       pl.BlockSpec((8, D), lambda i, n: (0, 0)), pl.BlockSpec((8, FF), lambda i, n: (0, 0)),
                       ANY, ANY, ANY, ANY],
            scratch_shapes=[
                pltpu.VMEM((D, FF), BF), pltpu.VMEM((FF, D), BF),
                pltpu.VMEM((rows, FF), BF), pltpu.VMEM((rows, FF), BF),
                pltpu.VMEM((rows, D), BF), pltpu.VMEM((rows, D), F32),
                pltpu.VMEM((rows, D), BF), pltpu.VMEM((rows, D), F32),
                pltpu.VMEM((BUF_ROWS, HALF), BF), pltpu.VMEM((BUF_ROWS, HALF), BF),
                pltpu.SemaphoreType.DMA((6,)),
            ],
        ),
        out_shape=[
            sds((rows, D), BF), sds((rows, D), BF), sds((rows, D), BF), sds((rows, D), F32),
            sds((8, D), F32), sds((8, FF), F32),
        ] + [sds((BUF_ROWS // 2, HALF), BF)] * 4,
        compiler_params=params(),
        cost_estimate=cost(2 * rows * D * D * 26, 30 * MIB, rows * FF),
        name="ffn_last",
    )(info, mixed, resid, cot, w_out, w_up, w_down, up_bias, gain, nbias, obias)


def ffn_bwd_kernel(
    info_ref, dy_ref, x2_ref, r2_ref, mixed_ref, hid_ref, x1_ref, r1_ref, gain_ref, wout_ref,
    wup_hbm, wdown_hbm, act_hbm, slope_hbm,
    dmixed_ref, dbranch_ref, dres_ref, small_ref, upg_ref, ka, sa, kb, sb,
    wup, wdown, act, slope, dffn_s, dhid_s, buf_a, buf_b, sems,
):
    loads = [
        pltpu.make_async_copy(wdown_hbm.at[0], wdown, sems.at[4]),
        pltpu.make_async_copy(act_hbm, act, sems.at[5]),
        pltpu.make_async_copy(slope_hbm, slope, sems.at[6]),
        pltpu.make_async_copy(wup_hbm.at[0], wup, sems.at[7]),
    ]
    for copy in loads:
        copy.start()
    dy = dy_ref[...]
    for copy in loads:
        copy.wait()
    ffn_back(
        info_ref, dy, x2_ref[...], r2_ref[:, 0:1], gain_ref[0, 1:2, :], gain_ref[0, 0:1, :], wout_ref, wup, wdown,
        act, slope, hid_ref, lambda: x1_ref[...], lambda: r1_ref[:, 0:1], mixed_ref, small_ref, upg_ref,
        dmixed_ref, dbranch_ref, dres_ref, dffn_s, dhid_s, buf_a, buf_b, (ka, sa, kb, sb), sems,
    )


def ffn_bwd(info, dy, x2, r2, mixed, hid, x1, r1, gain, w_out, w_up, w_down, act, slope):
    rows = mixed.shape[0]
    whole = pl.BlockSpec((rows, D), lambda i, n: (0, 0))
    thin = pl.BlockSpec((rows, 128), lambda i, n: (0, 0))
    return pl.pallas_call(
        ffn_bwd_kernel,
        grid_spec=pltpu.PrefetchScalarGridSpec(
            num_scalar_prefetch=1,
            grid=(1,),
            in_specs=[
                whole, whole, thin, whole, whole, whole, thin,
                pl.BlockSpec((1, 2, D), lambda i, n: (0, 0, 0)),
                pl.BlockSpec((1, D, D), lambda i, n: (0, 0, 0)),
                ANY, ANY, ANY, ANY,
            ],
            out_specs=[whole, whole, whole,
                       pl.BlockSpec((8, D), lambda i, n: (0, 0)), pl.BlockSpec((8, FF), lambda i, n: (0, 0)),
                       ANY, ANY, ANY, ANY],
            scratch_shapes=[
                pltpu.VMEM((D, FF), BF), pltpu.VMEM((FF, D), BF),
                pltpu.VMEM((rows, FF), BF), pltpu.VMEM((rows, FF), BF),
                pltpu.VMEM((rows, D), BF), pltpu.VMEM((rows, D), F32),
                pltpu.VMEM((BUF_ROWS, HALF), BF), pltpu.VMEM((BUF_ROWS, HALF), BF),
                pltpu.SemaphoreType.DMA((8,)),
            ],
        ),
        out_shape=[
            sds((rows, D), BF), sds((rows, D), BF), sds((rows, D), F32),
            sds((8, D), F32), sds((8, FF), F32),
        ] + [sds((BUF_ROWS // 2, HALF), BF)] * 4,
        compiler_params=params(),
        cost_estimate=cost(2 * rows * D * D * 17, 36 * MIB),
        name="ffn_bwd",
    )(info, dy, x2, r2, mixed, hid, x1, r1, gain, w_out, w_up, w_down, act, slope)


def first_back_kernel(dres_ref, dq_ref, dk_ref, dv_ref, w_ref, out_ref):
    out_ref[...] = dres_ref[...] + (
        mm_nt(dq_ref[...], w_ref[0, 0]) + mm_nt(dk_ref[...], w_ref[0, 1]) + mm_nt(dv_ref[...], w_ref[0, 2])
    )


def first_back(dres, dq, dk, dv, w_qkv):
    rows = dres.shape[0]
    row = lambda i: (i, 0)
    blk = 256
    wide = pl.BlockSpec((blk, D), row)
    return pl.pallas_call(
        first_back_kernel,
        grid=(rows // blk,),
        in_specs=[wide] * 4 + [pl.BlockSpec((1, 3, D, D), lambda i: (1, 0, 0, 0), pipeline_mode=pl.Buffered(1))],
        out_specs=wide,
        out_shape=sds((rows, D), F32),
        compiler_params=params(),
        cost_estimate=cost(2 * rows * D * D * 3, 8 * MIB),
        name="first_back",
    )(dres, dq, dk, dv, w_qkv)


def tokens_back_kernel(dres_ref, dq_ref, dk_ref, dv_ref, w_ref, out_ref):
    dpool = dres_ref[0] + mm_nt(dq_ref[0], w_ref[0, 0])
    hi, lo = split_hi_lo(dpool)
    spread = pool_matrix_t(dk_ref.shape[1], dpool.shape[0])
    out_ref[0] = mm_nt(dk_ref[0], w_ref[0, 1]) + mm_nt(dv_ref[0], w_ref[0, 2]) + (mm(spread, hi) + mm(spread, lo))


def tokens_back(dres, dq, dk, dv, w_qkv):
    s, length, _ = dk.shape
    queries = dq.shape[1]
    seq = lambda i: (i, 0, 0)
    return pl.pallas_call(
        tokens_back_kernel,
        grid=(s,),
        in_specs=[
            pl.BlockSpec((1, queries, D), seq),
            pl.BlockSpec((1, queries, D), seq),
            pl.BlockSpec((1, length, D), seq),
            pl.BlockSpec((1, length, D), seq),
            pl.BlockSpec((1, 3, D, D), lambda i: (0, 0, 0, 0)),
        ],
        out_specs=pl.BlockSpec((1, length, D), seq),
        out_shape=sds((s, length, D), F32),
        compiler_params=params(),
        cost_estimate=cost(2 * s * length * D * D * 3, 14 * MIB),
        name="tokens_back",
    )(dres, dq, dk, dv, w_qkv)


A_MATS = 3
B_MATS = 2


def qkv_grad_kernel(
    info_ref, xq_ref, xk_ref, dq_ref, dk_ref, dv_ref, mixed_ref, dbranch_ref, enc_ref, dtab_ref,
    ka, sa, kb, sb, buf_a, buf_b, sems,
):
    order_x, _ = bases(info_ref, A_MATS * ROW)
    _, order_s = bases(info_ref, B_MATS * ROW)
    every = range(SHARDS)
    put(buf_a, order_x, 0, mm_tn(mixed_ref[...], dbranch_ref[...]), every, ROW)
    put(buf_a, order_x, ROW, mm_tn(xq_ref[...], dq_ref[...]), every, ROW)
    put(buf_a, order_x, 2 * ROW, mm_tn(xk_ref[...], dk_ref[...]), every, ROW)
    put(buf_b, order_s, 0, mm_tn(xk_ref[...], dv_ref[...]), every, ROW)
    put(buf_b, order_s, ROW, mm_tn(enc_ref[...], dtab_ref[...].astype(BF)), every, ROW)
    n, m = ka.shape[0], kb.shape[0]
    copies = [
        pltpu.make_async_copy(buf_a.at[pl.ds(n, n)], sa, sems.at[0]),
        pltpu.make_async_copy(buf_b.at[pl.ds(m, m)], sb, sems.at[1]),
        pltpu.make_async_copy(buf_a.at[pl.ds(0, n)], ka, sems.at[2]),
        pltpu.make_async_copy(buf_b.at[pl.ds(0, m)], kb, sems.at[3]),
    ]
    for copy in copies:
        copy.start()
    for copy in copies:
        copy.wait()


def qkv_grad(info, xq, xk, dq, dk, dv, mixed, dbranch, enc, dtab):
    whole = lambda x: pl.BlockSpec(x.shape, lambda i, n: (0, 0))
    ins = (xq, xk, dq, dk, dv, mixed, dbranch, enc, dtab)
    n, m = SHARDS * A_MATS * ROW, SHARDS * B_MATS * ROW
    return pl.pallas_call(
        qkv_grad_kernel,
        grid_spec=pltpu.PrefetchScalarGridSpec(
            num_scalar_prefetch=1,
            grid=(1,),
            in_specs=[whole(x) for x in ins],
            out_specs=[ANY, ANY, ANY, ANY],
            scratch_shapes=[
                pltpu.VMEM((2 * n, HALF), BF), pltpu.VMEM((2 * m, HALF), BF), pltpu.SemaphoreType.DMA((4,)),
            ],
        ),
        out_shape=[sds((n, HALF), BF)] * 2 + [sds((m, HALF), BF)] * 2,
        compiler_params=params(),
        cost_estimate=cost(2 * D * D * (2 * xq.shape[0] + 2 * xk.shape[0] + enc.shape[0]), 16 * MIB),
        name="qkv_grad",
    )(info, *ins)


def swap(x, axis, bit):
    n = lax.axis_size(axis)
    return lax.ppermute(x, axis, [(i, i ^ bit) for i in range(n)])


def halving(keep, send, steps):
    total = keep + swap(send, *steps[0])
    for step in steps[1:]:
        n = total.shape[0] // 2
        total = total[:n] + swap(total[n:], *step)
    return total


X_FIRST = (("rows", 1), ("rows", 2), ("seq", 1), ("rows", 4), ("rows", 8))
S_FIRST = (("rows", 1), ("seq", 1), ("rows", 2), ("rows", 4), ("rows", 8))


def reduce_stream(keep, send, order, side):
    mine = halving(keep, send, order)
    other = swap(mine, "seq", 1)
    low = jnp.where(side == 0, mine, other)
    high = jnp.where(side == 0, other, mine)
    return jnp.concatenate([low, high], axis=1).astype(F32)


def generic_stream(keep, send, order, mats):
    both = jnp.concatenate([keep, send], axis=0)
    if order is X_FIRST:
        view = both.reshape(2, 2, 2, 2, 2, mats, -1, HALF)
        view = view.transpose(5, 4, 3, 1, 0, 6, 2, 7)
    else:
        view = both.reshape(2, 2, 2, 2, 2, mats, -1, HALF)
        view = view.transpose(5, 4, 3, 2, 0, 6, 1, 7)
    whole = view.reshape(mats, -1, D)
    mine = lax.psum_scatter(whole, "rows", scatter_dimension=1, tiled=True)
    return lax.psum(mine.astype(F32), "seq").reshape(-1, D)


def all_sum(x):
    for step in X_FIRST:
        x = x + swap(x, *step)
    return x


def sinusoid(distance):
    half_width = D // 2
    frequency = 10000.0 ** (-jnp.arange(half_width, dtype=F32) / half_width)
    angles = distance.astype(F32)[:, None] * frequency[None, :]
    return jnp.concatenate([jnp.sin(angles), jnp.cos(angles)], axis=1)


def to_sequences(x, side, parts):
    own = x.shape[0] // parts
    mine = lax.dynamic_slice_in_dim(x, side * own, own, 0)
    other = swap(lax.dynamic_slice_in_dim(x, (1 - side) * own, own, 0), "seq", 1)
    return jnp.where(
        side == 0, jnp.concatenate([mine, other], axis=1), jnp.concatenate([other, mine], axis=1)
    )


def to_positions(x, side, parts, wire=None):
    own = x.shape[1] // parts
    mine = lax.dynamic_slice_in_dim(x, side * own, own, 1)
    sent = lax.dynamic_slice_in_dim(x, (1 - side) * own, own, 1)
    other = swap(sent if wire is None else sent.astype(wire), "seq", 1).astype(x.dtype)
    return jnp.where(
        side == 0, jnp.concatenate([mine, other], axis=0), jnp.concatenate([other, mine], axis=0)
    )


def on_device(
    tokens, lengths, key_mask, cotangent, w_qkv, w_out, w_pos, w_up, w_down, attn_bias, up_bias, norm_gain,
    norm_bias, out_bias,
):
    side = lax.axis_index("seq")
    parts = lax.axis_size("seq")
    n_rows = lax.axis_size("rows")
    me = lax.axis_index("rows")
    halved = n_rows == SHARDS and parts == 2
    zero = jnp.int32(0)
    info = jnp.stack([me, side]) if halved else jnp.stack([zero, zero])
    info = info.astype(jnp.int32)

    tok = to_sequences(tokens, side, parts)
    cot = to_sequences(cotangent, side, parts)
    seqs, length, _ = tok.shape
    queries = length // 2
    mine = lambda x: lax.dynamic_slice_in_dim(x, side * seqs, seqs, 0)
    places = jnp.arange(length, dtype=jnp.int32)[None, :]
    key_valid = jnp.where(places < mine(lengths)[:, None], mine(key_mask), 0)
    shifted_valid = jnp.concatenate([key_valid[:, :1], key_valid[:, :-1]], axis=1)
    pooled_valid = jnp.max(shifted_valid.reshape(seqs, queries, 2), axis=2)

    enc0 = sinusoid(2 * (queries - 1) - jnp.arange(2 * length, dtype=jnp.int32)).astype(BF)
    enc1 = enc0[::2]
    tab0 = mm(enc0, w_pos[0]).astype(BF)
    tab1 = mm(enc1, w_pos[1]).astype(BF)

    flat = lambda x: x.reshape(-1, x.shape[-1])
    sets = lambda x: x.reshape(seqs, -1, D)

    pooled, pooled_low, qw0, qr0, k0, v0 = proj0(tok, w_qkv, attn_bias)
    mixed0, p0 = attn_fwd(2, key_valid[:, None, :], qw0, qr0, k0, v0, tab0)
    mixed0 = flat(mixed0)
    hid, x1, r1, act, slope, x2, r2, first, first_low, qw1, qr1, k1, v1 = ffn_fwd(
        mixed0, flat(pooled), w_out, w_up, w_down, w_qkv, attn_bias, up_bias, norm_gain, norm_bias, out_bias
    )
    qw1, qr1, k1, v1 = sets(qw1), sets(qr1), sets(k1), sets(v1)
    mixed1, p1 = attn_fwd(1, pooled_valid[:, None, :], qw1, qr1, k1, v1, tab1)
    mixed1 = flat(mixed1)
    lout, dmixed1, dbranch1, dres1, small1, upg1, ka1, sa1, kb1, sb1 = ffn_last(
        info, mixed1, first, flat(cot), w_out, w_up, w_down, up_bias, norm_gain, norm_bias, out_bias
    )
    dq1, dk1, dv1, dtab1, dbias1 = attn_bwd(1, p1, qw1, qr1, k1, v1, tab1, sets(dmixed1))
    dq1, dk1, dv1 = flat(dq1), flat(dk1), flat(dv1)
    dfirst = first_back(dres1, dq1, dk1, dv1, w_qkv)
    ja1, ta1, jb1, tb1 = qkv_grad(info, first_low, first_low, dq1, dk1, dv1, mixed1, dbranch1, enc1, dtab1)
    dmixed0, dbranch0, dres0, small0, upg0, ka0, sa0, kb0, sb0 = ffn_bwd(
        info, dfirst, x2, r2, mixed0, hid, x1, r1, norm_gain, w_out, w_up, w_down, act, slope
    )
    dq0, dk0, dv0, dtab0, dbias0 = attn_bwd(2, p0, qw0, qr0, k0, v0, tab0, sets(dmixed0))
    dtok = tokens_back(sets(dres0), dq0, dk0, dv0, w_qkv)
    ja0, ta0, jb0, tb0 = qkv_grad(
        info, flat(pooled_low), flat(tok), flat(dq0), flat(dk0), flat(dv0), mixed0, dbranch0, enc0, dtab0
    )

    if halved:
        stream = lambda k, s, order, mats: reduce_stream(k, s, order, side)
    else:
        stream = generic_stream
    up1 = stream(ka1, sa1, X_FIRST, PANELS)
    down1 = stream(kb1, sb1, S_FIRST, 1)
    att_a1 = stream(ja1, ta1, X_FIRST, A_MATS)
    att_b1 = stream(jb1, tb1, S_FIRST, B_MATS)
    up0 = stream(ka0, sa0, X_FIRST, PANELS)
    down0 = stream(kb0, sb0, S_FIRST, 1)
    att_a0 = stream(ja0, ta0, X_FIRST, A_MATS)
    att_b0 = stream(jb0, tb0, S_FIRST, B_MATS)

    small = lambda s, u, b: jnp.concatenate([s[:6], b[:2], u[0].reshape(PANELS, D)], axis=0)
    if halved:
        sums = jnp.stack([all_sum(small(small0, upg0, dbias0)), all_sum(small(small1, upg1, dbias1))])
    else:
        sums = lax.psum(jnp.stack([small(small0, upg0, dbias0), small(small1, upg1, dbias1)]), ("rows", "seq"))
    own = D // n_rows
    cut = lambda x: lax.dynamic_slice_in_dim(x, me * own, own, 2)
    upb = lax.dynamic_slice_in_dim(sums[:, 8:].reshape(2, FF), me * (FF // n_rows), FF // n_rows, 1)

    thirds = lambda x: x.reshape(A_MATS, -1, D)
    pairs = lambda x: x.reshape(B_MATS, -1, D)
    a0, a1, b0, b1 = thirds(att_a0), thirds(att_a1), pairs(att_b0), pairs(att_b1)
    panels = lambda x: jnp.concatenate(list(x.reshape(PANELS, -1, D)), axis=1)
    return (
        to_positions(sets(lout), side, parts),
        to_positions(dtok, side, parts, BF),
        jnp.stack([jnp.stack([a0[1], a0[2], b0[0]]), jnp.stack([a1[1], a1[2], b1[0]])]),
        jnp.stack([a0[0], a1[0]]),
        jnp.stack([b0[1], b1[1]]),
        jnp.stack([panels(up0), panels(up1)]),
        jnp.stack([down0, down1]),
        cut(sums[:, 6:8]),
        upb,
        cut(sums[:, 0:2]),
        cut(sums[:, 2:4]),
        cut(sums[:, 4:6]),
    )


def solution(mesh):
    seq3 = P("rows", "seq", None)
    in_specs = (seq3, P("rows"), P("rows", None), seq3) + (P(),) * 10
    mat = P(None, "rows", None)
    vec = P(None, None, "rows")
    out_specs = (seq3, seq3, P(None, None, "rows", None), mat, mat, mat, mat, vec, P(None, "rows"), vec, vec, vec)
    return jax.shard_map(on_device, mesh=mesh, in_specs=in_specs, out_specs=out_specs, check_vma=False)
```

```python
import functools

import jax
import jax.numpy as jnp
from jax import lax
from jax.experimental import pallas as pl
from jax.experimental.pallas import tpu as pltpu
from jax.sharding import PartitionSpec as P

D = 768
HEADS = 12
HEAD_DIM = 64
FF = 3072
PANELS = FF // D
HALF = D // 2
EPS = 1e-06
MASKED = -1000000000.0
SCALE = HEAD_DIM ** (-0.5)
BF = jnp.bfloat16
F32 = jnp.float32
MIB = 1 << 20

SHARDS = 16
MESH = pl.DeviceIdType.MESH
UP_ROWS = PANELS * D // SHARDS
ROW = D // SHARDS
WIDE = 2
SMALL_ROWS = 12


def mm(a, b):
    return lax.dot_general(a, b, (((1,), (0,)), ((), ())), preferred_element_type=F32)


def mm_nt(a, b):
    return lax.dot_general(a, b, (((1,), (1,)), ((), ())), preferred_element_type=F32)


def mm_tn(a, b):
    return lax.dot_general(a, b, (((0,), (0,)), ((), ())), preferred_element_type=F32)


def ln_fwd(z):
    center = z - jnp.mean(z, axis=-1, keepdims=True)
    var = jnp.mean(center * center, axis=-1, keepdims=True)
    rstd = lax.rsqrt(var + EPS)
    return center * rstd, rstd


def ln_bwd(dy, xhat, rstd, gain):
    dx = dy * gain
    m1 = jnp.mean(dx, axis=-1, keepdims=True)
    m2 = jnp.mean(dx * xhat, axis=-1, keepdims=True)
    return rstd * (dx - m1 - xhat * m2)


GELU_K = 0.7978845608028654
GELU_C = 0.044715


def gelu_and_slope(z):
    z2 = z * z
    t = jnp.tanh(GELU_K * z * (1.0 + GELU_C * z2))
    half = 0.5 * (1.0 + t)
    slope = half + 0.5 * z * (1.0 - t * t) * (GELU_K * (1.0 + 3.0 * GELU_C * z2))
    return z * half, slope


def split_hi_lo(x):
    hi = x.astype(BF)
    return hi, (x - hi.astype(F32)).astype(BF)


def cost(flops, nbytes, trans=0):
    return pl.CostEstimate(flops=int(flops), bytes_accessed=int(nbytes), transcendentals=int(trans))


def params(limit=56, **kw):
    return pltpu.CompilerParams(vmem_limit_bytes=limit * MIB, **kw)


def full_spec(shape, memory_space=pltpu.VMEM):
    return pl.BlockSpec(memory_space=memory_space)


ANY = pl.BlockSpec(memory_space=pl.ANY)
VM = pl.BlockSpec(memory_space=pltpu.VMEM)
SM = pl.BlockSpec(memory_space=pltpu.SMEM)


def sds(shape, dtype):
    return jax.ShapeDtypeStruct(shape, dtype)


CORE = ("rows", 1)
ALONG_X = ("rows", 2)
ALONG_Y = ("seq", 1)
Z_NEAR = ("rows", 4)
Z_FAR = ("rows", 8)
Z_DIAG = ("rows", 12)
Z_ALL = ("rows", 0)
XZY = (CORE, ALONG_X, Z_NEAR, ALONG_Y, Z_FAR)
ZYX = (CORE, Z_NEAR, ALONG_Y, ALONG_X, Z_FAR)
XY = (CORE, ALONG_X, ALONG_Y, Z_ALL)
YX = (CORE, ALONG_Y, ALONG_X, Z_ALL)
BLOCK = 128
BLOCKS = D // (2 * BLOCK)


def bit(v, b):
    return lax.rem(lax.div(v, b), 2)


def partner(step):
    if isinstance(step[0], tuple):
        return {axis: spot for one in step for axis, spot in partner(one).items()}
    axis, b = step
    me = lax.axis_index(axis)
    spot = me
    for k in (1, 2, 4, 8):
        if b & k:
            spot = spot + k - 2 * k * bit(me, k)
    return {axis: spot}


def singles(step):
    return (Z_FAR, Z_NEAR, Z_DIAG) if step == Z_ALL else (step,)


def bits_of(order):
    return [one for step in order for one in ((Z_NEAR, Z_FAR) if step == Z_ALL else (step,))]


def greet(steps):
    steps = list(dict.fromkeys(one for step in steps for one in singles(step)))
    sem = pltpu.get_barrier_semaphore()
    for step in steps:
        pl.semaphore_signal(sem, inc=1, device_id=partner(step), device_id_type=MESH)
    pl.semaphore_wait(sem, len(steps))


def remote(src, dst, sems, i, step):
    return pltpu.make_async_remote_copy(
        src_ref=src,
        dst_ref=dst,
        send_sem=sems.at[i, 0],
        recv_sem=sems.at[i, 1],
        device_id=partner(step),
        device_id_type=MESH,
    )


def add_to(dst, m, b, bm, rows):
    blk = rows
    while blk * dst.shape[2] > 96 * HALF:
        blk //= 2

    def one(i, _):
        at = pl.ds(pl.multiple_of(i * blk, 16), blk)
        dst[m, at, :] = dst[m, at, :] + b[bm, at, :]
        return 0

    lax.fori_loop(0, rows // blk, one, 0)


class Kernel:
    def __init__(self):
        self.args, self.in_specs, self.out_specs, self.out_shape, self.scr = [], [], [], [], []

    def inp(self, x, spec=ANY):
        self.args.append(x)
        self.in_specs.append(spec)
        return ("i", len(self.args) - 1)

    def out(self, shape, dtype, spec=ANY):
        self.out_shape.append(sds(shape, dtype))
        self.out_specs.append(spec)
        return ("o", len(self.out_shape) - 1)

    def mem(self, shape, dtype=BF):
        self.scr.append(pltpu.VMEM(shape, dtype))
        return ("s", len(self.scr) - 1)

    def sems(self, *shape):
        self.scr.append(pltpu.SemaphoreType.DMA(shape))
        return ("s", len(self.scr) - 1)

    def run(self, body, name, cost_estimate, grid=(), cid=None, limit=56):
        n, m = len(self.args), len(self.out_shape)

        def kernel(*refs):
            groups = {"i": refs[:n], "o": refs[n : n + m], "s": refs[n + m :]}
            body(lambda handle: groups[handle[0]][handle[1]])

        kw = {} if cid is None else dict(collective_id=cid, has_side_effects=True)
        return pl.pallas_call(
            kernel,
            grid=grid,
            in_specs=self.in_specs,
            out_specs=self.out_specs,
            out_shape=self.out_shape,
            scratch_shapes=self.scr,
            compiler_params=params(limit, **kw),
            cost_estimate=cost_estimate,
            name=name,
        )(*self.args)


class Chain:
    def __init__(self, kn, whole, steps, close=False, born=None):
        self.steps, self.close, self.born, self.whole = steps, close, born is not None, whole
        j = len(steps)
        self.j = j
        if self.born:
            self.total, self.m, self.n, width = born
            self.arr = kn.mem((self.m, self.n, width))
        else:
            self.m, self.n, width = whole.shape
            self.src = kn.inp(whole)
            if j:
                self.total = kn.mem((self.m, self.n // (1 + len(singles(steps[0]))), width))
        m = self.m
        self.size = [self.n]
        for step in steps:
            self.size.append(self.size[-1] // (1 + len(singles(step))))
        self.land = [kn.mem((m * len(singles(s)), self.size[k + 1], width)) for k, s in enumerate(steps)]
        self.nf = self.size[-1]
        self.out = kn.out((m, self.nf, width), BF) if j else None
        self.other = kn.out((m, self.nf, width), BF) if close else None
        self.sem = kn.sems(2 * m + 3 * j + 3, 2)

    def bind(self, get):
        self.ref = get
        return self

    def core(self, i):
        g = self.ref
        return remote(g(self.total).at[i, pl.ds(self.n, self.n)], g(self.arr).at[i], g(self.sem), i, CORE)

    def sends(self, k, only=None):
        g, m, j = self.ref, self.m, self.j
        sem = g(self.sem)
        if k == j:
            mine = g(self.total).at[:, pl.ds(0, self.nf)] if j else g(self.src)
            return [remote(mine, g(self.other), sem, 2 * m + 3 * j, ALONG_Y)]
        n = self.size[k + 1]
        if self.born and k == 0:
            every = range(m) if only is None else [only]
            return [
                remote(g(self.total).at[i, pl.ds(n, n)], g(self.land[0]).at[i], sem, m + i, self.steps[0])
                for i in every
            ]
        source = g(self.total) if k or self.born else g(self.src)
        return [
            remote(
                source.at[:, pl.ds((i + 1) * n, n)], g(self.land[k]).at[pl.ds(i * m, m)], sem, 2 * m + 3 * k + i, one
            )
            for i, one in enumerate(singles(self.steps[k]))
        ]

    def fetch(self):
        g = self.ref
        return pltpu.make_async_copy(
            g(self.src).at[:, pl.ds(0, self.size[1])], g(self.total), g(self.sem).at[2 * self.m + 3 * self.j + 1, 0]
        )

    def keep(self):
        g = self.ref
        return pltpu.make_async_copy(
            g(self.total).at[:, pl.ds(0, self.nf)], g(self.out), g(self.sem).at[2 * self.m + 3 * self.j + 2, 0]
        )

    def first(self, i):
        g = self.ref
        self.core(i).wait()
        add_to(g(self.total), i, g(self.arr), i, self.n)
        for copy in self.sends(0, i):
            copy.start()

    def go(self, k):
        g = self.ref
        if k == 0 and self.j:
            self.fetch().start()
        if k > 0:
            if k == 1 and not self.born:
                self.fetch().wait()
            for copy in self.sends(k - 1):
                copy.wait()
            for b in range(len(singles(self.steps[k - 1]))):
                for i in range(self.m):
                    add_to(g(self.total), i, g(self.land[k - 1]), b * self.m + i, self.size[k])
        if k < self.j or self.close:
            for copy in self.sends(k):
                copy.start()
        if k == self.j and self.j:
            self.keep().start()

    def end(self):
        if self.close:
            for copy in self.sends(self.j):
                copy.wait()
        if self.j:
            self.keep().wait()

    def result(self, res):
        mine = res[self.out[1]] if self.j else self.whole
        return (mine, res[self.other[1]]) if self.close else mine


class Group:
    def __init__(self, kn, far, order, mats, rows_each, width=HALF):
        self.far, self.order, self.mats, self.rows = far, order, mats, rows_each
        self.n = SHARDS * rows_each
        self.buf = kn.mem((mats, 2 * self.n, width))
        if far:
            self.arr = kn.mem((mats, self.n, width))
        self.out = kn.out((mats, self.n if far else 2 * self.n, width), BF)
        self.sem = kn.sems(mats * SHARDS, 2)
        self.done = kn.sems(mats)

    def bind(self, get):
        self.ref = get
        self.sent = {i: [] for i in range(self.mats)}

    def locate(self):
        self.base = places(self.order, self.rows, self.far)

    def put(self, mat, tile, shards, first=0, pitch=None):
        put(self.ref(self.buf), mat, self.base, tile, shards, self.rows, first, pitch or self.rows)

    def leave(self, mat, start=0, n=None):
        if not self.far:
            return
        n = n or self.n
        self.sent[mat].append((start, n))
        self.copy(mat, len(self.sent[mat]) - 1).start()

    def copy(self, mat, i):
        g = self.ref
        start, n = self.sent[mat][i]
        source = g(self.buf).at[mat, pl.ds(self.n + start, n)]
        return remote(source, g(self.arr).at[mat, pl.ds(start, n)], g(self.sem), mat * SHARDS + i, CORE)

    def leave_shards(self, mat, first):
        if not self.far:
            return
        core = bit(lax.axis_index("rows"), 1)
        for x in range(2):
            for half in range(2):
                shard = first + 2 * x
                spot = jnp.where(core == 0, self.base[shard + 1, half], self.base[shard, half])
                self.leave(mat, pl.multiple_of(spot - self.n, 16), self.rows)

    def settle(self, mat):
        g = self.ref
        if self.far:
            for i in range(len(self.sent[mat])):
                self.copy(mat, i).wait()
            add_to(g(self.buf), mat, g(self.arr), mat, self.n)
        self.store(mat).start()

    def store(self, mat):
        g = self.ref
        n = self.n if self.far else 2 * self.n
        return pltpu.make_async_copy(g(self.buf).at[mat, pl.ds(0, n)], g(self.out).at[mat], g(self.done).at[mat])

    def end(self):
        for mat in range(self.mats):
            self.store(mat).wait()

    def result(self, res):
        return res[self.out[1]]


def pool_matrix(rows, cols):
    k = lax.broadcasted_iota(jnp.int32, (rows, cols), 0)
    t = lax.broadcasted_iota(jnp.int32, (rows, cols), 1)
    both = jnp.where((t == 2 * k) | (t == 2 * k - 1), 0.5, 0.0)
    return jnp.where((k == 0) & (t == 0), 1.0, both).astype(BF)


def pool_matrix_t(rows, cols):
    t = lax.broadcasted_iota(jnp.int32, (rows, cols), 0)
    k = lax.broadcasted_iota(jnp.int32, (rows, cols), 1)
    both = jnp.where((t == 2 * k) | (t == 2 * k - 1), 0.5, 0.0)
    return jnp.where((k == 0) & (t == 0), 1.0, both).astype(BF)


def head_masks():
    lane = lax.broadcasted_iota(jnp.int32, (1, 128), 1)
    first = jnp.where(lane < HEAD_DIM, 1.0, 0.0)
    return first.astype(BF), (1.0 - first).astype(BF)


def both_heads(x, masks):
    return jnp.concatenate([x * masks[0], x * masks[1]], axis=0)


QB = 128


def attn_fwd_step(stride, pairs, valid_ref, qw_ref, qr_ref, k_ref, v_ref, tab_ref, mixed_ref, inv_ref, p_ref):
    masks = head_masks()
    lane = lax.broadcasted_iota(jnp.int32, (1, 128), 1)
    keys = k_ref.shape[1]
    queries = qw_ref.shape[1]
    width = stride * QB + keys
    valid = valid_ref[0] > 0
    for pr in range(pairs):
        lanes = slice(pr * 128, (pr + 1) * 128)
        k = k_ref[0, :, lanes]
        v = jnp.concatenate([v_ref[0, :, lanes], jnp.ones((keys, 128), BF)], axis=1)
        outs = []
        for h in range(2):
            content = mm_nt(qw_ref[0, :, lanes] * (masks[h] * SCALE).astype(BF), k)
            relative = mm_nt(qr_ref[0, :, lanes] * (masks[h] * SCALE).astype(BF), tab_ref[:, lanes])
            parts = []
            for b in range(queries // QB):
                rows = slice(b * QB, (b + 1) * QB)
                t0 = stride * (queries - QB - b * QB)
                rolled = pltpu.roll(
                    relative[rows, t0 : t0 + width], width - stride * (QB - 1), 1, stride=stride, stride_axis=0
                )
                scores = jnp.where(valid, content[rows] + rolled[:, :keys], MASKED)
                terms = jnp.exp(scores - jnp.max(scores, axis=-1, keepdims=True)).astype(BF)
                p_ref[0, 2 * pr + h, rows, :] = terms
                parts.append(terms)
            outs.append(mm(jnp.concatenate(parts, axis=0), v))
        inv = 1.0 / jnp.where(lane < HEAD_DIM, outs[0][:, 128:], outs[1][:, 128:])
        inv_ref[0, :, lanes] = inv
        mixed_ref[0, :, lanes] = (jnp.where(lane < HEAD_DIM, outs[0][:, :128], outs[1][:, :128]) * inv).astype(BF)


def attn_fwd(stride, valid, qw, qr, k, v, tab, far=False, cid=None, extra=None):
    s, queries, _ = qw.shape
    keys = k.shape[1]
    table = tab.shape[0]
    pairs = 2
    steps = HEADS // 2 // pairs
    kn = Kernel()
    block = lambda n: pl.BlockSpec((1, n, 128 * pairs), lambda i, j: (i, 0, j))
    handles = [
        kn.inp(valid, pl.BlockSpec((1, 1, keys), lambda i, j: (i, 0, 0))),
        kn.inp(qw, block(queries)),
        kn.inp(qr, block(queries)),
        kn.inp(k, block(keys)),
        kn.inp(v, block(keys)),
        kn.inp(tab, pl.BlockSpec((table, 128 * pairs), lambda i, j: (0, j))),
        kn.out((s, queries, D), BF, block(queries)),
        kn.out((s, queries, D), F32, block(queries)),
        kn.out((s, HEADS, queries, keys), BF, pl.BlockSpec((1, 2 * pairs, queries, keys), lambda i, j: (i, j, 0, 0))),
    ]
    if extra is not None and far:
        part = extra.shape[1]
        h_ex, h_full, r_sem, l_sem = kn.inp(extra), kn.out((s, 2 * part, D), BF), kn.sems(1, 2), kn.sems(1)

    def body(get):
        if extra is not None and far:
            side = lax.axis_index("seq")
            here = get(h_full).at[:, pl.ds(side * part, part)]
            copies = lambda: (
                remote(get(h_ex).at[pl.ds((1 - side) * s, s)], here, get(r_sem), 0, ALONG_Y),
                pltpu.make_async_copy(get(h_ex).at[pl.ds(side * s, s)], here, get(l_sem).at[0]),
            )
            first = jnp.logical_and(pl.program_id(0) == 0, pl.program_id(1) == 0)
            end = jnp.logical_and(pl.program_id(0) == s - 1, pl.program_id(1) == steps - 1)

            @pl.when(first)
            def _():
                greet([ALONG_Y])
                for copy in copies():
                    copy.start()

        attn_fwd_step(stride, pairs, *[get(h) for h in handles])
        if extra is not None and far:

            @pl.when(end)
            def _():
                for copy in copies():
                    copy.wait()

    return kn.run(
        body,
        "attn_fwd_%d" % stride,
        cost(2 * s * HEADS * queries * keys * 64 * 4, 12 * MIB, s * HEADS * queries * keys),
        grid=(s, steps),
        cid=cid if extra is not None and far else None,
    )


def ffn_fwd(mixed, resid, w_out, w_up, w_down, w_qkv, attn_bias, up_bias, gain, nbias, obias):
    rows = mixed.shape[0]
    kn = Kernel()
    h_mixed, h_resid = kn.inp(mixed, VM), kn.inp(resid, VM)
    h_wout, h_up, h_down, h_qkv = (kn.inp(x) for x in (w_out, w_up, w_down, w_qkv))
    h_ab, h_upb, h_gain, h_nb, h_ob = (kn.inp(x, VM) for x in (attn_bias, up_bias, gain, nbias, obias))
    wout, wup, wdown, wqkv = kn.mem((D, D)), kn.mem((D, FF)), kn.mem((FF, D)), kn.mem((3, D, D))
    shapes = {"hid": (D, BF), "x1": (D, F32), "r1": (128, F32), "act": (FF, BF), "slope": (FF, BF), "x2": (D, F32)}
    shapes.update({"r2": (128, F32), "out": (D, F32), "low": (D, BF), "qw": (D, BF), "qr": (D, BF), "k": (D, BF), "v": (D, BF)})
    order = list(shapes)
    outs = {n: (kn.out((rows, c), t), kn.mem((rows, c), t)) for n, (c, t) in shapes.items()}
    l_sem, o_sem = kn.sems(4), kn.sems(len(order))
    h_total = kn.mem((rows, D), F32)

    def body(get):
        mem = lambda n: get(outs[n][1])
        store = lambda n: pltpu.make_async_copy(mem(n), get(outs[n][0]), get(o_sem).at[order.index(n)])
        pairs = ((get(h_wout).at[0], wout), (get(h_up).at[0], wup), (get(h_down).at[0], wdown), (get(h_qkv).at[1], wqkv))
        loads = [pltpu.make_async_copy(src, get(dst), get(l_sem).at[i]) for i, (src, dst) in enumerate(pairs)]
        for copy in loads:
            copy.start()
        gain_ref, nb_ref, ob_ref, ab_ref = get(h_gain), get(h_nb), get(h_ob), get(h_ab)
        loads[0].wait()
        x1, r1 = ln_fwd(get(h_resid)[...] + (mm(get(h_mixed)[...], get(wout)[...]) + ob_ref[0, 0:1, :]))
        mem("x1")[...] = x1
        mem("r1")[...] = jnp.broadcast_to(r1, (rows, 128))
        hidden = x1 * gain_ref[0, 0:1, :] + nb_ref[0, 0:1, :]
        mem("hid")[...] = hidden.astype(BF)
        for n in ("x1", "r1", "hid"):
            store(n).start()
        total = get(h_total)
        total[...] = hidden + ob_ref[0, 1:2, :]
        loads[1].wait()
        for c in range(0, PANELS, WIDE):
            cols = slice(c * D, (c + WIDE) * D)
            act, slope = gelu_and_slope(mm(mem("hid")[...], get(wup)[:, cols]) + get(h_upb)[0:1, cols])
            act = act.astype(BF)
            mem("act")[:, cols] = act
            mem("slope")[:, cols] = slope.astype(BF)
            if c == 0:
                loads[2].wait()
            total[...] += mm(act, get(wdown)[cols, :])
        store("act").start()
        store("slope").start()
        x2, r2 = ln_fwd(total[...])
        mem("x2")[...] = x2
        mem("r2")[...] = jnp.broadcast_to(r2, (rows, 128))
        out = x2 * gain_ref[0, 1:2, :] + nb_ref[0, 1:2, :]
        mem("out")[...] = out
        low = out.astype(BF)
        mem("low")[...] = low
        for n in ("x2", "r2", "out", "low"):
            store(n).start()
        loads[3].wait()
        q = mm(low, get(wqkv)[0])
        mem("qw")[...] = (q + ab_ref[1, 0:1, :]).astype(BF)
        mem("qr")[...] = (q + ab_ref[1, 1:2, :]).astype(BF)
        store("qw").start()
        store("qr").start()
        mem("k")[...] = mm(low, get(wqkv)[1]).astype(BF)
        store("k").start()
        mem("v")[...] = mm(low, get(wqkv)[2]).astype(BF)
        store("v").start()
        for n in order:
            store(n).wait()

    return kn.run(body, "ffn_fwd", cost(2 * rows * D * D * 12, 34 * MIB, rows * FF), limit=60)


def places(order, rows_each, far):
    me = lax.axis_index("rows") if far else 0
    side = lax.axis_index("seq") if far else 0
    base = {}
    for r in range(SHARDS):
        for half in range(2):
            spot = 0
            for axis, b in bits_of(order):
                c = half if axis == "seq" else (r // b) % 2
                mine = side if axis == "seq" else me
                spot = spot * 2 + (lax.rem(bit(mine, b) + c, 2) if far else c)
            base[r, half] = spot * rows_each
    return base


def put(buf_ref, mat, base, tile, shards, rows, first=0, pitch=None):
    low = tile.astype(BF)
    width = buf_ref.shape[2]
    for n, r in enumerate(shards):
        for half in range(2):
            start = base[r, half]
            if not isinstance(start, int):
                start = pl.multiple_of(start, 16)
            top = n * pitch + first
            buf_ref[mat, pl.ds(start, rows), :] = low[top : top + rows, half * width : (half + 1) * width]


NA = SHARDS * ROW
DOWN = 2
BORN_POINTS = ({1: 8, 2: 12}, {1: 12})
SMALL_STEPS = (
    (CORE,),
    (ALONG_X, ALONG_Y, (ALONG_X, ALONG_Y)),
    (Z_NEAR, Z_FAR, Z_DIAG),
)
FFN_ORDERS = ((XZY, YX, YX, ZYX, XY), (XZY, YX, YX, ZYX, ZYX))
ATT_ORDERS = (XY, YX)
DOWN_ROWS = UP_ROWS // DOWN


class FfnGrads:
    def __init__(self, kn, far, rows, layer):
        orders = FFN_ORDERS[layer]
        full = lambda shape: pl.BlockSpec(shape, lambda *g: (0,) * len(shape))
        self.dmixed = kn.out((rows, D), BF, full((rows, D)))
        self.dbranch = kn.out((rows, D), BF, full((rows, D)))
        self.dres = kn.out((rows, D), F32, full((rows, D)))
        self.small = kn.out((8, D), F32, full((8, D)))
        self.upg = kn.out((8, FF), F32, full((8, FF)))
        self.up = [Group(kn, far, orders[0], 3, ROW), Group(kn, far, orders[1], 1, ROW)]
        self.down = [Group(kn, far, order, 1, DOWN_ROWS) for order in orders[2:4]]
        self.outp = [Group(kn, far, orders[4], 1, ROW)]
        self.groups = self.up + self.down + self.outp
        self.wup, self.wdown = kn.mem((D, FF)), kn.mem((FF, D))
        self.act, self.slope = kn.mem((rows, FF)), kn.mem((rows, FF))
        self.dffn, self.dhid = kn.mem((rows, D)), kn.mem((rows, D), F32)
        self.near = kn.sems(4)

    def run(self, get, dy, x2, r2, gain2, gain1, wout_ref, hid_ref, mixed_ref, x1, r1, at):
        small_ref, upg_ref, dffn_ref, dhid_ref = get(self.small), get(self.upg), get(self.dffn), get(self.dhid)
        act, slope, wup, wdown = get(self.act), get(self.slope), get(self.wup), get(self.wdown)
        for group in self.groups:
            group.bind(get)
            group.locate()
        small_ref[...] = jnp.zeros_like(small_ref)
        dpost = ln_bwd(dy, x2, r2, gain2)
        small_ref[1:2, :] = jnp.sum(dy * x2, axis=0, keepdims=True)
        small_ref[3:4, :] = jnp.sum(dy, axis=0, keepdims=True)
        dffn = dpost.astype(BF)
        small_ref[5:6, :] = jnp.sum(dffn.astype(F32), axis=0, keepdims=True)
        dffn_ref[...] = dffn
        dhid_ref[...] = dpost
        at(0)
        each = SHARDS // PANELS
        for w in range(0, PANELS, WIDE):
            cols = slice(w * D, (w + WIDE) * D)
            dffn = dffn_ref[...]
            ddown = mm_tn(act[:, cols], dffn)
            shards = range(w * each, (w + WIDE) * each)
            for i, group in enumerate(self.down):
                group.put(0, ddown, shards, i * DOWN_ROWS, UP_ROWS)
                for p in range(w, w + WIDE):
                    group.leave_shards(0, p * each)
            dact = mm_nt(dffn, wdown[cols, :])
            dpre = (dact * slope[:, cols].astype(F32)).astype(BF)
            upg_ref[:, cols] = jnp.broadcast_to(jnp.sum(dpre.astype(F32), axis=0, keepdims=True), (8, WIDE * D))
            dup = mm_tn(hid_ref[...], dpre)
            for i in range(WIDE):
                group, mat = (self.up[0], w + i) if w + i < 3 else (self.up[1], 0)
                group.put(mat, dup[:, i * D : (i + 1) * D], range(SHARDS))
                group.leave(mat)
            dhid_ref[...] += mm_nt(dpre, wup[:, cols])
            if w + WIDE >= PANELS:
                self.up[0].settle(0)
                self.up[0].settle(1)
            at(w // WIDE + 1)
        dhid = dhid_ref[...]
        xh = x1()
        small_ref[0:1, :] = jnp.sum(dhid * xh, axis=0, keepdims=True)
        small_ref[2:3, :] = jnp.sum(dhid, axis=0, keepdims=True)
        dres = ln_bwd(dhid, xh, r1(), gain1)
        get(self.dres)[...] = dres
        dbranch = dres.astype(BF)
        get(self.dbranch)[...] = dbranch
        small_ref[4:5, :] = jnp.sum(dbranch.astype(F32), axis=0, keepdims=True)
        for group in self.outp:
            group.put(0, mm_tn(mixed_ref[...], dbranch), range(SHARDS))
            group.leave(0)
        get(self.dmixed)[...] = mm_nt(dbranch, wout_ref[0]).astype(BF)
        for group in self.down:
            group.settle(0)
        self.up[0].settle(2)
        self.up[1].settle(0)
        for group in self.outp:
            group.settle(0)
        for group in self.groups:
            group.end()

    def results(self, res):
        own = [res[h[1]] for h in (self.dmixed, self.dbranch, self.dres, self.small, self.upg)]
        return own, [group.result(res) for group in self.groups]


def ffn_last(far, cid, mixed, resid, cot, w_out, w_up, w_down, up_bias, gain, nbias, obias):
    rows = mixed.shape[0]
    kn = Kernel()
    whole = pl.BlockSpec((rows, D), lambda i: (0, 0))
    layer = pl.BlockSpec((1, 2, D), lambda i: (1, 0, 0))
    h_mixed, h_resid, h_cot = (kn.inp(x, whole) for x in (mixed, resid, cot))
    h_wout = kn.inp(w_out, pl.BlockSpec((1, D, D), lambda i: (1, 0, 0)))
    h_up, h_down = kn.inp(w_up), kn.inp(w_down)
    h_upb = kn.inp(up_bias, pl.BlockSpec((2, FF), lambda i: (0, 0)))
    h_gain, h_nbias, h_obias = (kn.inp(x, layer) for x in (gain, nbias, obias))
    h_lout = kn.out((rows, D), BF, whole)
    grads = FfnGrads(kn, far, rows, 1)
    h_hid, h_x1 = kn.mem((rows, D)), kn.mem((rows, D), F32)

    def body(get):
        if far:
            greet([CORE])
        near = get(grads.near)
        wup, wdown, act, slope, hid, x1s = (
            get(h) for h in (grads.wup, grads.wdown, grads.act, grads.slope, h_hid, h_x1)
        )
        dhid_s = get(grads.dhid)
        gain_ref, nbias_ref, obias_ref, upb_ref, wout_ref = (
            get(h) for h in (h_gain, h_nbias, h_obias, h_upb, h_wout)
        )
        cp_up = pltpu.make_async_copy(get(h_up).at[1], wup, near.at[0])
        cp_down = pltpu.make_async_copy(get(h_down).at[1], wdown, near.at[1])
        cp_up.start()
        cp_down.start()
        pre_norm = get(h_resid)[...] + (mm(get(h_mixed)[...], wout_ref[0]) + obias_ref[0, 0:1, :])
        x1, r1 = ln_fwd(pre_norm)
        x1s[...] = x1
        hidden = x1 * gain_ref[0, 0:1, :] + nbias_ref[0, 0:1, :]
        hid[...] = hidden.astype(BF)
        dhid_s[...] = hidden + obias_ref[0, 1:2, :]
        cp_up.wait()
        cp_down.wait()
        for c in range(0, PANELS, WIDE):
            cols = slice(c * D, (c + WIDE) * D)
            a, s = gelu_and_slope(mm(hid[...], wup[:, cols]) + upb_ref[1:2, cols])
            a = a.astype(BF)
            act[:, cols] = a
            slope[:, cols] = s.astype(BF)
            dhid_s[...] += mm(a, wdown[cols, :])
        x2, r2 = ln_fwd(dhid_s[...])
        get(h_lout)[...] = (x2 * gain_ref[0, 1:2, :] + nbias_ref[0, 1:2, :]).astype(BF)
        grads.run(
            get, get(h_cot)[...].astype(F32), x2, r2, gain_ref[0, 1:2, :], gain_ref[0, 0:1, :], wout_ref, hid,
            get(h_mixed), lambda: x1s[...], lambda: r1, lambda point: None,
        )

    res = kn.run(
        body, "ffn_last", cost(2 * rows * D * D * 26, 30 * MIB, rows * FF), grid=(1,), cid=cid if far else None, limit=63
    )
    return res[h_lout[1]], *grads.results(res)


def ffn_bwd(far, cid, chains, lout, dy, x2, r2, hid, mixed, x1, r1, gain, w_out, w_up, w_down, act, slope):
    rows = hid.shape[0]
    seqs, queries, _ = lout.shape
    kn = Kernel()
    whole = pl.BlockSpec((rows, D), lambda i: (0, 0))
    thin = pl.BlockSpec((rows, 128), lambda i: (0, 0))
    h_dy, h_x2, h_hid, h_mixed, h_x1 = (kn.inp(x, whole) for x in (dy, x2, hid, mixed, x1))
    h_r2, h_r1 = (kn.inp(x, thin) for x in (r2, r1))
    h_gain = kn.inp(gain, pl.BlockSpec((1, 2, D), lambda i: (0, 0, 0)))
    h_wout = kn.inp(w_out, pl.BlockSpec((1, D, D), lambda i: (0, 0, 0)))
    h_up, h_down, h_act, h_slope = (kn.inp(x) for x in (w_up, w_down, act, slope))
    grads = FfnGrads(kn, far, rows, 0)
    links = [Chain(kn, *c[:3]) for c in chains]
    if far:
        h_lout, h_got = kn.inp(lout), kn.out((seqs, queries // 2, D), BF)
        h_swap = kn.sems(1, 2)

    def body(get):
        near = get(grads.near)
        if far:
            greet([CORE, ALONG_X, ALONG_Y, Z_ALL])
            side = lax.axis_index("seq")
            swap_lout = remote(
                get(h_lout).at[:, pl.ds((1 - side) * (queries // 2), queries // 2)], get(h_got), get(h_swap), 0, ALONG_Y
            )
        for link in links:
            link.bind(get)
            link.go(0)
        loads = [
            pltpu.make_async_copy(get(h_act), get(grads.act), near.at[0]),
            pltpu.make_async_copy(get(h_down).at[0], get(grads.wdown), near.at[1]),
            pltpu.make_async_copy(get(h_slope), get(grads.slope), near.at[2]),
            pltpu.make_async_copy(get(h_up).at[0], get(grads.wup), near.at[3]),
        ]
        for copy in loads:
            copy.start()

        def at(point):
            if point == 0:
                for copy in loads:
                    copy.wait()
            for link, (_, _, _, when) in zip(links, chains):
                if point in when:
                    link.go(when[point])
            if far and point == 1:
                swap_lout.start()

        gain_ref = get(h_gain)
        grads.run(
            get, get(h_dy)[...], get(h_x2)[...], get(h_r2)[:, 0:1], gain_ref[0, 1:2, :], gain_ref[0, 0:1, :],
            get(h_wout), get(h_hid), get(h_mixed), lambda: get(h_x1)[...], lambda: get(h_r1)[:, 0:1], at,
        )
        for link, (_, _, close, _) in zip(links, chains):
            if not close:
                link.go(link.j)
        for link in links:
            link.end()
        if far:
            swap_lout.wait()

    res = kn.run(
        body, "ffn_bwd", cost(2 * rows * D * D * 18, 40 * MIB), grid=(1,), cid=cid if far else None, limit=63
    )
    return *grads.results(res), [link.result(res) for link in links], res[h_got[1]] if far else None


def attn_bwd_step(
    stride, seq, lanes, p_ref, inv_ref, qw_ref, qr_ref, k_ref, v_ref, tab_ref, dm_ref, dq, dk_out, dv_out, dtab, dbias
):
    masks = head_masks()
    lane = lax.broadcasted_iota(jnp.int32, (1, 128), 1)
    first = lane < HEAD_DIM
    keys = k_ref.shape[1]
    queries = qw_ref.shape[1]
    blocks = queries // QB
    width = stride * QB + keys
    flip_i = lax.broadcasted_iota(jnp.int32, (queries, queries), 0)
    flip_j = lax.broadcasted_iota(jnp.int32, (queries, queries), 1)
    flip = jnp.where(flip_i + flip_j == queries - 1, 1.0, 0.0).astype(BF)

    @pl.when(seq == 0)
    def _():
        dtab[:, lanes] = jnp.zeros((dtab.shape[0], 128), F32)
        dbias[:, lanes] = jnp.zeros((dbias.shape[0], 128), F32)

    k = k_ref[0]
    v = v_ref[0]
    inv = inv_ref[0]
    scaled = (dm_ref[0].astype(F32) * inv).astype(BF)
    qr_rev = mm(flip, qr_ref[0]).astype(BF)
    dk = jnp.zeros((keys, 128), F32)
    dv = jnp.zeros((keys, 128), F32)
    dqws, dqrs = [], []
    for h in range(2):
        dmh = scaled * masks[h]
        terms = p_ref[0, h]
        dprob = mm_nt(dmh, v)
        wide = terms.astype(F32)
        inner = jnp.sum(dprob * wide, axis=-1, keepdims=True) * inv[:, h * HEAD_DIM : h * HEAD_DIM + 1]
        ds = (wide * (dprob - inner)).astype(BF)
        dv = dv + mm_tn(terms, dmh)
        dk = dk + mm_tn(ds, qw_ref[0] * masks[h])
        dqws.append(mm(ds, k))
        rev = mm(flip, ds)
        back = []
        for b in range(blocks):
            rows = slice(b * QB, (b + 1) * QB)
            t0 = stride * b * QB
            padded = jnp.concatenate([rev[rows], jnp.zeros((QB, width - keys), F32)], axis=1)
            rel = pltpu.roll(padded, 0, 1, stride=stride, stride_axis=0).astype(BF)
            dtab[t0 : t0 + width, lanes] += mm_tn(rel, qr_rev[rows] * masks[h]) * SCALE
            back.append(mm(rel, tab_ref[t0 : t0 + width, :]))
        dqrs.append(jnp.concatenate(back, axis=0))
    dqw = jnp.where(first, dqws[0], dqws[1]) * SCALE
    hi, lo = split_hi_lo(jnp.where(first, dqrs[0], dqrs[1]))
    dqr = (mm(flip, hi) + mm(flip, lo)) * SCALE
    dq[pl.ds(pl.multiple_of(seq * queries, QB), queries), lanes] = (dqw + dqr).astype(BF)
    at = pl.ds(pl.multiple_of(seq * keys, QB), keys)
    dk_out[at, lanes] = (dk * SCALE).astype(BF)
    dv_out[at, lanes] = dv.astype(BF)
    dbias[0:1, lanes] += jnp.sum(dqw, axis=0, keepdims=True)
    dbias[1:2, lanes] += jnp.sum(dqr, axis=0, keepdims=True)


def back_layer(
    far, cid, layer, plan, p, inv, qw, qr, k, v, tab, dmixed, dres, w_qkv, xq, xk, enc, smalls=None
):
    s, queries, _ = qw.shape
    keys = k.shape[1]
    table = tab.shape[0]
    last = s * (HEADS // 2)
    nq, nk = s * queries, s * keys
    tail = smalls is not None
    kn = Kernel()
    seq_of = lambda g: lax.rem(jnp.minimum(g, last - 1), s)
    pair_of = lambda g: lax.div(jnp.minimum(g, last - 1), s)
    pair_block = lambda n: pl.BlockSpec((1, n, 128), lambda g: (seq_of(g), 0, pair_of(g)))
    h_p = kn.inp(p, pl.BlockSpec((1, 2, queries, keys), lambda g: (seq_of(g), pair_of(g), 0, 0)))
    h_inv, h_qw, h_qr, h_dm = (kn.inp(x, pair_block(queries)) for x in (inv, qw, qr, dmixed))
    h_k, h_v = (kn.inp(x, pair_block(keys)) for x in (k, v))
    h_tab = kn.inp(tab, pl.BlockSpec((table, 128), lambda g: (0, pair_of(g))))
    dq_s, dk_s, dv_s = kn.mem((nq, D)), kn.mem((nk, D)), kn.mem((nk, D))
    dtab_s, dbias_s = kn.mem((table, D), F32), kn.mem((8, D), F32)
    late = [(dres, F32), (xq, BF), (enc, BF)]
    if layer == 0 or xk is not xq:
        late.append((xk, BF))
    late_in = [kn.inp(x) for x, _ in late]
    late_mem = [kn.mem(x.shape, t) for x, t in late]
    h_w, h_wm = kn.inp(w_qkv), kn.mem((3, D, D))
    l_sem = kn.sems(len(late) + 1)
    chains = [Chain(kn, so_far, steps, close) for so_far, steps, close, _ in plan]
    whole = lambda shape: pl.BlockSpec(shape, lambda g: (0,) * len(shape))
    half = keys // 2
    born, groups = [], []
    for _ in range(BLOCKS):
        if tail and far:
            born += [Chain(kn, None, o[1:], True, (kn.mem((2, 2 * NA, BLOCK)), 2, NA, BLOCK)) for o in ATT_ORDERS]
        else:
            groups += [Group(kn, far, o, 2, ROW, BLOCK) for o in ATT_ORDERS]
    if tail and far:
        h_small = [kn.inp(x, whole(x.shape)) for x in smalls]
        sum_shape = (2 * SMALL_ROWS, D)
        h_sum = kn.out(sum_shape, F32, whole(sum_shape))
        sm = [kn.mem(sum_shape, F32) for _ in range(len(SMALL_STEPS))]
        sm_in = [kn.mem(sum_shape, F32) for step in SMALL_STEPS for _ in step]
        sm_sem = kn.sems(len(sm_in), 2)
        h_dx = kn.out((s, half, D), F32, whole((s, half, D)))
        h_piece, h_got, h_swap = kn.mem((s, half, D)), kn.out((s, half, D), BF), kn.sems(s, 2)
    else:
        h_dx = kn.out((nk, D), F32, whole((nk, D)))
        h_bias = kn.out((8, D), F32, whole((8, D)))
    greeted = [step for _, steps, _, _ in plan for step in steps] + [CORE]
    if tail:
        greeted = [CORE, ALONG_X, ALONG_Y, (ALONG_X, ALONG_Y), Z_ALL]

    def body(get):
        g = pl.program_id(0)
        dq, dk, dv, dtab, dbias = (get(h) for h in (dq_s, dk_s, dv_s, dtab_s, dbias_s))
        loads = [pltpu.make_async_copy(get(a), get(b), get(l_sem).at[i]) for i, (a, b) in enumerate(zip(late_in, late_mem))]
        loads.append(pltpu.make_async_copy(get(h_w).at[layer], get(h_wm), get(l_sem).at[len(late)]))
        for chain in chains + born:
            chain.bind(get)

        @pl.when(g == 0)
        def _():
            if far:
                greet(greeted)
            for copy in loads:
                copy.start()

        @pl.when(g < last)
        def _():
            lanes = pl.ds(pl.multiple_of(pair_of(g) * 128, 128), 128)
            attn_bwd_step(
                2 - layer, seq_of(g), lanes, get(h_p), get(h_inv), get(h_qw), get(h_qr), get(h_k), get(h_v), get(h_tab), get(h_dm),
                dq, dk, dv, dtab, dbias,
            )

        for point in range(last):
            acts = [(c, k) for c, (_, _, _, when) in zip(chains, plan) for k, w in when.items() if w == point]
            if acts:

                @pl.when(g == point)
                def _():
                    for chain, k in acts:
                        chain.go(k)

        dres_ref, xq_ref, enc_ref = (get(h) for h in late_mem[:3])
        xk_ref = get(late_mem[3]) if layer == 0 or xk is not xq else xq_ref
        for group in groups:
            group.bind(get)
        per = last // BLOCKS

        def swap_piece(i):
            return remote(get(h_piece).at[i], get(h_got).at[i], get(h_swap), i, ALONG_Y)

        def make(t):
            cols = slice(2 * t * BLOCK, 2 * (t + 1) * BLOCK)
            return (
                (1, 0, lambda: mm_tn(xk_ref[...], dv[:, cols])),
                (0, 0, lambda: mm_tn(xq_ref[...], dq[:, cols])),
                (1, 1, lambda: mm_tn(enc_ref[...], dtab[:, cols].astype(BF))),
                (0, 1, lambda: mm_tn(xk_ref[...], dk[:, cols])),
            )

        def gradients(t):
            bases = [places(order, ROW, far) for order in ATT_ORDERS]
            for group in groups:
                group.locate()
            for which, mat, tile in make(t):
                if tail and far:
                    chain = born[2 * t + which]
                    put(get(chain.total), mat, bases[which], tile(), range(SHARDS), ROW, 0, ROW)
                    chain.core(mat).start()
                else:
                    groups[2 * t + which].put(mat, tile(), range(SHARDS))
                    groups[2 * t + which].leave(mat)

        def settled(t):
            for which, mat, _ in make(t):
                if tail and far:
                    born[2 * t + which].first(mat)
                else:
                    groups[2 * t + which].settle(mat)

        for t in range(BLOCKS):

            @pl.when(g == (t + 1) * per - 1)
            def _():
                if t == 0:
                    for copy in loads:
                        copy.wait()
                gradients(t)

            if t < BLOCKS - 1:

                @pl.when(g == (t + 1) * per)
                def _():
                    settled(t)

                for chain in born[2 * t : 2 * t + 2]:
                    for k, point in BORN_POINTS[t].items():

                        @pl.when(g == point)
                        def _():
                            chain.go(k)

        @pl.when(g == last)
        def _():
            w = get(h_wm)
            dx_ref = get(h_dx)

            def at(point):
                for chain, (_, _, _, when) in zip(chains, plan):
                    for step, due in when.items():
                        if due == point:
                            chain.go(step)

            if tail and far:
                small_start(get, dbias)
            settled(BLOCKS - 1)
            if tail and far:
                small_round(get, 0)
            at(last)
            if layer == 1:
                dx_ref[...] = dres_ref[...] + (mm_nt(dq[...], w[0]) + mm_nt(dk[...], w[1]) + mm_nt(dv[...], w[2]))
            else:
                spread = pool_matrix_t(keys, queries)
                side = lax.axis_index("seq") if far else 0
                for i in range(s):
                    q_at, k_at = slice(i * queries, (i + 1) * queries), slice(i * keys, (i + 1) * keys)
                    hi, lo = split_hi_lo(dres_ref[q_at, :] + mm_nt(dq[q_at, :], w[0]))
                    dtok = mm_nt(dk[k_at, :], w[1]) + mm_nt(dv[k_at, :], w[2]) + (mm(spread, hi) + mm(spread, lo))
                    if tail and far:
                        low_half, high_half = dtok[:half], dtok[half:]
                        is_low = side == 0
                        dx_ref[i] = jnp.where(is_low, low_half, high_half)
                        get(h_piece)[i] = jnp.where(is_low, high_half, low_half).astype(BF)
                        swap_piece(i).start()
                    else:
                        dx_ref[k_at, :] = dtok
            at(last + 1)
            if tail and far:
                finish_tail(get, swap_piece)
                return
            get(h_bias)[...] = dbias[...]
            for chain in chains:
                chain.go(chain.j)
            for group in groups:
                group.end()
            for chain in chains:
                chain.end()

    def small_copies(get, k):
        top = sum(len(step) for step in SMALL_STEPS[:k])
        came = [get(h) for h in sm_in]
        return [
            (came[top + i], remote(get(sm[k]), came[top + i], get(sm_sem), top + i, one))
            for i, one in enumerate(SMALL_STEPS[k])
        ]

    def small_start(get, dbias):
        own = get(sm[0])
        small0, upg0, small1, upg1, bias1 = (get(h) for h in h_small)
        for top, small, upg, bias in ((0, small0, upg0, dbias), (SMALL_ROWS, small1, upg1, bias1)):
            own[top : top + 6, :] = small[0:6, :]
            own[top + 6 : top + 8, :] = bias[0:2, :]
            for p in range(PANELS):
                own[top + 8 + p : top + 9 + p, :] = upg[0:1, p * D : (p + 1) * D]
        for _, copy in small_copies(get, 0):
            copy.start()

    def small_round(get, k):
        pieces = small_copies(get, k)
        for _, copy in pieces:
            copy.wait()
        own = get(sm[k])
        dst = get(sm[k + 1]) if k + 1 < len(SMALL_STEPS) else get(h_sum)
        if len(pieces) == 1:
            dst[...] = own[...] + pieces[0][0][...]
        else:
            a, b, c = (ref[...] for ref, _ in pieces)
            dst[...] = (own[...] + a) + (b + c)
        if k + 1 < len(SMALL_STEPS):
            for _, copy in small_copies(get, k + 1):
                copy.start()

    def finish_tail(get, swap_piece):
        pending = {c: max(when) + 1 for c, (_, _, _, when) in zip(chains, plan)}
        for t in range(BLOCKS):
            for chain in born[2 * t : 2 * t + 2]:
                pending[chain] = max(BORN_POINTS[t]) + 1 if t < BLOCKS - 1 else 1
        order = born[2:4] + chains[:5] + born[4:] + born[:2] + chains[5:]
        for r in range(5):
            for chain in order:
                k = pending[chain]
                if k <= chain.j:
                    chain.go(k)
                    pending[chain] = k + 1
            if r + 1 < len(SMALL_STEPS):
                small_round(get, r + 1)
        for chain in order:
            chain.end()
        for i in range(s):
            swap_piece(i).wait()

    flops = 2 * s * HEADS * queries * keys * 64 * 9 + 2 * D * D * (4 * nq + 4 * nk + table)
    res = kn.run(
        body, "back_layer_%d" % layer, cost(flops, 40 * MIB), grid=(last + 1,), cid=cid if far else None, limit=62
    )
    moved = [chain.result(res) for chain in chains]
    if tail and far:
        return res[h_dx[1]], res[h_got[1]], res[h_sum[1]], moved, [chain.result(res) for chain in born]
    return res[h_dx[1]], res[h_bias[1]], moved, [group.result(res) for group in groups]


def steps_of(distances):
    half_width = D // 2
    frequency = 10000.0 ** (-jnp.arange(half_width, dtype=F32) / half_width)
    angles = distances.astype(F32)[:, None] * frequency[None, :]
    return jnp.stack([jnp.sin(angles), jnp.cos(angles)])


FINE = 32


def prologue(far, cid, tokens, w_qkv, w_pos, attn_bias):
    parts = 2 if far else 1
    s, part_len = tokens.shape[0] // parts, tokens.shape[1]
    length = part_len * parts
    queries = length // 2
    table = 2 * length
    coarse = steps_of(2 * (queries - 1) - FINE * jnp.arange(table // FINE, dtype=jnp.int32))
    fine = steps_of(-jnp.arange(FINE, dtype=jnp.int32))
    fine2 = steps_of(-2 * jnp.arange(FINE // 2, dtype=jnp.int32))
    kn = Kernel()
    h_tok, h_w, h_wp = (kn.inp(x) for x in (tokens, w_qkv, w_pos))
    h_coarse, h_fine, h_fine2, h_bias = (kn.inp(x, VM) for x in (coarse, fine, fine2, attn_bias))
    names = {}

    def result(name, shape, dtype=BF):
        names[name] = (kn.out(shape, dtype), kn.mem(shape, dtype))

    result("tok", (s, length, D))
    result("enc0", (table, D))
    result("enc1", (table // 2, D))
    result("tab0", (table, D))
    result("tab1", (table // 2, D))
    result("pooled", (s * queries, D), F32)
    for name in ("low", "qw", "qr"):
        result(name, (s * queries, D))
    for name in ("k", "v"):
        result(name, (s, length, D))
    h_wm, h_wpm = kn.mem((3, D, D)), kn.mem((2, D, D))
    o_sem, l_sem, r_sem = kn.sems(len(names)), kn.sems(3), kn.sems(1, 2)
    order = list(names)

    def body(get):
        mem = lambda name: get(names[name][1])

        def store(name):
            return pltpu.make_async_copy(mem(name), get(names[name][0]), get(o_sem).at[order.index(name)])

        ls = get(l_sem)
        tok = mem("tok")
        if far:
            side = lax.axis_index("seq")
            mine, other = pl.ds(side * s, s), pl.ds((1 - side) * s, s)
            greet([ALONG_Y])
            here = pl.ds(side * part_len, part_len)
            sends = [remote(get(h_tok).at[other], tok.at[:, here], get(r_sem), 0, ALONG_Y)]
            loads = [pltpu.make_async_copy(get(h_tok).at[mine], tok.at[:, here], ls.at[0])]
        else:
            sends = []
            loads = [pltpu.make_async_copy(get(h_tok), tok, ls.at[0])]
        loads += [
            pltpu.make_async_copy(get(h_wp), get(h_wpm), ls.at[1]),
            pltpu.make_async_copy(get(h_w).at[0], get(h_wm), ls.at[2]),
        ]
        for copy in sends + loads:
            copy.start()
        w = get(h_wm)

        def encode(dst, table_rows, fine_ref):
            n = fine_ref.shape[1]
            fs, fc = fine_ref[0], fine_ref[1]
            for a in range(table_rows // n):
                cs, cc = get(h_coarse)[0, a : a + 1, :], get(h_coarse)[1, a : a + 1, :]
                dst[a * n : (a + 1) * n, :HALF] = (cs * fc + cc * fs).astype(BF)
                dst[a * n : (a + 1) * n, HALF:] = (cc * fc - cs * fs).astype(BF)

        encode(mem("enc0"), table, get(h_fine))
        store("enc0").start()
        encode(mem("enc1"), table // 2, get(h_fine2))
        store("enc1").start()
        loads[1].wait()
        wp = get(h_wpm)
        mem("tab0")[...] = mm(mem("enc0")[...], wp[0]).astype(BF)
        store("tab0").start()
        mem("tab1")[...] = mm(mem("enc1")[...], wp[1]).astype(BF)
        store("tab1").start()
        for i in (0, 2):
            loads[i].wait()

        def keys_of(part):
            for i in range(s):
                x = tok[i, part, :]
                mem("k")[i, part, :] = mm(x, w[1]).astype(BF)
                mem("v")[i, part, :] = mm(x, w[2]).astype(BF)

        if far:
            keys_of(pl.ds(pl.multiple_of(side * part_len, part_len), part_len))
            for copy in sends:
                copy.wait()
            store("tok").start()
            keys_of(pl.ds(pl.multiple_of((1 - side) * part_len, part_len), part_len))
        else:
            store("tok").start()
            keys_of(pl.ds(0, length))
        store("k").start()
        store("v").start()
        gather = pool_matrix(queries, length)
        for i in range(s):
            at = slice(i * queries, (i + 1) * queries)
            pooled = mm(gather, tok[i])
            mem("pooled")[at, :] = pooled
            low = pooled.astype(BF)
            mem("low")[at, :] = low
            q = mm(low, w[0])
            mem("qw")[at, :] = (q + get(h_bias)[0, 0:1, :]).astype(BF)
            mem("qr")[at, :] = (q + get(h_bias)[0, 1:2, :]).astype(BF)
        for name in ("pooled", "low", "qw", "qr"):
            store(name).start()
        for name in order:
            store(name).wait()

    res = kn.run(
        body, "prologue", cost(2 * D * D * (3 * s * length + 2 * table), 30 * MIB), cid=cid if far else None
    )
    found = {name: res[h[0][1]] for name, h in names.items()}
    return found


def finish(done, sums, dtok, got, lout, lout_got):
    s, half, _ = dtok.shape
    q = lout_got.shape[1]
    names = [kind % (0, t) for t in range(BLOCKS) for kind in ("qk%d%d", "vp%d%d")]
    names += ["ua0", "ub0", "da0", "db0", "out0"]
    names += [kind % (1, t) for t in range(BLOCKS) for kind in ("qk%d%d", "vp%d%d")]
    names += ["ua1", "ub1", "da1", "db1", "out1"]
    kn = Kernel()
    hs = {n: (kn.inp(m, VM), kn.inp(o, VM)) for n, (m, o) in zip(names, done)}
    h_sum, h_dtok, h_got, h_lgot = (kn.inp(x, VM) for x in (sums, dtok, got, lout_got))
    h_lout = kn.inp(lout)
    o_lout = kn.out((2 * s, q, D), BF, VM)
    o_tok = kn.out((2 * s, half, D), F32, VM)
    o_qkv = kn.out((2, 3, ROW, D), F32, VM)
    o_out, o_pos = (kn.out((2, ROW, D), F32, VM) for _ in range(2))
    o_up = kn.out((2, ROW, FF), F32, VM)
    o_down = kn.out((2, UP_ROWS, D), F32, VM)
    o_attn = kn.out((2, 2, ROW), F32, VM)
    o_upb = kn.out((2, FF // SHARDS), F32, VM)
    o_gain, o_nb, o_ob = (kn.out((2, 2, ROW), F32, VM) for _ in range(3))
    h_lmem, h_sem = kn.mem((s, q, D)), kn.sems(1)

    def body(get):
        side, me = lax.axis_index("seq"), lax.axis_index("rows")
        copy = pltpu.make_async_copy(
            get(h_lout).at[:, pl.ds(pl.multiple_of(side * q, q), q)], get(h_lmem), get(h_sem).at[0]
        )
        copy.start()
        mine, other = pl.ds(side * s, s), pl.ds((1 - side) * s, s)
        get(o_tok)[mine] = get(h_dtok)[...]
        get(o_tok)[other] = get(h_got)[...].astype(F32)
        get(o_lout)[other] = get(h_lgot)[...]

        def halves(name, mat, dst, lead, base=0, rows=slice(None)):
            for h, which in zip(hs[name], (side, 1 - side)):
                width = get(h).shape[2]
                lanes = pl.ds(pl.multiple_of(base + which * width, 128), width)
                dst[(*lead, rows, lanes)] = get(h)[mat].astype(F32)

        for l in range(2):
            at = lambda name: "%s%d" % (name, l)
            for t in range(BLOCKS):
                for i, (kind, mat) in enumerate((("qk", 0), ("qk", 1), ("vp", 0))):
                    halves("%s%d%d" % (kind, l, t), mat, get(o_qkv), (l, i), 2 * t * BLOCK)
                halves("vp%d%d" % (l, t), 1, get(o_pos), (l,), 2 * t * BLOCK)
            halves(at("out"), 0, get(o_out), (l,))
            for p in range(PANELS):
                halves(at("ua") if p < 3 else at("ub"), p % 3, get(o_up), (l,), p * D)
            for i, name in enumerate(("da", "db")):
                halves(at(name), 0, get(o_down), (l,), rows=slice(i * DOWN_ROWS, (i + 1) * DOWN_ROWS))
        both = get(h_sum)[...]
        turned = pltpu.roll(both, lax.rem(D - me * ROW, D), 1)
        for l in range(2):
            r = 12 * l
            for o, row in ((o_gain, 0), (o_nb, 2), (o_ob, 4), (o_attn, 6)):
                get(o)[l] = turned[r + row : r + row + 2, :ROW]
        wide = FF // SHARDS
        per = D // wide
        shifted = pltpu.roll(both, lax.rem(D - lax.rem(me, per) * wide, D), 1)
        for l in range(2):
            picked = jnp.zeros((1, D), F32)
            for p in range(PANELS):
                picked = picked + jnp.where(lax.div(me, per) == p, shifted[12 * l + 8 + p : 12 * l + 9 + p, :], 0.0)
            get(o_upb)[l : l + 1, :] = picked[:, :wide]
        copy.wait()
        get(o_lout)[mine] = get(h_lmem)[...]

    return tuple(kn.run(body, "finish", cost(1e6, 16 * MIB)))


def swap(x, axis, b):
    n = lax.axis_size(axis)
    return lax.ppermute(x, axis, [(i, i ^ b) for i in range(n)])


def natural(both, order, rows_each):
    mats = both.shape[0]
    both = both.reshape(mats, 2, 2, 2, 2, 2, rows_each, both.shape[-1])
    at = {step: 1 + i for i, step in enumerate(bits_of(order))}
    return both.transpose(0, at[Z_FAR], at[Z_NEAR], at[ALONG_X], at[CORE], 6, at[ALONG_Y], 7)


def to_sequences(x, side, parts):
    own = x.shape[0] // parts
    mine = lax.dynamic_slice_in_dim(x, side * own, own, 0)
    other = swap(lax.dynamic_slice_in_dim(x, (1 - side) * own, own, 0), "seq", 1)
    return jnp.where(
        side == 0, jnp.concatenate([mine, other], axis=1), jnp.concatenate([other, mine], axis=1)
    )


def to_positions(x, side, parts, wire):
    own = x.shape[1] // parts
    mine = lax.dynamic_slice_in_dim(x, side * own, own, 1)
    other = swap(lax.dynamic_slice_in_dim(x, (1 - side) * own, own, 1).astype(wire), "seq", 1).astype(x.dtype)
    return jnp.where(
        side == 0, jnp.concatenate([mine, other], axis=0), jnp.concatenate([other, mine], axis=0)
    )


def elsewhere(att0, ffn0, att1, ffn1, smalls, n_rows, me):
    flat = lambda x: x.reshape(x.shape[0], -1, x.shape[-1] * x.shape[-2])
    rows = lambda x, order: flat(natural(x, order, ROW))
    total = lambda x: lax.psum(lax.psum_scatter(x, "rows", scatter_dimension=1, tiled=True).astype(F32), "seq")

    def down(a, b):
        parts = [natural(x, order, DOWN_ROWS) for x, order in zip((a, b), FFN_ORDERS[0][2:4])]
        return flat(jnp.concatenate(parts, axis=5))

    def att(x):
        both = [jnp.concatenate([rows(b, o) for b, o in zip(x[2 * t : 2 * t + 2], ATT_ORDERS)]) for t in range(BLOCKS)]
        return total(jnp.concatenate(both, axis=2))

    att0, att1 = att(att0), att(att1)
    outs = [total(rows(f[4], FFN_ORDERS[l][4])) for l, f in enumerate((ffn0, ffn1))]
    ups = [total(jnp.concatenate([rows(x, o) for x, o in zip(f[:2], FFN_ORDERS[0])])) for f in (ffn0, ffn1)]
    downs = [total(down(f[2], f[3])) for f in (ffn0, ffn1)]
    sums = lax.psum(smalls, ("rows", "seq")).reshape(2, -1, D)
    own = D // n_rows
    cut = lambda x: lax.dynamic_slice_in_dim(x, me * own, own, 2)
    upb = lax.dynamic_slice_in_dim(sums[:, 8:].reshape(2, FF), me * (FF // n_rows), FF // n_rows, 1)
    panels = lambda x: jnp.concatenate(list(x), axis=1)
    return (
        jnp.stack([att0[:3], att1[:3]]),
        jnp.concatenate(outs),
        jnp.stack([att0[3], att1[3]]),
        jnp.stack([panels(x) for x in ups]),
        jnp.concatenate(downs),
        cut(sums[:, 6:8]),
        upb,
        cut(sums[:, 0:2]),
        cut(sums[:, 2:4]),
        cut(sums[:, 4:6]),
    )


def on_device(
    tokens, lengths, key_mask, cotangent, w_qkv, w_out, w_pos, w_up, w_down, attn_bias, up_bias, norm_gain,
    norm_bias, out_bias,
):
    side = lax.axis_index("seq")
    parts = lax.axis_size("seq")
    n_rows = lax.axis_size("rows")
    me = lax.axis_index("rows")
    far = n_rows == SHARDS and parts == 2
    seqs = tokens.shape[0] // parts
    length = tokens.shape[1] * parts
    queries = length // 2
    mine = lambda x: lax.dynamic_slice_in_dim(x, side * seqs, seqs, 0)
    spots = jnp.arange(length, dtype=jnp.int32)[None, :]
    key_valid = jnp.where(spots < mine(lengths)[:, None], mine(key_mask), 0)
    shifted_valid = jnp.concatenate([key_valid[:, :1], key_valid[:, :-1]], axis=1)
    pooled_valid = jnp.max(shifted_valid.reshape(seqs, queries, 2), axis=2)
    flat = lambda x: x.reshape(-1, x.shape[-1])
    sets = lambda x: x.reshape(seqs, -1, D)

    if not far:
        tokens, cotangent = to_sequences(tokens, side, parts), to_sequences(cotangent, side, parts)
    start = prologue(far, 1, tokens, w_qkv, w_pos, attn_bias)
    tab0, tab1, enc0, enc1 = (start[n] for n in ("tab0", "tab1", "enc0", "enc1"))
    qw0, qr0, k0, v0 = sets(start["qw"]), sets(start["qr"]), start["k"], start["v"]
    mixed0, inv0, p0, *swapped = attn_fwd(2, key_valid[:, None, :], qw0, qr0, k0, v0, tab0, far, 6, cotangent)
    cot = swapped[0] if far else cotangent
    mixed0 = flat(mixed0)
    hid, x1, r1, act, slope, x2, r2, first, first_low, qw1, qr1, k1, v1 = ffn_fwd(
        mixed0, start["pooled"], w_out, w_up, w_down, w_qkv, attn_bias, up_bias, norm_gain, norm_bias, out_bias
    )
    qw1, qr1, k1, v1 = sets(qw1), sets(qr1), sets(k1), sets(v1)
    mixed1, inv1, p1 = attn_fwd(1, pooled_valid[:, None, :], qw1, qr1, k1, v1, tab1)
    mixed1 = flat(mixed1)
    lout, (dmixed1, dbranch1, dres1, small1, upg1), ffn1 = ffn_last(
        far, 2, mixed1, first, flat(cot), w_out, w_up, w_down, up_bias, norm_gain, norm_bias, out_bias
    )
    lout = sets(lout)
    plan = []
    if far:
        plan = [(x, order[1:3], False, {0: 0, 1: 9}) for x, order in zip(ffn1, FFN_ORDERS[1])]
    dfirst, dbias1, moved, att1 = back_layer(
        far, 3, 1, plan, p1, inv1, qw1, qr1, k1, v1, tab1, sets(dmixed1), dres1, w_qkv, first_low, first_low, enc1,
    )
    chains = []
    if far:
        for x, order in zip(moved, FFN_ORDERS[1]):
            steps = order[3:]
            chains.append((x, steps, True, {k: k for k in range(1, len(steps) + 1)}))
        chains += [(x, order[1:3], False, {2: 1}) for x, order in zip(att1, ATT_ORDERS * BLOCKS)]
    (dmixed0, dbranch0, dres0, small0, upg0), ffn0, moved, lout_got = ffn_bwd(
        far, 4, chains, lout, dfirst, x2, r2, hid, mixed0, x1, r1, norm_gain, w_out, w_up, w_down, act, slope
    )
    plan = []
    if far:
        late = {0: 0, 1: 8, 2: 11}
        when = ({0: 0, 1: 7, 2: 11}, {0: 0, 1: 7, 2: 11}, {0: 0, 1: 7, 2: 11}, {0: 0, 1: 7, 2: 11}, late)
        plan = [(x, order[1:], True, due) for x, order, due in zip(ffn0, FFN_ORDERS[0], when)]
        plan += [(x, order[3:], True, {0: 8}) for x, order in zip(moved[5:], ATT_ORDERS * BLOCKS)]
    args = (p0, inv0, qw0, qr0, k0, v0, tab0, sets(dmixed0), dres0, w_qkv, start["low"], flat(start["tok"]), enc0)
    if far:
        dtok, got, sums, ended, att0 = back_layer(far, 5, 0, plan, *args, smalls=(small0, upg0, small1, upg1, dbias1))
        done = att0 + ended + moved[:5]
        return finish(done, sums, dtok, got, lout, lout_got)
    dtok, dbias0, _, att0 = back_layer(far, 5, 0, plan, *args)
    small = lambda s, u, b: jnp.concatenate([s[:6], b[:2], u[0].reshape(PANELS, D)], axis=0)
    smalls = jnp.concatenate([small(small0, upg0, dbias0), small(small1, upg1, dbias1)], axis=0)
    return (
        to_positions(lout, side, parts, BF),
        to_positions(sets(dtok), side, parts, BF),
        *elsewhere(att0, ffn0, att1, ffn1, smalls, n_rows, me),
    )


def solution(mesh):
    seq3 = P("rows", "seq", None)
    in_specs = (seq3, P("rows"), P("rows", None), seq3) + (P(),) * 10
    mat = P(None, "rows", None)
    vec = P(None, None, "rows")
    out_specs = (seq3, seq3, P(None, None, "rows", None), mat, mat, mat, mat, vec, P(None, "rows"), vec, vec, vec)
    return jax.shard_map(on_device, mesh=mesh, in_specs=in_specs, out_specs=out_specs, check_vma=False)
```

```python
import functools

import jax
import jax.numpy as jnp
from jax import lax
from jax.experimental import pallas as pl
from jax.experimental.pallas import tpu as pltpu
from jax.sharding import PartitionSpec as P

D = 768
HEADS = 12
HEAD_DIM = 64
FF = 3072
PANELS = FF // D
HALF = D // 2
EPS = 1e-06
MASKED = -1000000000.0
SCALE = HEAD_DIM ** (-0.5)
BF = jnp.bfloat16
F32 = jnp.float32
MIB = 1 << 20

SHARDS = 16
MESH = pl.DeviceIdType.MESH
UP_ROWS = PANELS * D // SHARDS
ROW = D // SHARDS
WIDE = 2
SMALL_ROWS = 12


def mm(a, b):
    return lax.dot_general(a, b, (((1,), (0,)), ((), ())), preferred_element_type=F32)


def mm_nt(a, b):
    return lax.dot_general(a, b, (((1,), (1,)), ((), ())), preferred_element_type=F32)


def mm_tn(a, b):
    return lax.dot_general(a, b, (((0,), (0,)), ((), ())), preferred_element_type=F32)


def ln_fwd(z):
    center = z - jnp.mean(z, axis=-1, keepdims=True)
    var = jnp.mean(center * center, axis=-1, keepdims=True)
    rstd = lax.rsqrt(var + EPS)
    return center * rstd, rstd


def ln_bwd(dy, xhat, rstd, gain):
    dx = dy * gain
    m1 = jnp.mean(dx, axis=-1, keepdims=True)
    m2 = jnp.mean(dx * xhat, axis=-1, keepdims=True)
    return rstd * (dx - m1 - xhat * m2)


GELU_K = 0.7978845608028654
GELU_C = 0.044715


def gelu_and_slope(z):
    z2 = z * z
    t = jnp.tanh(GELU_K * z * (1.0 + GELU_C * z2))
    half = 0.5 * (1.0 + t)
    slope = half + 0.5 * z * (1.0 - t * t) * (GELU_K * (1.0 + 3.0 * GELU_C * z2))
    return z * half, slope


def split_hi_lo(x):
    hi = x.astype(BF)
    return hi, (x - hi.astype(F32)).astype(BF)


def cost(flops, nbytes, trans=0):
    return pl.CostEstimate(flops=int(flops), bytes_accessed=int(nbytes), transcendentals=int(trans))


def params(limit=56, **kw):
    return pltpu.CompilerParams(vmem_limit_bytes=limit * MIB, **kw)


def full_spec(shape, memory_space=pltpu.VMEM):
    return pl.BlockSpec(memory_space=memory_space)


ANY = pl.BlockSpec(memory_space=pl.ANY)
VM = pl.BlockSpec(memory_space=pltpu.VMEM)
SM = pl.BlockSpec(memory_space=pltpu.SMEM)


def sds(shape, dtype):
    return jax.ShapeDtypeStruct(shape, dtype)


CORE = ("rows", 1)
ALONG_X = ("rows", 2)
ALONG_Y = ("seq", 1)
Z_NEAR = ("rows", 4)
Z_FAR = ("rows", 8)
Z_DIAG = ("rows", 12)
Z_ALL = ("rows", 0)
XZY = (CORE, ALONG_X, Z_NEAR, ALONG_Y, Z_FAR)
ZYX = (CORE, Z_NEAR, ALONG_Y, ALONG_X, Z_FAR)
YZX = (CORE, ALONG_Y, Z_NEAR, ALONG_X, Z_FAR)
XY = (CORE, ALONG_X, ALONG_Y, Z_ALL)
YX = (CORE, ALONG_Y, ALONG_X, Z_ALL)
BLOCK = 128
BLOCKS = D // (2 * BLOCK)


def bit(v, b):
    return lax.rem(lax.div(v, b), 2)


def partner(step):
    if isinstance(step[0], tuple):
        return {axis: spot for one in step for axis, spot in partner(one).items()}
    axis, b = step
    me = lax.axis_index(axis)
    spot = me
    for k in (1, 2, 4, 8):
        if b & k:
            spot = spot + k - 2 * k * bit(me, k)
    return {axis: spot}


def singles(step):
    return (Z_FAR, Z_NEAR, Z_DIAG) if step == Z_ALL else (step,)


def bits_of(order):
    return [one for step in order for one in ((Z_NEAR, Z_FAR) if step == Z_ALL else (step,))]


def greet(steps):
    steps = list(dict.fromkeys(one for step in steps for one in singles(step)))
    sem = pltpu.get_barrier_semaphore()
    for step in steps:
        pl.semaphore_signal(sem, inc=1, device_id=partner(step), device_id_type=MESH)
    pl.semaphore_wait(sem, len(steps))


def remote(src, dst, sems, i, step):
    return pltpu.make_async_remote_copy(
        src_ref=src,
        dst_ref=dst,
        send_sem=sems.at[i, 0],
        recv_sem=sems.at[i, 1],
        device_id=partner(step),
        device_id_type=MESH,
    )


def add_to(dst, first, b, b_first, mats, rows):
    blk = rows
    while blk * dst.shape[2] > 96 * HALF:
        blk //= 2
    per = rows // blk

    def one(i, _):
        m = lax.div(i, per)
        at = pl.ds(pl.multiple_of(lax.rem(i, per) * blk, 16), blk)
        dst[first + m, at, :] = dst[first + m, at, :] + b[b_first + m, at, :]
        return 0

    lax.fori_loop(0, mats * per, one, 0)


class Kernel:
    def __init__(self):
        self.args, self.in_specs, self.out_specs, self.out_shape, self.scr = [], [], [], [], []

    def inp(self, x, spec=ANY):
        self.args.append(x)
        self.in_specs.append(spec)
        return ("i", len(self.args) - 1)

    def out(self, shape, dtype, spec=ANY):
        self.out_shape.append(sds(shape, dtype))
        self.out_specs.append(spec)
        return ("o", len(self.out_shape) - 1)

    def mem(self, shape, dtype=BF):
        self.scr.append(pltpu.VMEM(shape, dtype))
        return ("s", len(self.scr) - 1)

    def sems(self, *shape):
        self.scr.append(pltpu.SemaphoreType.DMA(shape))
        return ("s", len(self.scr) - 1)

    def run(self, body, name, cost_estimate, grid=(), cid=None, limit=56):
        n, m = len(self.args), len(self.out_shape)

        def kernel(*refs):
            groups = {"i": refs[:n], "o": refs[n : n + m], "s": refs[n + m :]}
            body(lambda handle: groups[handle[0]][handle[1]])

        kw = {} if cid is None else dict(collective_id=cid, has_side_effects=True)
        return pl.pallas_call(
            kernel,
            grid=grid,
            in_specs=self.in_specs,
            out_specs=self.out_specs,
            out_shape=self.out_shape,
            scratch_shapes=self.scr,
            compiler_params=params(limit, **kw),
            cost_estimate=cost_estimate,
            name=name,
        )(*self.args)


class Chain:
    def __init__(self, kn, whole, steps, close=False, born=None):
        self.steps, self.close, self.born, self.whole = steps, close, born is not None, whole
        j = len(steps)
        self.j = j
        if self.born:
            self.total, self.m, self.n, width = born
            self.arr = kn.mem((self.m, self.n, width))
        else:
            self.m, self.n, width = whole.shape
            self.src = kn.inp(whole)
            if j:
                self.total = kn.mem((self.m, self.n // (1 + len(singles(steps[0]))), width))
        m = self.m
        self.size = [self.n]
        for step in steps:
            self.size.append(self.size[-1] // (1 + len(singles(step))))
        self.land = [kn.mem((m * len(singles(s)), self.size[k + 1], width)) for k, s in enumerate(steps)]
        self.nf = self.size[-1]
        self.out = kn.out((m, self.nf, width), BF) if j else None
        self.other = kn.out((m, self.nf, width), BF) if close else None
        self.sem = kn.sems(2 * m + 3 * j + 3, 2)

    def bind(self, get):
        self.ref = get
        return self

    def core(self):
        g = self.ref
        return remote(g(self.total).at[:, pl.ds(self.n, self.n)], g(self.arr), g(self.sem), 0, CORE)

    def sends(self, k):
        g, m, j = self.ref, self.m, self.j
        sem = g(self.sem)
        if k == j:
            mine = g(self.total).at[:, pl.ds(0, self.nf)] if j else g(self.src)
            return [remote(mine, g(self.other), sem, 2 * m + 3 * j, ALONG_Y)]
        n = self.size[k + 1]
        source = g(self.total) if k or self.born else g(self.src)
        return [
            remote(
                source.at[:, pl.ds((i + 1) * n, n)], g(self.land[k]).at[pl.ds(i * m, m)], sem, 2 * m + 3 * k + i, one
            )
            for i, one in enumerate(singles(self.steps[k]))
        ]

    def fetch(self):
        g = self.ref
        return pltpu.make_async_copy(
            g(self.src).at[:, pl.ds(0, self.size[1])], g(self.total), g(self.sem).at[2 * self.m + 3 * self.j + 1, 0]
        )

    def keep(self):
        g = self.ref
        return pltpu.make_async_copy(
            g(self.total).at[:, pl.ds(0, self.nf)], g(self.out), g(self.sem).at[2 * self.m + 3 * self.j + 2, 0]
        )

    def first(self):
        g = self.ref
        self.core().wait()
        add_to(g(self.total), 0, g(self.arr), 0, self.m, self.n)
        for copy in self.sends(0):
            copy.start()

    def go(self, k):
        g = self.ref
        if k == 0 and self.j:
            self.fetch().start()
        if k > 0:
            if k == 1 and not self.born:
                self.fetch().wait()
            for copy in self.sends(k - 1):
                copy.wait()
            for b in range(len(singles(self.steps[k - 1]))):
                add_to(g(self.total), 0, g(self.land[k - 1]), b * self.m, self.m, self.size[k])
        if k < self.j or self.close:
            for copy in self.sends(k):
                copy.start()
        if k == self.j and self.j:
            self.keep().start()

    def end(self):
        if self.close:
            for copy in self.sends(self.j):
                copy.wait()
        if self.j:
            self.keep().wait()

    def result(self, res):
        mine = res[self.out[1]] if self.j else self.whole
        return (mine, res[self.other[1]]) if self.close else mine


class Group:
    def __init__(self, kn, far, order, mats, rows_each, width=HALF):
        self.far, self.order, self.mats, self.rows = far, order, mats, rows_each
        self.n = SHARDS * rows_each
        self.buf = kn.mem((mats, 2 * self.n, width))
        if far:
            self.arr = kn.mem((mats, self.n, width))
        self.out = kn.out((mats, self.n if far else 2 * self.n, width), BF)
        self.sem = kn.sems(mats * SHARDS, 2)
        self.done = kn.sems(mats)

    def bind(self, get):
        self.ref = get
        self.sent = {i: [] for i in range(self.mats)}

    def locate(self):
        self.base = places(self.order, self.rows, self.far)

    def put(self, mat, tile, shards, first=0, pitch=None):
        put(self.ref(self.buf), mat, self.base, tile, shards, self.rows, first, pitch or self.rows)

    def leave(self, mat, start=0, n=None):
        if not self.far:
            return
        n = n or self.n
        self.sent[mat].append((start, n))
        self.copy(mat, len(self.sent[mat]) - 1).start()

    def copy(self, mat, i):
        g = self.ref
        start, n = self.sent[mat][i]
        source = g(self.buf).at[mat, pl.ds(self.n + start, n)]
        return remote(source, g(self.arr).at[mat, pl.ds(start, n)], g(self.sem), mat * SHARDS + i, CORE)

    def settle(self, mat):
        g = self.ref
        if self.far:
            for i in range(len(self.sent[mat])):
                self.copy(mat, i).wait()
            add_to(g(self.buf), mat, g(self.arr), mat, 1, self.n)
        self.store(mat).start()

    def store(self, mat):
        g = self.ref
        n = self.n if self.far else 2 * self.n
        return pltpu.make_async_copy(g(self.buf).at[mat, pl.ds(0, n)], g(self.out).at[mat], g(self.done).at[mat])

    def end(self):
        for mat in range(self.mats):
            self.store(mat).wait()

    def result(self, res):
        return res[self.out[1]]


def pool_matrix(rows, cols):
    k = lax.broadcasted_iota(jnp.int32, (rows, cols), 0)
    t = lax.broadcasted_iota(jnp.int32, (rows, cols), 1)
    both = jnp.where((t == 2 * k) | (t == 2 * k - 1), 0.5, 0.0)
    return jnp.where((k == 0) & (t == 0), 1.0, both).astype(BF)


def pool_matrix_t(rows, cols):
    t = lax.broadcasted_iota(jnp.int32, (rows, cols), 0)
    k = lax.broadcasted_iota(jnp.int32, (rows, cols), 1)
    both = jnp.where((t == 2 * k) | (t == 2 * k - 1), 0.5, 0.0)
    return jnp.where((k == 0) & (t == 0), 1.0, both).astype(BF)


def head_masks():
    lane = lax.broadcasted_iota(jnp.int32, (1, 128), 1)
    first = jnp.where(lane < HEAD_DIM, 1.0, 0.0)
    return first.astype(BF), (1.0 - first).astype(BF)


def both_heads(x, masks):
    return jnp.concatenate([x * masks[0], x * masks[1]], axis=0)


QB = 128


def attn_fwd_step(stride, pairs, valid_ref, qw_ref, qr_ref, k_ref, v_ref, tab_ref, mixed_ref, inv_ref, p_ref):
    masks = head_masks()
    lane = lax.broadcasted_iota(jnp.int32, (1, 128), 1)
    keys = k_ref.shape[1]
    queries = qw_ref.shape[1]
    width = stride * QB + keys
    valid = valid_ref[0] > 0
    for pr in range(pairs):
        lanes = slice(pr * 128, (pr + 1) * 128)
        k = k_ref[0, :, lanes]
        v = jnp.concatenate([v_ref[0, :, lanes], jnp.ones((keys, 128), BF)], axis=1)
        outs = []
        for h in range(2):
            content = mm_nt(qw_ref[0, :, lanes] * (masks[h] * SCALE).astype(BF), k)
            relative = mm_nt(qr_ref[0, :, lanes] * (masks[h] * SCALE).astype(BF), tab_ref[:, lanes])
            parts = []
            for b in range(queries // QB):
                rows = slice(b * QB, (b + 1) * QB)
                t0 = stride * (queries - QB - b * QB)
                rolled = pltpu.roll(
                    relative[rows, t0 : t0 + width], width - stride * (QB - 1), 1, stride=stride, stride_axis=0
                )
                scores = jnp.where(valid, content[rows] + rolled[:, :keys], MASKED)
                terms = jnp.exp(scores - jnp.max(scores, axis=-1, keepdims=True)).astype(BF)
                p_ref[0, 2 * pr + h, rows, :] = terms
                parts.append(terms)
            outs.append(mm(jnp.concatenate(parts, axis=0), v))
        inv = 1.0 / jnp.where(lane < HEAD_DIM, outs[0][:, 128:], outs[1][:, 128:])
        inv_ref[0, :, lanes] = inv
        mixed_ref[0, :, lanes] = (jnp.where(lane < HEAD_DIM, outs[0][:, :128], outs[1][:, :128]) * inv).astype(BF)


def attn_fwd(stride, valid, qw, qr, k, v, tab, far=False, cid=None, extra=None):
    s, queries, _ = qw.shape
    keys = k.shape[1]
    table = tab.shape[0]
    pairs = 2
    steps = HEADS // 2 // pairs
    kn = Kernel()
    block = lambda n: pl.BlockSpec((1, n, 128 * pairs), lambda i, j: (i, 0, j))
    handles = [
        kn.inp(valid, pl.BlockSpec((1, 1, keys), lambda i, j: (i, 0, 0))),
        kn.inp(qw, block(queries)),
        kn.inp(qr, block(queries)),
        kn.inp(k, block(keys)),
        kn.inp(v, block(keys)),
        kn.inp(tab, pl.BlockSpec((table, 128 * pairs), lambda i, j: (0, j))),
        kn.out((s, queries, D), BF, block(queries)),
        kn.out((s, queries, D), F32, block(queries)),
        kn.out((s, HEADS, queries, keys), BF, pl.BlockSpec((1, 2 * pairs, queries, keys), lambda i, j: (i, j, 0, 0))),
    ]
    if extra is not None and far:
        part = extra.shape[1]
        h_ex, h_full, r_sem, l_sem = kn.inp(extra), kn.out((s, 2 * part, D), BF), kn.sems(1, 2), kn.sems(1)

    def body(get):
        if extra is not None and far:
            side = lax.axis_index("seq")
            here = get(h_full).at[:, pl.ds(side * part, part)]
            copies = lambda: (
                remote(get(h_ex).at[pl.ds((1 - side) * s, s)], here, get(r_sem), 0, ALONG_Y),
                pltpu.make_async_copy(get(h_ex).at[pl.ds(side * s, s)], here, get(l_sem).at[0]),
            )
            first = jnp.logical_and(pl.program_id(0) == 0, pl.program_id(1) == 0)
            end = jnp.logical_and(pl.program_id(0) == s - 1, pl.program_id(1) == steps - 1)

            @pl.when(first)
            def _():
                greet([ALONG_Y])
                for copy in copies():
                    copy.start()

        attn_fwd_step(stride, pairs, *[get(h) for h in handles])
        if extra is not None and far:

            @pl.when(end)
            def _():
                for copy in copies():
                    copy.wait()

    return kn.run(
        body,
        "attn_fwd_%d" % stride,
        cost(2 * s * HEADS * queries * keys * 64 * 4, 12 * MIB, s * HEADS * queries * keys),
        grid=(s, steps),
        cid=cid if extra is not None and far else None,
    )


def ffn_fwd(mixed, resid, w_out, w_up, w_down, w_qkv, attn_bias, up_bias, gain, nbias, obias):
    rows = mixed.shape[0]
    kn = Kernel()
    h_mixed, h_resid = kn.inp(mixed, VM), kn.inp(resid, VM)
    h_wout, h_up, h_down, h_qkv = (kn.inp(x) for x in (w_out, w_up, w_down, w_qkv))
    h_ab, h_upb, h_gain, h_nb, h_ob = (kn.inp(x, VM) for x in (attn_bias, up_bias, gain, nbias, obias))
    wout, wup, wdown, wqkv = kn.mem((D, D)), kn.mem((D, FF)), kn.mem((FF, D)), kn.mem((3, D, D))
    shapes = {"hid": (D, BF), "x1": (D, F32), "r1": (128, F32), "act": (FF, BF), "slope": (FF, BF), "x2": (D, F32)}
    shapes.update({"r2": (128, F32), "out": (D, F32), "low": (D, BF), "qw": (D, BF), "qr": (D, BF), "k": (D, BF), "v": (D, BF)})
    order = list(shapes)
    outs = {n: (kn.out((rows, c), t), kn.mem((rows, c), t)) for n, (c, t) in shapes.items()}
    l_sem, o_sem = kn.sems(4), kn.sems(len(order))
    h_total = kn.mem((rows, D), F32)

    def body(get):
        mem = lambda n: get(outs[n][1])
        store = lambda n: pltpu.make_async_copy(mem(n), get(outs[n][0]), get(o_sem).at[order.index(n)])
        pairs = ((get(h_wout).at[0], wout), (get(h_up).at[0], wup), (get(h_down).at[0], wdown), (get(h_qkv).at[1], wqkv))
        loads = [pltpu.make_async_copy(src, get(dst), get(l_sem).at[i]) for i, (src, dst) in enumerate(pairs)]
        for copy in loads:
            copy.start()
        gain_ref, nb_ref, ob_ref, ab_ref = get(h_gain), get(h_nb), get(h_ob), get(h_ab)
        loads[0].wait()
        x1, r1 = ln_fwd(get(h_resid)[...] + (mm(get(h_mixed)[...], get(wout)[...]) + ob_ref[0, 0:1, :]))
        mem("x1")[...] = x1
        mem("r1")[...] = jnp.broadcast_to(r1, (rows, 128))
        hidden = x1 * gain_ref[0, 0:1, :] + nb_ref[0, 0:1, :]
        mem("hid")[...] = hidden.astype(BF)
        for n in ("x1", "r1", "hid"):
            store(n).start()
        total = get(h_total)
        total[...] = hidden + ob_ref[0, 1:2, :]
        loads[1].wait()
        for c in range(0, PANELS, WIDE):
            cols = slice(c * D, (c + WIDE) * D)
            act, slope = gelu_and_slope(mm(mem("hid")[...], get(wup)[:, cols]) + get(h_upb)[0:1, cols])
            act = act.astype(BF)
            mem("act")[:, cols] = act
            mem("slope")[:, cols] = slope.astype(BF)
            if c == 0:
                loads[2].wait()
            total[...] += mm(act, get(wdown)[cols, :])
        store("act").start()
        store("slope").start()
        x2, r2 = ln_fwd(total[...])
        mem("x2")[...] = x2
        mem("r2")[...] = jnp.broadcast_to(r2, (rows, 128))
        out = x2 * gain_ref[0, 1:2, :] + nb_ref[0, 1:2, :]
        mem("out")[...] = out
        low = out.astype(BF)
        mem("low")[...] = low
        for n in ("x2", "r2", "out", "low"):
            store(n).start()
        loads[3].wait()
        q = mm(low, get(wqkv)[0])
        mem("qw")[...] = (q + ab_ref[1, 0:1, :]).astype(BF)
        mem("qr")[...] = (q + ab_ref[1, 1:2, :]).astype(BF)
        store("qw").start()
        store("qr").start()
        mem("k")[...] = mm(low, get(wqkv)[1]).astype(BF)
        store("k").start()
        mem("v")[...] = mm(low, get(wqkv)[2]).astype(BF)
        store("v").start()
        for n in order:
            store(n).wait()

    return kn.run(body, "ffn_fwd", cost(2 * rows * D * D * 12, 34 * MIB, rows * FF), limit=60)


def places(order, rows_each, far):
    me = lax.axis_index("rows") if far else 0
    side = lax.axis_index("seq") if far else 0
    base = {}
    for r in range(SHARDS):
        for half in range(2):
            spot = 0
            for axis, b in bits_of(order):
                c = half if axis == "seq" else (r // b) % 2
                mine = side if axis == "seq" else me
                spot = spot * 2 + (lax.rem(bit(mine, b) + c, 2) if far else c)
            base[r, half] = spot * rows_each
    return base


def put(buf_ref, mat, base, tile, shards, rows, first=0, pitch=None):
    low = tile.astype(BF)
    width = buf_ref.shape[2]
    for n, r in enumerate(shards):
        for half in range(2):
            start = base[r, half]
            if not isinstance(start, int):
                start = pl.multiple_of(start, 16)
            top = n * pitch + first
            buf_ref[mat, pl.ds(start, rows), :] = low[top : top + rows, half * width : (half + 1) * width]


NA = SHARDS * ROW
BORN_ORDERS = (XY, XY, XY)
BORN_POINTS = ({1: 11}, {})
SMALL_STEPS = (
    (CORE,),
    (ALONG_X, ALONG_Y, (ALONG_X, ALONG_Y)),
    (Z_NEAR, Z_FAR, Z_DIAG),
)
UP_AT = ((0, 0), (0, 1), (0, 2), (1, 0))
DOWN_AT = ((1, 1), (1, 2), (2, 0), (2, 1))
OUT_AT = (2, 2)
FFN_ORDERS = (XZY, YX, ZYX)
FFN_MATS = (3, 3, 3)
ATT_ORDERS = ((XY, YX), (XZY, YZX))


class FfnGrads:
    def __init__(self, kn, far, rows):
        full = lambda shape: pl.BlockSpec(shape, lambda *g: (0,) * len(shape))
        self.dmixed = kn.out((rows, D), BF, full((rows, D)))
        self.dbranch = kn.out((rows, D), BF, full((rows, D)))
        self.dres = kn.out((rows, D), F32, full((rows, D)))
        self.small = kn.out((8, D), F32, full((8, D)))
        self.upg = kn.out((8, FF), F32, full((8, FF)))
        self.groups = [Group(kn, far, order, mats, ROW) for order, mats in zip(FFN_ORDERS, FFN_MATS)]
        self.wup, self.wdown = kn.mem((D, FF)), kn.mem((FF, D))
        self.act, self.slope = kn.mem((rows, FF)), kn.mem((rows, FF))
        self.dffn, self.dhid = kn.mem((rows, D)), kn.mem((rows, D), F32)
        self.near = kn.sems(4)

    def run(self, get, dy, x2, r2, gain2, gain1, wout_ref, hid_ref, mixed_ref, x1, r1, at):
        small_ref, upg_ref, dffn_ref, dhid_ref = get(self.small), get(self.upg), get(self.dffn), get(self.dhid)
        act, slope, wup, wdown = get(self.act), get(self.slope), get(self.wup), get(self.wdown)
        for group in self.groups:
            group.bind(get)
            group.locate()
        small_ref[...] = jnp.zeros_like(small_ref)
        dpost = ln_bwd(dy, x2, r2, gain2)
        small_ref[1:2, :] = jnp.sum(dy * x2, axis=0, keepdims=True)
        small_ref[3:4, :] = jnp.sum(dy, axis=0, keepdims=True)
        dffn = dpost.astype(BF)
        small_ref[5:6, :] = jnp.sum(dffn.astype(F32), axis=0, keepdims=True)
        dffn_ref[...] = dffn
        dhid_ref[...] = dpost
        at(0)
        each = SHARDS // PANELS
        groups = self.groups
        for w in range(0, PANELS, WIDE):
            ddown = mm_tn(act[:, w * D : (w + WIDE) * D], dffn_ref[...])
            shards = range(w * each, (w + WIDE) * each)
            for i, (group, mat) in enumerate(DOWN_AT):
                groups[group].put(mat, ddown, shards, i * ROW, UP_ROWS)
        for group, mat in DOWN_AT:
            groups[group].leave(mat)
        for w in range(0, PANELS, WIDE):
            cols = slice(w * D, (w + WIDE) * D)
            dact = mm_nt(dffn_ref[...], wdown[cols, :])
            dpre = (dact * slope[:, cols].astype(F32)).astype(BF)
            upg_ref[:, cols] = jnp.broadcast_to(jnp.sum(dpre.astype(F32), axis=0, keepdims=True), (8, WIDE * D))
            dup = mm_tn(hid_ref[...], dpre)
            for i in range(WIDE):
                group, mat = UP_AT[w + i]
                groups[group].put(mat, dup[:, i * D : (i + 1) * D], range(SHARDS))
                groups[group].leave(mat)
            dhid_ref[...] += mm_nt(dpre, wup[:, cols])
            at(w // WIDE + 1)
        for group, mat in DOWN_AT + UP_AT[:WIDE]:
            groups[group].settle(mat)
        dhid = dhid_ref[...]
        xh = x1()
        small_ref[0:1, :] = jnp.sum(dhid * xh, axis=0, keepdims=True)
        small_ref[2:3, :] = jnp.sum(dhid, axis=0, keepdims=True)
        dres = ln_bwd(dhid, xh, r1(), gain1)
        get(self.dres)[...] = dres
        dbranch = dres.astype(BF)
        get(self.dbranch)[...] = dbranch
        small_ref[4:5, :] = jnp.sum(dbranch.astype(F32), axis=0, keepdims=True)
        group, mat = OUT_AT
        groups[group].put(mat, mm_tn(mixed_ref[...], dbranch), range(SHARDS))
        groups[group].leave(mat)
        get(self.dmixed)[...] = mm_nt(dbranch, wout_ref[0]).astype(BF)
        for group, mat in UP_AT[WIDE:] + (OUT_AT,):
            groups[group].settle(mat)
        for group in groups:
            group.end()

    def results(self, res):
        own = [res[h[1]] for h in (self.dmixed, self.dbranch, self.dres, self.small, self.upg)]
        return own, [group.result(res) for group in self.groups]


def ffn_last(far, cid, mixed, resid, cot, w_out, w_up, w_down, up_bias, gain, nbias, obias):
    rows = mixed.shape[0]
    kn = Kernel()
    whole = pl.BlockSpec((rows, D), lambda i: (0, 0))
    layer = pl.BlockSpec((1, 2, D), lambda i: (1, 0, 0))
    h_mixed, h_resid, h_cot = (kn.inp(x, whole) for x in (mixed, resid, cot))
    h_wout = kn.inp(w_out, pl.BlockSpec((1, D, D), lambda i: (1, 0, 0)))
    h_up, h_down = kn.inp(w_up), kn.inp(w_down)
    h_upb = kn.inp(up_bias, pl.BlockSpec((2, FF), lambda i: (0, 0)))
    h_gain, h_nbias, h_obias = (kn.inp(x, layer) for x in (gain, nbias, obias))
    h_lout = kn.out((rows, D), BF, whole)
    grads = FfnGrads(kn, far, rows)
    h_hid, h_x1 = kn.mem((rows, D)), kn.mem((rows, D), F32)

    def body(get):
        if far:
            greet([CORE])
        near = get(grads.near)
        wup, wdown, act, slope, hid, x1s = (
            get(h) for h in (grads.wup, grads.wdown, grads.act, grads.slope, h_hid, h_x1)
        )
        dhid_s = get(grads.dhid)
        gain_ref, nbias_ref, obias_ref, upb_ref, wout_ref = (
            get(h) for h in (h_gain, h_nbias, h_obias, h_upb, h_wout)
        )
        cp_up = pltpu.make_async_copy(get(h_up).at[1], wup, near.at[0])
        cp_down = pltpu.make_async_copy(get(h_down).at[1], wdown, near.at[1])
        cp_up.start()
        cp_down.start()
        pre_norm = get(h_resid)[...] + (mm(get(h_mixed)[...], wout_ref[0]) + obias_ref[0, 0:1, :])
        x1, r1 = ln_fwd(pre_norm)
        x1s[...] = x1
        hidden = x1 * gain_ref[0, 0:1, :] + nbias_ref[0, 0:1, :]
        hid[...] = hidden.astype(BF)
        dhid_s[...] = hidden + obias_ref[0, 1:2, :]
        cp_up.wait()
        cp_down.wait()
        for c in range(0, PANELS, WIDE):
            cols = slice(c * D, (c + WIDE) * D)
            a, s = gelu_and_slope(mm(hid[...], wup[:, cols]) + upb_ref[1:2, cols])
            a = a.astype(BF)
            act[:, cols] = a
            slope[:, cols] = s.astype(BF)
            dhid_s[...] += mm(a, wdown[cols, :])
        x2, r2 = ln_fwd(dhid_s[...])
        get(h_lout)[...] = (x2 * gain_ref[0, 1:2, :] + nbias_ref[0, 1:2, :]).astype(BF)
        grads.run(
            get, get(h_cot)[...].astype(F32), x2, r2, gain_ref[0, 1:2, :], gain_ref[0, 0:1, :], wout_ref, hid,
            get(h_mixed), lambda: x1s[...], lambda: r1, lambda point: None,
        )

    res = kn.run(
        body, "ffn_last", cost(2 * rows * D * D * 26, 30 * MIB, rows * FF), grid=(1,), cid=cid if far else None, limit=63
    )
    return res[h_lout[1]], *grads.results(res)


def ffn_bwd(far, cid, chains, lout, dy, x2, r2, hid, mixed, x1, r1, gain, w_out, w_up, w_down, act, slope):
    rows = hid.shape[0]
    seqs, queries, _ = lout.shape
    kn = Kernel()
    whole = pl.BlockSpec((rows, D), lambda i: (0, 0))
    thin = pl.BlockSpec((rows, 128), lambda i: (0, 0))
    h_dy, h_x2, h_hid, h_mixed, h_x1 = (kn.inp(x, whole) for x in (dy, x2, hid, mixed, x1))
    h_r2, h_r1 = (kn.inp(x, thin) for x in (r2, r1))
    h_gain = kn.inp(gain, pl.BlockSpec((1, 2, D), lambda i: (0, 0, 0)))
    h_wout = kn.inp(w_out, pl.BlockSpec((1, D, D), lambda i: (0, 0, 0)))
    h_up, h_down, h_act, h_slope = (kn.inp(x) for x in (w_up, w_down, act, slope))
    grads = FfnGrads(kn, far, rows)
    links = [Chain(kn, *c[:3]) for c in chains]
    if far:
        h_lout, h_got = kn.inp(lout), kn.out((seqs, queries // 2, D), BF)
        h_swap = kn.sems(1, 2)

    def body(get):
        near = get(grads.near)
        if far:
            greet([CORE, ALONG_X, ALONG_Y, Z_ALL])
            side = lax.axis_index("seq")
            swap_lout = remote(
                get(h_lout).at[:, pl.ds((1 - side) * (queries // 2), queries // 2)], get(h_got), get(h_swap), 0, ALONG_Y
            )
        for link in links:
            link.bind(get)
            link.go(0)
        if far:
            swap_lout.start()
        loads = [
            pltpu.make_async_copy(get(h_act), get(grads.act), near.at[0]),
            pltpu.make_async_copy(get(h_down).at[0], get(grads.wdown), near.at[1]),
            pltpu.make_async_copy(get(h_slope), get(grads.slope), near.at[2]),
            pltpu.make_async_copy(get(h_up).at[0], get(grads.wup), near.at[3]),
        ]
        for copy in loads:
            copy.start()

        def at(point):
            if point == 0:
                for copy in loads:
                    copy.wait()
            for link, (_, _, _, when) in zip(links, chains):
                if point in when:
                    link.go(when[point])

        gain_ref = get(h_gain)
        grads.run(
            get, get(h_dy)[...], get(h_x2)[...], get(h_r2)[:, 0:1], gain_ref[0, 1:2, :], gain_ref[0, 0:1, :],
            get(h_wout), get(h_hid), get(h_mixed), lambda: get(h_x1)[...], lambda: get(h_r1)[:, 0:1], at,
        )
        for link, (_, _, close, _) in zip(links, chains):
            if not close:
                link.go(link.j)
        for link in links:
            link.end()
        if far:
            swap_lout.wait()

    res = kn.run(
        body, "ffn_bwd", cost(2 * rows * D * D * 18, 40 * MIB), grid=(1,), cid=cid if far else None, limit=63
    )
    return *grads.results(res), [link.result(res) for link in links], res[h_got[1]] if far else None


def attn_bwd_step(
    stride, seq, lanes, p_ref, inv_ref, qw_ref, qr_ref, k_ref, v_ref, tab_ref, dm_ref, dq, dk_out, dv_out, dtab, dbias
):
    masks = head_masks()
    lane = lax.broadcasted_iota(jnp.int32, (1, 128), 1)
    first = lane < HEAD_DIM
    keys = k_ref.shape[1]
    queries = qw_ref.shape[1]
    blocks = queries // QB
    width = stride * QB + keys
    flip_i = lax.broadcasted_iota(jnp.int32, (queries, queries), 0)
    flip_j = lax.broadcasted_iota(jnp.int32, (queries, queries), 1)
    flip = jnp.where(flip_i + flip_j == queries - 1, 1.0, 0.0).astype(BF)

    @pl.when(seq == 0)
    def _():
        dtab[:, lanes] = jnp.zeros((dtab.shape[0], 128), F32)
        dbias[:, lanes] = jnp.zeros((dbias.shape[0], 128), F32)

    k = k_ref[0]
    v = v_ref[0]
    inv = inv_ref[0]
    scaled = (dm_ref[0].astype(F32) * inv).astype(BF)
    qr_rev = mm(flip, qr_ref[0]).astype(BF)
    dk = jnp.zeros((keys, 128), F32)
    dv = jnp.zeros((keys, 128), F32)
    dqws, dqrs = [], []
    for h in range(2):
        dmh = scaled * masks[h]
        terms = p_ref[0, h]
        dprob = mm_nt(dmh, v)
        wide = terms.astype(F32)
        inner = jnp.sum(dprob * wide, axis=-1, keepdims=True) * inv[:, h * HEAD_DIM : h * HEAD_DIM + 1]
        ds = (wide * (dprob - inner)).astype(BF)
        dv = dv + mm_tn(terms, dmh)
        dk = dk + mm_tn(ds, qw_ref[0] * masks[h])
        dqws.append(mm(ds, k))
        rev = mm(flip, ds)
        back = []
        for b in range(blocks):
            rows = slice(b * QB, (b + 1) * QB)
            t0 = stride * b * QB
            padded = jnp.concatenate([rev[rows], jnp.zeros((QB, width - keys), F32)], axis=1)
            rel = pltpu.roll(padded, 0, 1, stride=stride, stride_axis=0).astype(BF)
            dtab[t0 : t0 + width, lanes] += mm_tn(rel, qr_rev[rows] * masks[h]) * SCALE
            back.append(mm(rel, tab_ref[t0 : t0 + width, :]))
        dqrs.append(jnp.concatenate(back, axis=0))
    dqw = jnp.where(first, dqws[0], dqws[1]) * SCALE
    hi, lo = split_hi_lo(jnp.where(first, dqrs[0], dqrs[1]))
    dqr = (mm(flip, hi) + mm(flip, lo)) * SCALE
    dq[pl.ds(pl.multiple_of(seq * queries, QB), queries), lanes] = (dqw + dqr).astype(BF)
    at = pl.ds(pl.multiple_of(seq * keys, QB), keys)
    dk_out[at, lanes] = (dk * SCALE).astype(BF)
    dv_out[at, lanes] = dv.astype(BF)
    dbias[0:1, lanes] += jnp.sum(dqw, axis=0, keepdims=True)
    dbias[1:2, lanes] += jnp.sum(dqr, axis=0, keepdims=True)


def back_layer(
    far, cid, layer, plan, p, inv, qw, qr, k, v, tab, dmixed, dres, w_qkv, xq, xk, enc, smalls=None
):
    s, queries, _ = qw.shape
    keys = k.shape[1]
    table = tab.shape[0]
    last = s * (HEADS // 2)
    nq, nk = s * queries, s * keys
    tail = smalls is not None
    kn = Kernel()
    seq_of = lambda g: lax.rem(jnp.minimum(g, last - 1), s)
    pair_of = lambda g: lax.div(jnp.minimum(g, last - 1), s)
    pair_block = lambda n: pl.BlockSpec((1, n, 128), lambda g: (seq_of(g), 0, pair_of(g)))
    h_p = kn.inp(p, pl.BlockSpec((1, 2, queries, keys), lambda g: (seq_of(g), pair_of(g), 0, 0)))
    h_inv, h_qw, h_qr, h_dm = (kn.inp(x, pair_block(queries)) for x in (inv, qw, qr, dmixed))
    h_k, h_v = (kn.inp(x, pair_block(keys)) for x in (k, v))
    h_tab = kn.inp(tab, pl.BlockSpec((table, 128), lambda g: (0, pair_of(g))))
    dq_s, dk_s, dv_s = kn.mem((nq, D)), kn.mem((nk, D)), kn.mem((nk, D))
    dtab_s, dbias_s = kn.mem((table, D), F32), kn.mem((8, D), F32)
    late = [(dres, F32), (xq, BF), (enc, BF)]
    if layer == 0 or xk is not xq:
        late.append((xk, BF))
    late_in = [kn.inp(x) for x, _ in late]
    late_mem = [kn.mem(x.shape, t) for x, t in late]
    h_w, h_wm = kn.inp(w_qkv), kn.mem((3, D, D))
    l_sem = kn.sems(len(late) + 1)
    chains = [Chain(kn, so_far, steps, close) for so_far, steps, close, _ in plan]
    whole = lambda shape: pl.BlockSpec(shape, lambda g: (0,) * len(shape))
    half = keys // 2
    born, groups = [], []
    if tail and far:
        for order in BORN_ORDERS:
            born.append(Chain(kn, None, order[1:], True, (kn.mem((4, 2 * NA, BLOCK)), 4, NA, BLOCK)))
    else:
        groups = [Group(kn, far, order, 2 * BLOCKS, ROW, BLOCK) for order in ATT_ORDERS[layer]]
    if tail and far:
        h_small = [kn.inp(x, whole(x.shape)) for x in smalls]
        sum_shape = (2 * SMALL_ROWS, D)
        h_sum = kn.out(sum_shape, F32, whole(sum_shape))
        sm = [kn.mem(sum_shape, F32) for _ in range(len(SMALL_STEPS))]
        sm_in = [kn.mem(sum_shape, F32) for step in SMALL_STEPS for _ in step]
        sm_sem = kn.sems(len(sm_in), 2)
        h_dx = kn.out((s, half, D), F32, whole((s, half, D)))
        h_piece, h_got, h_swap = kn.mem((s, half, D)), kn.out((s, half, D), BF), kn.sems(s, 2)
    else:
        h_dx = kn.out((nk, D), F32, whole((nk, D)))
        h_bias = kn.out((8, D), F32, whole((8, D)))
    greeted = [step for _, steps, _, _ in plan for step in steps] + [CORE]
    if tail:
        greeted = [CORE, ALONG_X, ALONG_Y, (ALONG_X, ALONG_Y), Z_ALL]

    def body(get):
        g = pl.program_id(0)
        dq, dk, dv, dtab, dbias = (get(h) for h in (dq_s, dk_s, dv_s, dtab_s, dbias_s))
        loads = [pltpu.make_async_copy(get(a), get(b), get(l_sem).at[i]) for i, (a, b) in enumerate(zip(late_in, late_mem))]
        loads.append(pltpu.make_async_copy(get(h_w).at[layer], get(h_wm), get(l_sem).at[len(late)]))
        for chain in chains + born:
            chain.bind(get)

        @pl.when(g == 0)
        def _():
            if far:
                greet(greeted)
            for copy in loads:
                copy.start()

        @pl.when(g < last)
        def _():
            lanes = pl.ds(pl.multiple_of(pair_of(g) * 128, 128), 128)
            attn_bwd_step(
                2 - layer, seq_of(g), lanes, get(h_p), get(h_inv), get(h_qw), get(h_qr), get(h_k), get(h_v), get(h_tab), get(h_dm),
                dq, dk, dv, dtab, dbias,
            )

        for point in range(last):
            acts = [(c, k) for c, (_, _, _, when) in zip(chains, plan) for k, w in when.items() if w == point]
            if acts:

                @pl.when(g == point)
                def _():
                    for chain, k in acts:
                        chain.go(k)

        dres_ref, xq_ref, enc_ref = (get(h) for h in late_mem[:3])
        xk_ref = get(late_mem[3]) if layer == 0 or xk is not xq else xq_ref
        for group in groups:
            group.bind(get)
        per = last // BLOCKS

        def swap_piece(i):
            return remote(get(h_piece).at[i], get(h_got).at[i], get(h_swap), i, ALONG_Y)

        def make(t):
            cols = slice(2 * t * BLOCK, 2 * (t + 1) * BLOCK)
            return (
                (1, 0, lambda: mm_tn(xk_ref[...], dv[:, cols])),
                (0, 0, lambda: mm_tn(xq_ref[...], dq[:, cols])),
                (1, 1, lambda: mm_tn(enc_ref[...], dtab[:, cols].astype(BF))),
                (0, 1, lambda: mm_tn(xk_ref[...], dk[:, cols])),
            )

        def gradients(t):
            for group in groups:
                group.locate()
            base = places(BORN_ORDERS[t], ROW, far) if tail and far else None
            for which, mat, tile in make(t):
                if tail and far:
                    put(get(born[t].total), 2 * which + mat, base, tile(), range(SHARDS), ROW, 0, ROW)
                else:
                    groups[which].put(2 * t + mat, tile(), range(SHARDS))
                    groups[which].leave(2 * t + mat)
            if tail and far:
                born[t].core().start()

        def settled(t):
            if tail and far:
                born[t].first()
                return
            for which, mat, _ in make(t):
                groups[which].settle(2 * t + mat)

        for t in range(BLOCKS):

            @pl.when(g == (t + 1) * per - 1)
            def _():
                if t == 0:
                    for copy in loads:
                        copy.wait()
                gradients(t)

            if t < BLOCKS - 1:

                @pl.when(g == (t + 1) * per)
                def _():
                    settled(t)

                for chain in born[t : t + 1]:
                    for k, point in BORN_POINTS[t].items():

                        @pl.when(g == point)
                        def _():
                            chain.go(k)

        @pl.when(g == last)
        def _():
            w = get(h_wm)
            dx_ref = get(h_dx)

            def at(point):
                for chain, (_, _, _, when) in zip(chains, plan):
                    for step, due in when.items():
                        if due == point:
                            chain.go(step)

            if tail and far:
                small_start(get, dbias)
            settled(BLOCKS - 1)
            if tail and far:
                small_round(get, 0)
            at(last)
            if layer == 1:
                dx_ref[...] = dres_ref[...] + (mm_nt(dq[...], w[0]) + mm_nt(dk[...], w[1]) + mm_nt(dv[...], w[2]))
            else:
                spread = pool_matrix_t(keys, queries)
                side = lax.axis_index("seq") if far else 0
                for i in range(s):
                    q_at, k_at = slice(i * queries, (i + 1) * queries), slice(i * keys, (i + 1) * keys)
                    hi, lo = split_hi_lo(dres_ref[q_at, :] + mm_nt(dq[q_at, :], w[0]))
                    dtok = mm_nt(dk[k_at, :], w[1]) + mm_nt(dv[k_at, :], w[2]) + (mm(spread, hi) + mm(spread, lo))
                    if tail and far:
                        low_half, high_half = dtok[:half], dtok[half:]
                        is_low = side == 0
                        dx_ref[i] = jnp.where(is_low, low_half, high_half)
                        get(h_piece)[i] = jnp.where(is_low, high_half, low_half).astype(BF)
                        if i < s - 1:
                            swap_piece(i).start()
                    else:
                        dx_ref[k_at, :] = dtok
            at(last + 1)
            if tail and far:
                finish_tail(get, swap_piece)
                return
            get(h_bias)[...] = dbias[...]
            for chain in chains:
                chain.go(chain.j)
            for group in groups:
                group.end()
            for chain in chains:
                chain.end()

    def small_copies(get, k):
        top = sum(len(step) for step in SMALL_STEPS[:k])
        came = [get(h) for h in sm_in]
        return [
            (came[top + i], remote(get(sm[k]), came[top + i], get(sm_sem), top + i, one))
            for i, one in enumerate(SMALL_STEPS[k])
        ]

    def small_start(get, dbias):
        own = get(sm[0])
        small0, upg0, small1, upg1, bias1 = (get(h) for h in h_small)
        for top, small, upg, bias in ((0, small0, upg0, dbias), (SMALL_ROWS, small1, upg1, bias1)):
            own[top : top + 6, :] = small[0:6, :]
            own[top + 6 : top + 8, :] = bias[0:2, :]
            for p in range(PANELS):
                own[top + 8 + p : top + 9 + p, :] = upg[0:1, p * D : (p + 1) * D]
        for _, copy in small_copies(get, 0):
            copy.start()

    def small_round(get, k):
        pieces = small_copies(get, k)
        for _, copy in pieces:
            copy.wait()
        own = get(sm[k])
        dst = get(sm[k + 1]) if k + 1 < len(SMALL_STEPS) else get(h_sum)
        if len(pieces) == 1:
            dst[...] = own[...] + pieces[0][0][...]
        else:
            a, b, c = (ref[...] for ref, _ in pieces)
            dst[...] = (own[...] + a) + (b + c)
        if k + 1 < len(SMALL_STEPS):
            for _, copy in small_copies(get, k + 1):
                copy.start()

    def finish_tail(get, swap_piece):
        pending = {c: max(when) + 1 for c, (_, _, _, when) in zip(chains, plan)}
        for t, chain in enumerate(born):
            pending[chain] = max([0, *BORN_POINTS[t]]) + 1 if t < BLOCKS - 1 else 1
        order = [chains[1], born[0], born[1], chains[0], chains[2], born[2], *chains[3:]]
        for r in range(5):
            for chain in order:
                k = pending[chain]
                if k <= chain.j:
                    chain.go(k)
                    pending[chain] = k + 1
            if r == 0:
                swap_piece(s - 1).start()
            if r + 1 < len(SMALL_STEPS):
                small_round(get, r + 1)
        for chain in order:
            chain.end()
        for i in range(s):
            swap_piece(i).wait()

    flops = 2 * s * HEADS * queries * keys * 64 * 9 + 2 * D * D * (4 * nq + 4 * nk + table)
    res = kn.run(
        body, "back_layer_%d" % layer, cost(flops, 40 * MIB), grid=(last + 1,), cid=cid if far else None, limit=62
    )
    moved = [chain.result(res) for chain in chains]
    if tail and far:
        return res[h_dx[1]], res[h_got[1]], res[h_sum[1]], moved, [chain.result(res) for chain in born]
    return res[h_dx[1]], res[h_bias[1]], moved, [group.result(res) for group in groups]


def steps_of(distances):
    half_width = D // 2
    frequency = 10000.0 ** (-jnp.arange(half_width, dtype=F32) / half_width)
    angles = distances.astype(F32)[:, None] * frequency[None, :]
    return jnp.stack([jnp.sin(angles), jnp.cos(angles)])


FINE = 32


def prologue(far, cid, tokens, w_qkv, w_pos, attn_bias):
    parts = 2 if far else 1
    s, part_len = tokens.shape[0] // parts, tokens.shape[1]
    length = part_len * parts
    queries = length // 2
    table = 2 * length
    coarse = steps_of(2 * (queries - 1) - FINE * jnp.arange(table // FINE, dtype=jnp.int32))
    fine = steps_of(-jnp.arange(FINE, dtype=jnp.int32))
    fine2 = steps_of(-2 * jnp.arange(FINE // 2, dtype=jnp.int32))
    kn = Kernel()
    h_tok, h_w, h_wp = (kn.inp(x) for x in (tokens, w_qkv, w_pos))
    h_coarse, h_fine, h_fine2, h_bias = (kn.inp(x, VM) for x in (coarse, fine, fine2, attn_bias))
    names = {}

    def result(name, shape, dtype=BF):
        names[name] = (kn.out(shape, dtype), kn.mem(shape, dtype))

    result("tok", (s, length, D))
    result("enc0", (table, D))
    result("enc1", (table // 2, D))
    result("tab0", (table, D))
    result("tab1", (table // 2, D))
    result("pooled", (s * queries, D), F32)
    for name in ("low", "qw", "qr"):
        result(name, (s * queries, D))
    for name in ("k", "v"):
        result(name, (s, length, D))
    h_wm, h_wpm = kn.mem((3, D, D)), kn.mem((2, D, D))
    o_sem, l_sem, r_sem = kn.sems(len(names)), kn.sems(3), kn.sems(1, 2)
    order = list(names)

    def body(get):
        mem = lambda name: get(names[name][1])

        def store(name):
            return pltpu.make_async_copy(mem(name), get(names[name][0]), get(o_sem).at[order.index(name)])

        ls = get(l_sem)
        tok = mem("tok")
        if far:
            side = lax.axis_index("seq")
            mine, other = pl.ds(side * s, s), pl.ds((1 - side) * s, s)
            greet([ALONG_Y])
            here = pl.ds(side * part_len, part_len)
            sends = [remote(get(h_tok).at[other], tok.at[:, here], get(r_sem), 0, ALONG_Y)]
            loads = [pltpu.make_async_copy(get(h_tok).at[mine], tok.at[:, here], ls.at[0])]
        else:
            sends = []
            loads = [pltpu.make_async_copy(get(h_tok), tok, ls.at[0])]
        loads += [
            pltpu.make_async_copy(get(h_wp), get(h_wpm), ls.at[1]),
            pltpu.make_async_copy(get(h_w).at[0], get(h_wm), ls.at[2]),
        ]
        for copy in sends + loads:
            copy.start()
        w = get(h_wm)

        def encode(dst, table_rows, fine_ref):
            n = fine_ref.shape[1]
            fs, fc = fine_ref[0], fine_ref[1]
            for a in range(table_rows // n):
                cs, cc = get(h_coarse)[0, a : a + 1, :], get(h_coarse)[1, a : a + 1, :]
                dst[a * n : (a + 1) * n, :HALF] = (cs * fc + cc * fs).astype(BF)
                dst[a * n : (a + 1) * n, HALF:] = (cc * fc - cs * fs).astype(BF)

        encode(mem("enc0"), table, get(h_fine))
        store("enc0").start()
        encode(mem("enc1"), table // 2, get(h_fine2))
        store("enc1").start()
        loads[1].wait()
        wp = get(h_wpm)
        mem("tab0")[...] = mm(mem("enc0")[...], wp[0]).astype(BF)
        store("tab0").start()
        mem("tab1")[...] = mm(mem("enc1")[...], wp[1]).astype(BF)
        store("tab1").start()
        for i in (0, 2):
            loads[i].wait()

        def keys_of(part):
            for i in range(s):
                x = tok[i, part, :]
                mem("k")[i, part, :] = mm(x, w[1]).astype(BF)
                mem("v")[i, part, :] = mm(x, w[2]).astype(BF)

        if far:
            keys_of(pl.ds(pl.multiple_of(side * part_len, part_len), part_len))
            for copy in sends:
                copy.wait()
            store("tok").start()
            keys_of(pl.ds(pl.multiple_of((1 - side) * part_len, part_len), part_len))
        else:
            store("tok").start()
            keys_of(pl.ds(0, length))
        store("k").start()
        store("v").start()
        gather = pool_matrix(queries, length)
        for i in range(s):
            at = slice(i * queries, (i + 1) * queries)
            pooled = mm(gather, tok[i])
            mem("pooled")[at, :] = pooled
            low = pooled.astype(BF)
            mem("low")[at, :] = low
            q = mm(low, w[0])
            mem("qw")[at, :] = (q + get(h_bias)[0, 0:1, :]).astype(BF)
            mem("qr")[at, :] = (q + get(h_bias)[0, 1:2, :]).astype(BF)
        for name in ("pooled", "low", "qw", "qr"):
            store(name).start()
        for name in order:
            store(name).wait()

    res = kn.run(
        body, "prologue", cost(2 * D * D * (3 * s * length + 2 * table), 30 * MIB), cid=cid if far else None
    )
    found = {name: res[h[0][1]] for name, h in names.items()}
    return found


def finish(done, sums, dtok, got, lout, lout_got):
    s, half, _ = dtok.shape
    q = lout_got.shape[1]
    names = ["b00", "b01", "b02", "g00", "g10", "g20", "qk1", "vp1", "g01", "g11", "g21"]
    kn = Kernel()
    hs = {n: (kn.inp(m, VM), kn.inp(o, VM)) for n, (m, o) in zip(names, done)}
    h_sum, h_dtok, h_got, h_lgot = (kn.inp(x, VM) for x in (sums, dtok, got, lout_got))
    h_lout = kn.inp(lout)
    o_lout = kn.out((2 * s, q, D), BF, VM)
    o_tok = kn.out((2 * s, half, D), F32, VM)
    o_qkv = kn.out((2, 3, ROW, D), F32, VM)
    o_out, o_pos = (kn.out((2, ROW, D), F32, VM) for _ in range(2))
    o_up = kn.out((2, ROW, FF), F32, VM)
    o_down = kn.out((2, UP_ROWS, D), F32, VM)
    o_attn = kn.out((2, 2, ROW), F32, VM)
    o_upb = kn.out((2, FF // SHARDS), F32, VM)
    o_gain, o_nb, o_ob = (kn.out((2, 2, ROW), F32, VM) for _ in range(3))
    h_lmem, h_sem = kn.mem((s, q, D)), kn.sems(1)

    def body(get):
        side, me = lax.axis_index("seq"), lax.axis_index("rows")
        copy = pltpu.make_async_copy(
            get(h_lout).at[:, pl.ds(pl.multiple_of(side * q, q), q)], get(h_lmem), get(h_sem).at[0]
        )
        copy.start()
        mine, other = pl.ds(side * s, s), pl.ds((1 - side) * s, s)
        get(o_tok)[mine] = get(h_dtok)[...]
        get(o_tok)[other] = get(h_got)[...].astype(F32)
        get(o_lout)[other] = get(h_lgot)[...]

        def halves(name, mat, dst, lead, base=0, rows=slice(None)):
            for h, which in zip(hs[name], (side, 1 - side)):
                width = get(h).shape[2]
                lanes = pl.ds(pl.multiple_of(base + which * width, 128), width)
                dst[(*lead, rows, lanes)] = get(h)[mat].astype(F32)

        for l in range(2):
            ffn = lambda at: ("g%d%d" % (at[0], l), at[1])
            for t in range(BLOCKS):
                for i, dst, lead in ((0, o_qkv, (l, 0)), (1, o_qkv, (l, 1)), (2, o_qkv, (l, 2)), (3, o_pos, (l,))):
                    name, mat = ("b0%d" % t, i) if l == 0 else (("qk1", "vp1")[i // 2], 2 * t + i % 2)
                    halves(name, mat, get(dst), lead, 2 * t * BLOCK)
            halves(*ffn(OUT_AT), get(o_out), (l,))
            for p in range(PANELS):
                halves(*ffn(UP_AT[p]), get(o_up), (l,), p * D)
                halves(*ffn(DOWN_AT[p]), get(o_down), (l,), rows=slice(p * ROW, (p + 1) * ROW))
        both = get(h_sum)[...]
        turned = pltpu.roll(both, lax.rem(D - me * ROW, D), 1)
        for l in range(2):
            r = 12 * l
            for o, row in ((o_gain, 0), (o_nb, 2), (o_ob, 4), (o_attn, 6)):
                get(o)[l] = turned[r + row : r + row + 2, :ROW]
        wide = FF // SHARDS
        per = D // wide
        shifted = pltpu.roll(both, lax.rem(D - lax.rem(me, per) * wide, D), 1)
        for l in range(2):
            picked = jnp.zeros((1, D), F32)
            for p in range(PANELS):
                picked = picked + jnp.where(lax.div(me, per) == p, shifted[12 * l + 8 + p : 12 * l + 9 + p, :], 0.0)
            get(o_upb)[l : l + 1, :] = picked[:, :wide]
        copy.wait()
        get(o_lout)[mine] = get(h_lmem)[...]

    return tuple(kn.run(body, "finish", cost(1e6, 16 * MIB)))


def swap(x, axis, b):
    n = lax.axis_size(axis)
    return lax.ppermute(x, axis, [(i, i ^ b) for i in range(n)])


def natural(both, order, rows_each):
    mats = both.shape[0]
    both = both.reshape(mats, 2, 2, 2, 2, 2, rows_each, both.shape[-1])
    at = {step: 1 + i for i, step in enumerate(bits_of(order))}
    return both.transpose(0, at[Z_FAR], at[Z_NEAR], at[ALONG_X], at[CORE], 6, at[ALONG_Y], 7)


def to_sequences(x, side, parts):
    own = x.shape[0] // parts
    mine = lax.dynamic_slice_in_dim(x, side * own, own, 0)
    other = swap(lax.dynamic_slice_in_dim(x, (1 - side) * own, own, 0), "seq", 1)
    return jnp.where(
        side == 0, jnp.concatenate([mine, other], axis=1), jnp.concatenate([other, mine], axis=1)
    )


def to_positions(x, side, parts, wire):
    own = x.shape[1] // parts
    mine = lax.dynamic_slice_in_dim(x, side * own, own, 1)
    other = swap(lax.dynamic_slice_in_dim(x, (1 - side) * own, own, 1).astype(wire), "seq", 1).astype(x.dtype)
    return jnp.where(
        side == 0, jnp.concatenate([mine, other], axis=0), jnp.concatenate([other, mine], axis=0)
    )


def elsewhere(att0, ffn0, att1, ffn1, smalls, n_rows, me):
    flat = lambda x: x.reshape(x.shape[0], -1, x.shape[-1] * x.shape[-2])
    rows = lambda x, order: flat(natural(x, order, ROW))
    total = lambda x: lax.psum(lax.psum_scatter(x, "rows", scatter_dimension=1, tiled=True).astype(F32), "seq")

    def quarter(f, at):
        return natural(f[at[0]], FFN_ORDERS[at[0]], ROW)[at[1] : at[1] + 1]

    def att(x, orders):
        qk, vp = (rows(b, o) for b, o in zip(x, orders))
        both = [jnp.concatenate([qk[2 * t : 2 * t + 2], vp[2 * t : 2 * t + 2]]) for t in range(BLOCKS)]
        return total(jnp.concatenate(both, axis=2))

    att0, att1 = att(att0, ATT_ORDERS[0]), att(att1, ATT_ORDERS[1])
    outs = [total(flat(quarter(f, OUT_AT))) for f in (ffn0, ffn1)]
    ups = [total(flat(jnp.concatenate([quarter(f, at) for at in UP_AT]))) for f in (ffn0, ffn1)]
    downs = [total(flat(jnp.concatenate([quarter(f, at) for at in DOWN_AT], axis=5))) for f in (ffn0, ffn1)]
    sums = lax.psum(smalls, ("rows", "seq")).reshape(2, -1, D)
    own = D // n_rows
    cut = lambda x: lax.dynamic_slice_in_dim(x, me * own, own, 2)
    upb = lax.dynamic_slice_in_dim(sums[:, 8:].reshape(2, FF), me * (FF // n_rows), FF // n_rows, 1)
    panels = lambda x: jnp.concatenate(list(x), axis=1)
    return (
        jnp.stack([att0[:3], att1[:3]]),
        jnp.concatenate(outs),
        jnp.stack([att0[3], att1[3]]),
        jnp.stack([panels(x) for x in ups]),
        jnp.concatenate(downs),
        cut(sums[:, 6:8]),
        upb,
        cut(sums[:, 0:2]),
        cut(sums[:, 2:4]),
        cut(sums[:, 4:6]),
    )


def on_device(
    tokens, lengths, key_mask, cotangent, w_qkv, w_out, w_pos, w_up, w_down, attn_bias, up_bias, norm_gain,
    norm_bias, out_bias,
):
    side = lax.axis_index("seq")
    parts = lax.axis_size("seq")
    n_rows = lax.axis_size("rows")
    me = lax.axis_index("rows")
    far = n_rows == SHARDS and parts == 2
    seqs = tokens.shape[0] // parts
    length = tokens.shape[1] * parts
    queries = length // 2
    mine = lambda x: lax.dynamic_slice_in_dim(x, side * seqs, seqs, 0)
    spots = jnp.arange(length, dtype=jnp.int32)[None, :]
    key_valid = jnp.where(spots < mine(lengths)[:, None], mine(key_mask), 0)
    shifted_valid = jnp.concatenate([key_valid[:, :1], key_valid[:, :-1]], axis=1)
    pooled_valid = jnp.max(shifted_valid.reshape(seqs, queries, 2), axis=2)
    flat = lambda x: x.reshape(-1, x.shape[-1])
    sets = lambda x: x.reshape(seqs, -1, D)

    if not far:
        tokens, cotangent = to_sequences(tokens, side, parts), to_sequences(cotangent, side, parts)
    start = prologue(far, 1, tokens, w_qkv, w_pos, attn_bias)
    tab0, tab1, enc0, enc1 = (start[n] for n in ("tab0", "tab1", "enc0", "enc1"))
    qw0, qr0, k0, v0 = sets(start["qw"]), sets(start["qr"]), start["k"], start["v"]
    mixed0, inv0, p0, *swapped = attn_fwd(2, key_valid[:, None, :], qw0, qr0, k0, v0, tab0, far, 6, cotangent)
    cot = swapped[0] if far else cotangent
    mixed0 = flat(mixed0)
    hid, x1, r1, act, slope, x2, r2, first, first_low, qw1, qr1, k1, v1 = ffn_fwd(
        mixed0, start["pooled"], w_out, w_up, w_down, w_qkv, attn_bias, up_bias, norm_gain, norm_bias, out_bias
    )
    qw1, qr1, k1, v1 = sets(qw1), sets(qr1), sets(k1), sets(v1)
    mixed1, inv1, p1 = attn_fwd(1, pooled_valid[:, None, :], qw1, qr1, k1, v1, tab1)
    mixed1 = flat(mixed1)
    lout, (dmixed1, dbranch1, dres1, small1, upg1), ffn1 = ffn_last(
        far, 2, mixed1, first, flat(cot), w_out, w_up, w_down, up_bias, norm_gain, norm_bias, out_bias
    )
    lout = sets(lout)
    plan = []
    if far:
        plan = [(x, order[1:3], False, {0: 0, 1: 8}) for x, order in zip(ffn1, FFN_ORDERS)]
    dfirst, dbias1, moved, att1 = back_layer(
        far, 3, 1, plan, p1, inv1, qw1, qr1, k1, v1, tab1, sets(dmixed1), dres1, w_qkv, first_low, first_low, enc1,
    )
    chains = []
    if far:
        for x, order in zip(moved, FFN_ORDERS):
            steps = order[3:]
            chains.append((x, steps, True, {k: k for k in range(1, len(steps) + 1)}))
        chains += [(x, order[1:3], False, {2: 1}) for x, order in zip(att1, ATT_ORDERS[1])]
    (dmixed0, dbranch0, dres0, small0, upg0), ffn0, moved, lout_got = ffn_bwd(
        far, 4, chains, lout, dfirst, x2, r2, hid, mixed0, x1, r1, norm_gain, w_out, w_up, w_down, act, slope
    )
    plan = []
    if far:
        when = ({0: 0, 1: 7, 2: 11}, {0: 0, 1: 7}, {0: 0, 1: 7, 2: 11})
        plan = [(x, order[1:], True, due) for x, order, due in zip(ffn0, FFN_ORDERS, when)]
        plan += [(x, order[3:], True, {0: 1, 1: 9}) for x, order in zip(moved[3:], ATT_ORDERS[1])]
    args = (p0, inv0, qw0, qr0, k0, v0, tab0, sets(dmixed0), dres0, w_qkv, start["low"], flat(start["tok"]), enc0)
    if far:
        dtok, got, sums, ended, att0 = back_layer(far, 5, 0, plan, *args, smalls=(small0, upg0, small1, upg1, dbias1))
        done = att0 + ended + moved[:3]
        return finish(done, sums, dtok, got, lout, lout_got)
    dtok, dbias0, _, att0 = back_layer(far, 5, 0, plan, *args)
    small = lambda s, u, b: jnp.concatenate([s[:6], b[:2], u[0].reshape(PANELS, D)], axis=0)
    smalls = jnp.concatenate([small(small0, upg0, dbias0), small(small1, upg1, dbias1)], axis=0)
    return (
        to_positions(lout, side, parts, BF),
        to_positions(sets(dtok), side, parts, BF),
        *elsewhere(att0, ffn0, att1, ffn1, smalls, n_rows, me),
    )


def solution(mesh):
    seq3 = P("rows", "seq", None)
    in_specs = (seq3, P("rows"), P("rows", None), seq3) + (P(),) * 10
    mat = P(None, "rows", None)
    vec = P(None, None, "rows")
    out_specs = (seq3, seq3, P(None, None, "rows", None), mat, mat, mat, mat, vec, P(None, "rows"), vec, vec, vec)
    return jax.shard_map(on_device, mesh=mesh, in_specs=in_specs, out_specs=out_specs, check_vma=False)
```

```python
import functools

import jax
import jax.numpy as jnp
from jax import lax
from jax.experimental import pallas as pl
from jax.experimental.pallas import tpu as pltpu
from jax.sharding import PartitionSpec as P

D = 768
HEADS = 12
HEAD_DIM = 64
FF = 3072
PANELS = FF // D
HALF = D // 2
EPS = 1e-06
MASKED = -1000000000.0
SCALE = HEAD_DIM ** (-0.5)
BF = jnp.bfloat16
F32 = jnp.float32
MIB = 1 << 20

SHARDS = 16
MESH = pl.DeviceIdType.MESH
UP_ROWS = PANELS * D // SHARDS
ROW = D // SHARDS
WIDE = 2
SMALL_ROWS = 12


def mm(a, b):
    return lax.dot_general(a, b, (((1,), (0,)), ((), ())), preferred_element_type=F32)


def mm_nt(a, b):
    return lax.dot_general(a, b, (((1,), (1,)), ((), ())), preferred_element_type=F32)


def mm_tn(a, b):
    return lax.dot_general(a, b, (((0,), (0,)), ((), ())), preferred_element_type=F32)


def ln_fwd(z):
    center = z - jnp.mean(z, axis=-1, keepdims=True)
    var = jnp.mean(center * center, axis=-1, keepdims=True)
    rstd = lax.rsqrt(var + EPS)
    return center * rstd, rstd


def ln_bwd(dy, xhat, rstd, gain):
    dx = dy * gain
    m1 = jnp.mean(dx, axis=-1, keepdims=True)
    m2 = jnp.mean(dx * xhat, axis=-1, keepdims=True)
    return rstd * (dx - m1 - xhat * m2)


GELU_K = 0.7978845608028654
GELU_C = 0.044715


def gelu_and_slope(z):
    z2 = z * z
    t = jnp.tanh(GELU_K * z * (1.0 + GELU_C * z2))
    half = 0.5 * (1.0 + t)
    slope = half + 0.5 * z * (1.0 - t * t) * (GELU_K * (1.0 + 3.0 * GELU_C * z2))
    return z * half, slope


def split_hi_lo(x):
    hi = x.astype(BF)
    return hi, (x - hi.astype(F32)).astype(BF)


def cost(flops, nbytes, trans=0):
    return pl.CostEstimate(flops=int(flops), bytes_accessed=int(nbytes), transcendentals=int(trans))


def params(limit=56, **kw):
    return pltpu.CompilerParams(vmem_limit_bytes=limit * MIB, **kw)


def full_spec(shape, memory_space=pltpu.VMEM):
    return pl.BlockSpec(memory_space=memory_space)


ANY = pl.BlockSpec(memory_space=pl.ANY)
VM = pl.BlockSpec(memory_space=pltpu.VMEM)
SM = pl.BlockSpec(memory_space=pltpu.SMEM)


def sds(shape, dtype):
    return jax.ShapeDtypeStruct(shape, dtype)


CORE = ("rows", 1)
ALONG_X = ("rows", 2)
ALONG_Y = ("seq", 1)
Z_NEAR = ("rows", 4)
Z_FAR = ("rows", 8)
Z_DIAG = ("rows", 12)
Z_ALL = ("rows", 0)
XZY = (CORE, ALONG_X, Z_NEAR, ALONG_Y, Z_FAR)
ZYX = (CORE, Z_NEAR, ALONG_Y, ALONG_X, Z_FAR)
XY = (CORE, ALONG_X, ALONG_Y, Z_ALL)
YX = (CORE, ALONG_Y, ALONG_X, Z_ALL)
BLOCK = 128
BLOCKS = D // (2 * BLOCK)


def bit(v, b):
    return lax.rem(lax.div(v, b), 2)


def partner(step):
    if isinstance(step[0], tuple):
        return {axis: spot for one in step for axis, spot in partner(one).items()}
    axis, b = step
    me = lax.axis_index(axis)
    spot = me
    for k in (1, 2, 4, 8):
        if b & k:
            spot = spot + k - 2 * k * bit(me, k)
    return {axis: spot}


def singles(step):
    return (Z_FAR, Z_NEAR, Z_DIAG) if step == Z_ALL else (step,)


def bits_of(order):
    return [one for step in order for one in ((Z_NEAR, Z_FAR) if step == Z_ALL else (step,))]


def greet(steps):
    steps = list(dict.fromkeys(one for step in steps for one in singles(step)))
    sem = pltpu.get_barrier_semaphore()
    for step in steps:
        pl.semaphore_signal(sem, inc=1, device_id=partner(step), device_id_type=MESH)
    pl.semaphore_wait(sem, len(steps))


def remote(src, dst, sems, i, step):
    return pltpu.make_async_remote_copy(
        src_ref=src,
        dst_ref=dst,
        send_sem=sems.at[i, 0],
        recv_sem=sems.at[i, 1],
        device_id=partner(step),
        device_id_type=MESH,
    )


def add_to(dst, first, b, b_first, mats, rows):
    blk = rows
    while blk * dst.shape[2] > 96 * HALF:
        blk //= 2
    per = rows // blk

    def one(i, _):
        m = lax.div(i, per)
        at = pl.ds(pl.multiple_of(lax.rem(i, per) * blk, 16), blk)
        dst[first + m, at, :] = dst[first + m, at, :] + b[b_first + m, at, :]
        return 0

    lax.fori_loop(0, mats * per, one, 0)


class Kernel:
    def __init__(self):
        self.args, self.in_specs, self.out_specs, self.out_shape, self.scr = [], [], [], [], []

    def inp(self, x, spec=ANY):
        self.args.append(x)
        self.in_specs.append(spec)
        return ("i", len(self.args) - 1)

    def out(self, shape, dtype, spec=ANY):
        self.out_shape.append(sds(shape, dtype))
        self.out_specs.append(spec)
        return ("o", len(self.out_shape) - 1)

    def mem(self, shape, dtype=BF):
        self.scr.append(pltpu.VMEM(shape, dtype))
        return ("s", len(self.scr) - 1)

    def sems(self, *shape):
        self.scr.append(pltpu.SemaphoreType.DMA(shape))
        return ("s", len(self.scr) - 1)

    def run(self, body, name, cost_estimate, grid=(), cid=None, limit=56):
        n, m = len(self.args), len(self.out_shape)

        def kernel(*refs):
            groups = {"i": refs[:n], "o": refs[n : n + m], "s": refs[n + m :]}
            body(lambda handle: groups[handle[0]][handle[1]])

        kw = {} if cid is None else dict(collective_id=cid, has_side_effects=True)
        return pl.pallas_call(
            kernel,
            grid=grid,
            in_specs=self.in_specs,
            out_specs=self.out_specs,
            out_shape=self.out_shape,
            scratch_shapes=self.scr,
            compiler_params=params(limit, **kw),
            cost_estimate=cost_estimate,
            name=name,
        )(*self.args)


class Chain:
    def __init__(self, kn, whole, steps, close=False, born=None):
        self.steps, self.close, self.born, self.whole = steps, close, born is not None, whole
        j = len(steps)
        self.j = j
        if self.born:
            self.total, self.m, self.n, width = born
            self.arr = kn.mem((self.m, self.n, width))
        else:
            self.m, self.n, width = whole.shape
            self.src = kn.inp(whole)
            if j:
                self.total = kn.mem((self.m, self.n // (1 + len(singles(steps[0]))), width))
        m = self.m
        self.size = [self.n]
        for step in steps:
            self.size.append(self.size[-1] // (1 + len(singles(step))))
        self.land = [kn.mem((m * len(singles(s)), self.size[k + 1], width)) for k, s in enumerate(steps)]
        self.nf = self.size[-1]
        self.out = kn.out((m, self.nf, width), BF) if j else None
        self.other = kn.out((m, self.nf, width), BF) if close else None
        self.sem = kn.sems(2 * m + 3 * j + 3, 2)

    def bind(self, get):
        self.ref = get
        return self

    def core(self):
        g = self.ref
        return remote(g(self.total).at[:, pl.ds(self.n, self.n)], g(self.arr), g(self.sem), 0, CORE)

    def sends(self, k):
        g, m, j = self.ref, self.m, self.j
        sem = g(self.sem)
        if k == j:
            mine = g(self.total).at[:, pl.ds(0, self.nf)] if j else g(self.src)
            return [remote(mine, g(self.other), sem, 2 * m + 3 * j, ALONG_Y)]
        n = self.size[k + 1]
        source = g(self.total) if k or self.born else g(self.src)
        return [
            remote(
                source.at[:, pl.ds((i + 1) * n, n)], g(self.land[k]).at[pl.ds(i * m, m)], sem, 2 * m + 3 * k + i, one
            )
            for i, one in enumerate(singles(self.steps[k]))
        ]

    def fetch(self):
        g = self.ref
        return pltpu.make_async_copy(
            g(self.src).at[:, pl.ds(0, self.size[1])], g(self.total), g(self.sem).at[2 * self.m + 3 * self.j + 1, 0]
        )

    def keep(self):
        g = self.ref
        return pltpu.make_async_copy(
            g(self.total).at[:, pl.ds(0, self.nf)], g(self.out), g(self.sem).at[2 * self.m + 3 * self.j + 2, 0]
        )

    def first(self):
        g = self.ref
        self.core().wait()
        add_to(g(self.total), 0, g(self.arr), 0, self.m, self.n)
        for copy in self.sends(0):
            copy.start()

    def go(self, k):
        g = self.ref
        if k == 0 and self.j:
            self.fetch().start()
        if k > 0:
            if k == 1 and not self.born:
                self.fetch().wait()
            for copy in self.sends(k - 1):
                copy.wait()
            for b in range(len(singles(self.steps[k - 1]))):
                add_to(g(self.total), 0, g(self.land[k - 1]), b * self.m, self.m, self.size[k])
        if k < self.j or self.close:
            for copy in self.sends(k):
                copy.start()
        if k == self.j and self.j:
            self.keep().start()

    def end(self):
        if self.close:
            for copy in self.sends(self.j):
                copy.wait()
        if self.j:
            self.keep().wait()

    def result(self, res):
        mine = res[self.out[1]] if self.j else self.whole
        return (mine, res[self.other[1]]) if self.close else mine


class Group:
    def __init__(self, kn, far, order, mats, rows_each, width=HALF):
        self.far, self.order, self.mats, self.rows = far, order, mats, rows_each
        self.n = SHARDS * rows_each
        self.buf = kn.mem((mats, 2 * self.n, width))
        if far:
            self.arr = kn.mem((mats, self.n, width))
        self.out = kn.out((mats, self.n if far else 2 * self.n, width), BF)
        self.sem = kn.sems(mats * SHARDS, 2)
        self.done = kn.sems(mats)

    def bind(self, get):
        self.ref = get
        self.sent = {i: [] for i in range(self.mats)}

    def locate(self):
        self.base = places(self.order, self.rows, self.far)

    def put(self, mat, tile, shards, first=0, pitch=None):
        put(self.ref(self.buf), mat, self.base, tile, shards, self.rows, first, pitch or self.rows)

    def leave(self, mat, start=0, n=None):
        if not self.far:
            return
        n = n or self.n
        self.sent[mat].append((start, n))
        self.copy(mat, len(self.sent[mat]) - 1).start()

    def copy(self, mat, i):
        g = self.ref
        start, n = self.sent[mat][i]
        source = g(self.buf).at[mat, pl.ds(self.n + start, n)]
        return remote(source, g(self.arr).at[mat, pl.ds(start, n)], g(self.sem), mat * SHARDS + i, CORE)

    def settle(self, mat):
        g = self.ref
        if self.far:
            for i in range(len(self.sent[mat])):
                self.copy(mat, i).wait()
            add_to(g(self.buf), mat, g(self.arr), mat, 1, self.n)
        self.store(mat).start()

    def store(self, mat):
        g = self.ref
        n = self.n if self.far else 2 * self.n
        return pltpu.make_async_copy(g(self.buf).at[mat, pl.ds(0, n)], g(self.out).at[mat], g(self.done).at[mat])

    def end(self):
        for mat in range(self.mats):
            self.store(mat).wait()

    def result(self, res):
        return res[self.out[1]]


def pool_matrix(rows, cols):
    k = lax.broadcasted_iota(jnp.int32, (rows, cols), 0)
    t = lax.broadcasted_iota(jnp.int32, (rows, cols), 1)
    both = jnp.where((t == 2 * k) | (t == 2 * k - 1), 0.5, 0.0)
    return jnp.where((k == 0) & (t == 0), 1.0, both).astype(BF)


def pool_matrix_t(rows, cols):
    t = lax.broadcasted_iota(jnp.int32, (rows, cols), 0)
    k = lax.broadcasted_iota(jnp.int32, (rows, cols), 1)
    both = jnp.where((t == 2 * k) | (t == 2 * k - 1), 0.5, 0.0)
    return jnp.where((k == 0) & (t == 0), 1.0, both).astype(BF)


def head_masks():
    lane = lax.broadcasted_iota(jnp.int32, (1, 128), 1)
    first = jnp.where(lane < HEAD_DIM, 1.0, 0.0)
    return first.astype(BF), (1.0 - first).astype(BF)


def both_heads(x, masks):
    return jnp.concatenate([x * masks[0], x * masks[1]], axis=0)


QB = 128


def attn_fwd_step(stride, pairs, valid, qw_ref, qr_ref, k_ref, v_ref, tab_ref, mixed_ref, inv_ref, p_ref):
    masks = head_masks()
    lane = lax.broadcasted_iota(jnp.int32, (1, 128), 1)
    keys = k_ref.shape[1]
    queries = qw_ref.shape[1]
    width = stride * QB + keys
    for pr in range(pairs):
        lanes = slice(pr * 128, (pr + 1) * 128)
        k = k_ref[0, :, lanes]
        v = jnp.concatenate([v_ref[0, :, lanes], jnp.ones((keys, 128), BF)], axis=1)
        outs = []
        for h in range(2):
            content = mm_nt(qw_ref[0, :, lanes] * (masks[h] * SCALE).astype(BF), k)
            relative = mm_nt(qr_ref[0, :, lanes] * (masks[h] * SCALE).astype(BF), tab_ref[:, lanes])
            parts = []
            for b in range(queries // QB):
                rows = slice(b * QB, (b + 1) * QB)
                t0 = stride * (queries - QB - b * QB)
                rolled = pltpu.roll(
                    relative[rows, t0 : t0 + width], width - stride * (QB - 1), 1, stride=stride, stride_axis=0
                )
                scores = jnp.where(valid, content[rows] + rolled[:, :keys], MASKED)
                terms = jnp.exp(scores - jnp.max(scores, axis=-1, keepdims=True)).astype(BF)
                p_ref[0, 2 * pr + h, rows, :] = terms
                parts.append(terms)
            outs.append(mm(jnp.concatenate(parts, axis=0), v))
        inv = 1.0 / jnp.where(lane < HEAD_DIM, outs[0][:, 128:], outs[1][:, 128:])
        inv_ref[0, :, lanes] = inv
        mixed_ref[0, :, lanes] = (jnp.where(lane < HEAD_DIM, outs[0][:, :128], outs[1][:, :128]) * inv).astype(BF)


def attn_fwd(stride, lengths, key_mask, qw, qr, k, v, tab, far=False, cid=None, extra=None):
    s, queries, _ = qw.shape
    keys = k.shape[1]
    table = tab.shape[0]
    pairs = 2
    steps = HEADS // 2 // pairs
    kn = Kernel()
    block = lambda n: pl.BlockSpec((1, n, 128 * pairs), lambda i, j: (i, 0, j))
    h_len, h_mask = kn.inp(lengths, SM), kn.inp(key_mask, VM)
    handles = [
        kn.inp(qw, block(queries)),
        kn.inp(qr, block(queries)),
        kn.inp(k, block(keys)),
        kn.inp(v, block(keys)),
        kn.inp(tab, pl.BlockSpec((table, 128 * pairs), lambda i, j: (0, j))),
        kn.out((s, queries, D), BF, block(queries)),
        kn.out((s, queries, D), F32, block(queries)),
        kn.out((s, HEADS, queries, keys), BF, pl.BlockSpec((1, 2 * pairs, queries, keys), lambda i, j: (i, j, 0, 0))),
    ]
    if extra is not None and far:
        part = extra.shape[1]
        h_ex, h_full, r_sem, l_sem = kn.inp(extra), kn.out((s, 2 * part, D), BF), kn.sems(1, 2), kn.sems(1)

    def body(get):
        if extra is not None and far:
            side = lax.axis_index("seq")
            here = get(h_full).at[:, pl.ds(side * part, part)]
            copies = lambda: (
                remote(get(h_ex).at[pl.ds((1 - side) * s, s)], here, get(r_sem), 0, ALONG_Y),
                pltpu.make_async_copy(get(h_ex).at[pl.ds(side * s, s)], here, get(l_sem).at[0]),
            )
            first = jnp.logical_and(pl.program_id(0) == 0, pl.program_id(1) == 0)
            end = jnp.logical_and(pl.program_id(0) == s - 1, pl.program_id(1) == steps - 1)

            @pl.when(first)
            def _():
                greet([ALONG_Y])
                for copy in copies():
                    copy.start()

        own = lax.axis_index("seq") * s + pl.program_id(0)
        kept = get(h_mask)[pl.ds(own, 1), :]
        spots = lax.broadcasted_iota(jnp.int32, kept.shape, 1)
        valid = jnp.where((kept > 0) & (spots < get(h_len)[own]), 1.0, 0.0)
        if stride == 1:
            rows = jnp.broadcast_to(valid, (8, valid.shape[1])).astype(BF)
            valid = mm_nt(rows, pool_matrix(keys, valid.shape[1]))[0:1]
        attn_fwd_step(stride, pairs, valid > 0.0, *[get(h) for h in handles])
        if extra is not None and far:

            @pl.when(end)
            def _():
                for copy in copies():
                    copy.wait()

    return kn.run(
        body,
        "attn_fwd_%d" % stride,
        cost(2 * s * HEADS * queries * keys * 64 * 4, 12 * MIB, s * HEADS * queries * keys),
        grid=(s, steps),
        cid=cid if extra is not None and far else None,
    )


def ffn_fwd(mixed, resid, w_out, w_up, w_down, w_qkv, attn_bias, up_bias, gain, nbias, obias):
    rows = mixed.shape[0]
    kn = Kernel()
    h_mixed, h_resid = kn.inp(mixed, VM), kn.inp(resid, VM)
    h_wout, h_up, h_down, h_qkv = (kn.inp(x) for x in (w_out, w_up, w_down, w_qkv))
    h_ab, h_upb, h_gain, h_nb, h_ob = (kn.inp(x, VM) for x in (attn_bias, up_bias, gain, nbias, obias))
    wout, wup, wdown, wqkv = kn.mem((D, D)), kn.mem((D, FF)), kn.mem((FF, D)), kn.mem((3, D, D))
    shapes = {"hid": (D, BF), "x1": (D, F32), "r1": (128, F32), "act": (FF, BF), "slope": (FF, BF), "x2": (D, F32)}
    shapes.update({"r2": (128, F32), "out": (D, F32), "low": (D, BF), "qw": (D, BF), "qr": (D, BF), "k": (D, BF), "v": (D, BF)})
    order = list(shapes)
    outs = {n: (kn.out((rows, c), t), kn.mem((rows, c), t)) for n, (c, t) in shapes.items()}
    l_sem, o_sem = kn.sems(4), kn.sems(len(order))
    h_total = kn.mem((rows, D), F32)

    def body(get):
        mem = lambda n: get(outs[n][1])
        store = lambda n: pltpu.make_async_copy(mem(n), get(outs[n][0]), get(o_sem).at[order.index(n)])
        pairs = ((get(h_wout).at[0], wout), (get(h_up).at[0], wup), (get(h_down).at[0], wdown), (get(h_qkv).at[1], wqkv))
        loads = [pltpu.make_async_copy(src, get(dst), get(l_sem).at[i]) for i, (src, dst) in enumerate(pairs)]
        for copy in loads:
            copy.start()
        gain_ref, nb_ref, ob_ref, ab_ref = get(h_gain), get(h_nb), get(h_ob), get(h_ab)
        loads[0].wait()
        x1, r1 = ln_fwd(get(h_resid)[...] + (mm(get(h_mixed)[...], get(wout)[...]) + ob_ref[0, 0:1, :]))
        mem("x1")[...] = x1
        mem("r1")[...] = jnp.broadcast_to(r1, (rows, 128))
        hidden = x1 * gain_ref[0, 0:1, :] + nb_ref[0, 0:1, :]
        mem("hid")[...] = hidden.astype(BF)
        for n in ("x1", "r1", "hid"):
            store(n).start()
        total = get(h_total)
        total[...] = hidden + ob_ref[0, 1:2, :]
        loads[1].wait()
        for c in range(0, PANELS, WIDE):
            cols = slice(c * D, (c + WIDE) * D)
            act, slope = gelu_and_slope(mm(mem("hid")[...], get(wup)[:, cols]) + get(h_upb)[0:1, cols])
            act = act.astype(BF)
            mem("act")[:, cols] = act
            mem("slope")[:, cols] = slope.astype(BF)
            if c == 0:
                loads[2].wait()
            total[...] += mm(act, get(wdown)[cols, :])
        store("act").start()
        store("slope").start()
        x2, r2 = ln_fwd(total[...])
        mem("x2")[...] = x2
        mem("r2")[...] = jnp.broadcast_to(r2, (rows, 128))
        out = x2 * gain_ref[0, 1:2, :] + nb_ref[0, 1:2, :]
        mem("out")[...] = out
        low = out.astype(BF)
        mem("low")[...] = low
        for n in ("x2", "r2", "out", "low"):
            store(n).start()
        loads[3].wait()
        q = mm(low, get(wqkv)[0])
        mem("qw")[...] = (q + ab_ref[1, 0:1, :]).astype(BF)
        mem("qr")[...] = (q + ab_ref[1, 1:2, :]).astype(BF)
        store("qw").start()
        store("qr").start()
        mem("k")[...] = mm(low, get(wqkv)[1]).astype(BF)
        store("k").start()
        mem("v")[...] = mm(low, get(wqkv)[2]).astype(BF)
        store("v").start()
        for n in order:
            store(n).wait()

    return kn.run(body, "ffn_fwd", cost(2 * rows * D * D * 12, 34 * MIB, rows * FF), limit=60)


def places(order, rows_each, far):
    me = lax.axis_index("rows") if far else 0
    side = lax.axis_index("seq") if far else 0
    base = {}
    for r in range(SHARDS):
        for half in range(2):
            spot = 0
            for axis, b in bits_of(order):
                c = half if axis == "seq" else (r // b) % 2
                mine = side if axis == "seq" else me
                spot = spot * 2 + (lax.rem(bit(mine, b) + c, 2) if far else c)
            base[r, half] = spot * rows_each
    return base


def put(buf_ref, mat, base, tile, shards, rows, first=0, pitch=None):
    low = tile.astype(BF)
    width = buf_ref.shape[2]
    for n, r in enumerate(shards):
        for half in range(2):
            start = base[r, half]
            if not isinstance(start, int):
                start = pl.multiple_of(start, 16)
            top = n * pitch + first
            buf_ref[mat, pl.ds(start, rows), :] = low[top : top + rows, half * width : (half + 1) * width]


NA = SHARDS * ROW
BORN_ORDERS = (XY, XY, XY)
SWAP_POINT = 9
BORN_POINTS = ({1: 11}, {})
SMALL_STEPS = (
    (CORE,),
    (ALONG_X, ALONG_Y, (ALONG_X, ALONG_Y)),
    (Z_NEAR, Z_FAR, Z_DIAG),
)
UP_AT = ((0, 0), (0, 1), (0, 2), (1, 0))
DOWN_AT = ((1, 1), (1, 2), (2, 0), (2, 1))
OUT_AT = (2, 2)
FFN_ORDERS = (XZY, YX, ZYX)
FFN_MATS = (3, 3, 3)
ATT_ORDERS = ((XY, YX), (XZY, YX))


class FfnGrads:
    def __init__(self, kn, far, rows):
        full = lambda shape: pl.BlockSpec(shape, lambda *g: (0,) * len(shape))
        self.dmixed = kn.out((rows, D), BF, full((rows, D)))
        self.dbranch = kn.out((rows, D), BF, full((rows, D)))
        self.dres = kn.out((rows, D), F32, full((rows, D)))
        self.small = kn.out((8, D), F32, full((8, D)))
        self.upg = kn.out((8, FF), F32, full((8, FF)))
        self.groups = [Group(kn, far, order, mats, ROW) for order, mats in zip(FFN_ORDERS, FFN_MATS)]
        self.wup, self.wdown = kn.mem((D, FF)), kn.mem((FF, D))
        self.act, self.slope = kn.mem((rows, FF)), kn.mem((rows, FF))
        self.dffn, self.dhid = kn.mem((rows, D)), kn.mem((rows, D), F32)
        self.near = kn.sems(4)

    def run(self, get, dy, x2, r2, gain2, gain1, wout_ref, hid_ref, mixed_ref, x1, r1, at):
        small_ref, upg_ref, dffn_ref, dhid_ref = get(self.small), get(self.upg), get(self.dffn), get(self.dhid)
        act, slope, wup, wdown = get(self.act), get(self.slope), get(self.wup), get(self.wdown)
        for group in self.groups:
            group.bind(get)
            group.locate()
        small_ref[...] = jnp.zeros_like(small_ref)
        dpost = ln_bwd(dy, x2, r2, gain2)
        small_ref[1:2, :] = jnp.sum(dy * x2, axis=0, keepdims=True)
        small_ref[3:4, :] = jnp.sum(dy, axis=0, keepdims=True)
        dffn = dpost.astype(BF)
        small_ref[5:6, :] = jnp.sum(dffn.astype(F32), axis=0, keepdims=True)
        dffn_ref[...] = dffn
        dhid_ref[...] = dpost
        at(0)
        each = SHARDS // PANELS
        groups = self.groups
        for w in range(0, PANELS, WIDE):
            ddown = mm_tn(act[:, w * D : (w + WIDE) * D], dffn_ref[...])
            shards = range(w * each, (w + WIDE) * each)
            for i, (group, mat) in enumerate(DOWN_AT):
                groups[group].put(mat, ddown, shards, i * ROW, UP_ROWS)
        for group, mat in DOWN_AT:
            groups[group].leave(mat)
        for w in range(0, PANELS, WIDE):
            cols = slice(w * D, (w + WIDE) * D)
            dact = mm_nt(dffn_ref[...], wdown[cols, :])
            dpre = (dact * slope[:, cols].astype(F32)).astype(BF)
            upg_ref[:, cols] = jnp.broadcast_to(jnp.sum(dpre.astype(F32), axis=0, keepdims=True), (8, WIDE * D))
            dup = mm_tn(hid_ref[...], dpre)
            for i in range(WIDE):
                group, mat = UP_AT[w + i]
                groups[group].put(mat, dup[:, i * D : (i + 1) * D], range(SHARDS))
                groups[group].leave(mat)
            dhid_ref[...] += mm_nt(dpre, wup[:, cols])
            at(w // WIDE + 1)
        for group, mat in DOWN_AT + UP_AT[:WIDE]:
            groups[group].settle(mat)
        dhid = dhid_ref[...]
        xh = x1()
        small_ref[0:1, :] = jnp.sum(dhid * xh, axis=0, keepdims=True)
        small_ref[2:3, :] = jnp.sum(dhid, axis=0, keepdims=True)
        dres = ln_bwd(dhid, xh, r1(), gain1)
        get(self.dres)[...] = dres
        dbranch = dres.astype(BF)
        get(self.dbranch)[...] = dbranch
        small_ref[4:5, :] = jnp.sum(dbranch.astype(F32), axis=0, keepdims=True)
        group, mat = OUT_AT
        groups[group].put(mat, mm_tn(mixed_ref[...], dbranch), range(SHARDS))
        groups[group].leave(mat)
        get(self.dmixed)[...] = mm_nt(dbranch, wout_ref[0]).astype(BF)
        for group, mat in UP_AT[WIDE:] + (OUT_AT,):
            groups[group].settle(mat)
        for group in groups:
            group.end()

    def results(self, res):
        own = [res[h[1]] for h in (self.dmixed, self.dbranch, self.dres, self.small, self.upg)]
        return own, [group.result(res) for group in self.groups]


def ffn_last(far, cid, mixed, resid, cot, w_out, w_up, w_down, up_bias, gain, nbias, obias):
    rows = mixed.shape[0]
    kn = Kernel()
    whole = pl.BlockSpec((rows, D), lambda i: (0, 0))
    layer = pl.BlockSpec((1, 2, D), lambda i: (1, 0, 0))
    h_mixed, h_resid, h_cot = (kn.inp(x, whole) for x in (mixed, resid, cot))
    h_wout = kn.inp(w_out, pl.BlockSpec((1, D, D), lambda i: (1, 0, 0)))
    h_up, h_down = kn.inp(w_up), kn.inp(w_down)
    h_upb = kn.inp(up_bias, pl.BlockSpec((2, FF), lambda i: (0, 0)))
    h_gain, h_nbias, h_obias = (kn.inp(x, layer) for x in (gain, nbias, obias))
    h_lout = kn.out((rows, D), BF, whole)
    grads = FfnGrads(kn, far, rows)
    h_hid, h_x1 = kn.mem((rows, D)), kn.mem((rows, D), F32)

    def body(get):
        if far:
            greet([CORE])
        near = get(grads.near)
        wup, wdown, act, slope, hid, x1s = (
            get(h) for h in (grads.wup, grads.wdown, grads.act, grads.slope, h_hid, h_x1)
        )
        dhid_s = get(grads.dhid)
        gain_ref, nbias_ref, obias_ref, upb_ref, wout_ref = (
            get(h) for h in (h_gain, h_nbias, h_obias, h_upb, h_wout)
        )
        cp_up = pltpu.make_async_copy(get(h_up).at[1], wup, near.at[0])
        cp_down = pltpu.make_async_copy(get(h_down).at[1], wdown, near.at[1])
        cp_up.start()
        cp_down.start()
        pre_norm = get(h_resid)[...] + (mm(get(h_mixed)[...], wout_ref[0]) + obias_ref[0, 0:1, :])
        x1, r1 = ln_fwd(pre_norm)
        x1s[...] = x1
        hidden = x1 * gain_ref[0, 0:1, :] + nbias_ref[0, 0:1, :]
        hid[...] = hidden.astype(BF)
        dhid_s[...] = hidden + obias_ref[0, 1:2, :]
        cp_up.wait()
        cp_down.wait()
        for c in range(0, PANELS, WIDE):
            cols = slice(c * D, (c + WIDE) * D)
            a, s = gelu_and_slope(mm(hid[...], wup[:, cols]) + upb_ref[1:2, cols])
            a = a.astype(BF)
            act[:, cols] = a
            slope[:, cols] = s.astype(BF)
            dhid_s[...] += mm(a, wdown[cols, :])
        x2, r2 = ln_fwd(dhid_s[...])
        get(h_lout)[...] = (x2 * gain_ref[0, 1:2, :] + nbias_ref[0, 1:2, :]).astype(BF)
        grads.run(
            get, get(h_cot)[...].astype(F32), x2, r2, gain_ref[0, 1:2, :], gain_ref[0, 0:1, :], wout_ref, hid,
            get(h_mixed), lambda: x1s[...], lambda: r1, lambda point: None,
        )

    res = kn.run(
        body, "ffn_last", cost(2 * rows * D * D * 26, 30 * MIB, rows * FF), grid=(1,), cid=cid if far else None, limit=63
    )
    return res[h_lout[1]], *grads.results(res)


def ffn_bwd(far, cid, chains, dy, x2, r2, hid, mixed, x1, r1, gain, w_out, w_up, w_down, act, slope):
    rows = hid.shape[0]
    kn = Kernel()
    whole = pl.BlockSpec((rows, D), lambda i: (0, 0))
    thin = pl.BlockSpec((rows, 128), lambda i: (0, 0))
    h_dy, h_x2, h_hid, h_mixed, h_x1 = (kn.inp(x, whole) for x in (dy, x2, hid, mixed, x1))
    h_r2, h_r1 = (kn.inp(x, thin) for x in (r2, r1))
    h_gain = kn.inp(gain, pl.BlockSpec((1, 2, D), lambda i: (0, 0, 0)))
    h_wout = kn.inp(w_out, pl.BlockSpec((1, D, D), lambda i: (0, 0, 0)))
    h_up, h_down, h_act, h_slope = (kn.inp(x) for x in (w_up, w_down, act, slope))
    grads = FfnGrads(kn, far, rows)
    links = [Chain(kn, *c[:3]) for c in chains]
    def body(get):
        near = get(grads.near)
        if far:
            greet([CORE, ALONG_X, ALONG_Y, Z_ALL])
        for link in links:
            link.bind(get)
            link.go(0)
        loads = [
            pltpu.make_async_copy(get(h_act), get(grads.act), near.at[0]),
            pltpu.make_async_copy(get(h_down).at[0], get(grads.wdown), near.at[1]),
            pltpu.make_async_copy(get(h_slope), get(grads.slope), near.at[2]),
            pltpu.make_async_copy(get(h_up).at[0], get(grads.wup), near.at[3]),
        ]
        for copy in loads:
            copy.start()

        def at(point):
            if point == 0:
                for copy in loads:
                    copy.wait()
            for link, (_, _, _, when) in zip(links, chains):
                if point in when:
                    link.go(when[point])

        gain_ref = get(h_gain)
        grads.run(
            get, get(h_dy)[...], get(h_x2)[...], get(h_r2)[:, 0:1], gain_ref[0, 1:2, :], gain_ref[0, 0:1, :],
            get(h_wout), get(h_hid), get(h_mixed), lambda: get(h_x1)[...], lambda: get(h_r1)[:, 0:1], at,
        )
        for link, (_, _, close, _) in zip(links, chains):
            if not close:
                link.go(link.j)
        for link in links:
            link.end()

    res = kn.run(
        body, "ffn_bwd", cost(2 * rows * D * D * 18, 40 * MIB), grid=(1,), cid=cid if far else None, limit=63
    )
    return *grads.results(res), [link.result(res) for link in links]


def attn_bwd_step(
    stride, seq, lanes, p_ref, inv_ref, qw_ref, qr_ref, k_ref, v_ref, tab_ref, dm_ref, dq, dk_out, dv_out, dtab, dbias
):
    masks = head_masks()
    lane = lax.broadcasted_iota(jnp.int32, (1, 128), 1)
    first = lane < HEAD_DIM
    keys = k_ref.shape[1]
    queries = qw_ref.shape[1]
    blocks = queries // QB
    width = stride * QB + keys
    flip_i = lax.broadcasted_iota(jnp.int32, (queries, queries), 0)
    flip_j = lax.broadcasted_iota(jnp.int32, (queries, queries), 1)
    flip = jnp.where(flip_i + flip_j == queries - 1, 1.0, 0.0).astype(BF)

    @pl.when(seq == 0)
    def _():
        dtab[:, lanes] = jnp.zeros((dtab.shape[0], 128), F32)
        dbias[:, lanes] = jnp.zeros((dbias.shape[0], 128), F32)

    k = k_ref[0]
    v = v_ref[0]
    inv = inv_ref[0]
    scaled = (dm_ref[0].astype(F32) * inv).astype(BF)
    qr_rev = mm(flip, qr_ref[0]).astype(BF)
    dk = jnp.zeros((keys, 128), F32)
    dv = jnp.zeros((keys, 128), F32)
    dqws, dqrs = [], []
    for h in range(2):
        dmh = scaled * masks[h]
        terms = p_ref[0, h]
        dprob = mm_nt(dmh, v)
        wide = terms.astype(F32)
        inner = jnp.sum(dprob * wide, axis=-1, keepdims=True) * inv[:, h * HEAD_DIM : h * HEAD_DIM + 1]
        ds = (wide * (dprob - inner)).astype(BF)
        dv = dv + mm_tn(terms, dmh)
        dk = dk + mm_tn(ds, qw_ref[0] * masks[h])
        dqws.append(mm(ds, k))
        rev = mm(flip, ds)
        back = []
        for b in range(blocks):
            rows = slice(b * QB, (b + 1) * QB)
            t0 = stride * b * QB
            padded = jnp.concatenate([rev[rows], jnp.zeros((QB, width - keys), F32)], axis=1)
            rel = pltpu.roll(padded, 0, 1, stride=stride, stride_axis=0).astype(BF)
            dtab[t0 : t0 + width, lanes] += mm_tn(rel, qr_rev[rows] * masks[h]) * SCALE
            back.append(mm(rel, tab_ref[t0 : t0 + width, :]))
        dqrs.append(jnp.concatenate(back, axis=0))
    dqw = jnp.where(first, dqws[0], dqws[1]) * SCALE
    hi, lo = split_hi_lo(jnp.where(first, dqrs[0], dqrs[1]))
    dqr = (mm(flip, hi) + mm(flip, lo)) * SCALE
    dq[pl.ds(pl.multiple_of(seq * queries, QB), queries), lanes] = (dqw + dqr).astype(BF)
    at = pl.ds(pl.multiple_of(seq * keys, QB), keys)
    dk_out[at, lanes] = (dk * SCALE).astype(BF)
    dv_out[at, lanes] = dv.astype(BF)
    dbias[0:1, lanes] += jnp.sum(dqw, axis=0, keepdims=True)
    dbias[1:2, lanes] += jnp.sum(dqr, axis=0, keepdims=True)


def back_layer(
    far, cid, layer, plan, p, inv, qw, qr, k, v, tab, dmixed, dres, w_qkv, xq, xk, enc, smalls=None, lout=None
):
    s, queries, _ = qw.shape
    keys = k.shape[1]
    table = tab.shape[0]
    last = s * (HEADS // 2)
    nq, nk = s * queries, s * keys
    tail = smalls is not None
    kn = Kernel()
    seq_of = lambda g: lax.rem(jnp.minimum(g, last - 1), s)
    pair_of = lambda g: lax.div(jnp.minimum(g, last - 1), s)
    pair_block = lambda n: pl.BlockSpec((1, n, 128), lambda g: (seq_of(g), 0, pair_of(g)))
    h_p = kn.inp(p, pl.BlockSpec((1, 2, queries, keys), lambda g: (seq_of(g), pair_of(g), 0, 0)))
    h_inv, h_qw, h_qr, h_dm = (kn.inp(x, pair_block(queries)) for x in (inv, qw, qr, dmixed))
    h_k, h_v = (kn.inp(x, pair_block(keys)) for x in (k, v))
    h_tab = kn.inp(tab, pl.BlockSpec((table, 128), lambda g: (0, pair_of(g))))
    dq_s, dk_s, dv_s = kn.mem((nq, D)), kn.mem((nk, D)), kn.mem((nk, D))
    dtab_s, dbias_s = kn.mem((table, D), F32), kn.mem((8, D), F32)
    late = [(dres, F32), (xq, BF), (enc, BF)]
    if layer == 0 or xk is not xq:
        late.append((xk, BF))
    late_in = [kn.inp(x) for x, _ in late]
    late_mem = [kn.mem(x.shape, t) for x, t in late]
    h_w, h_wm = kn.inp(w_qkv), kn.mem((3, D, D))
    l_sem = kn.sems(len(late) + 1)
    chains = [Chain(kn, so_far, steps, close) for so_far, steps, close, _ in plan]
    whole = lambda shape: pl.BlockSpec(shape, lambda g: (0,) * len(shape))
    half = keys // 2
    born, groups = [], []
    if tail and far:
        for order in BORN_ORDERS:
            born.append(Chain(kn, None, order[1:], True, (kn.mem((4, 2 * NA, BLOCK)), 4, NA, BLOCK)))
    else:
        groups = [Group(kn, far, order, 2 * BLOCKS, ROW, BLOCK) for order in ATT_ORDERS[layer]]
    if tail and far:
        h_small = [kn.inp(x, whole(x.shape)) for x in smalls]
        sum_shape = (2 * SMALL_ROWS, D)
        h_sum = kn.out(sum_shape, F32, whole(sum_shape))
        sm = [kn.mem(sum_shape, F32) for _ in range(len(SMALL_STEPS))]
        sm_in = [kn.mem(sum_shape, F32) for step in SMALL_STEPS for _ in step]
        sm_sem = kn.sems(len(sm_in), 2)
        h_dx = kn.out((s, half, D), F32, whole((s, half, D)))
        h_piece, h_got, h_swap = kn.mem((s, half, D)), kn.out((s, half, D), BF), kn.sems(s, 2)
    else:
        h_dx = kn.out((nk, D), F32, whole((nk, D)))
        h_bias = kn.out((8, D), F32, whole((8, D)))
    swaps = lout is not None and far
    if swaps:
        h_lout, h_lgot, l_swap = kn.inp(lout), kn.out((s, queries // 2, D), BF), kn.sems(1, 2)
    greeted = [step for _, steps, _, _ in plan for step in steps] + [CORE]
    if tail:
        greeted = [CORE, ALONG_X, ALONG_Y, (ALONG_X, ALONG_Y), Z_ALL]

    def body(get):
        g = pl.program_id(0)
        dq, dk, dv, dtab, dbias = (get(h) for h in (dq_s, dk_s, dv_s, dtab_s, dbias_s))
        loads = [pltpu.make_async_copy(get(a), get(b), get(l_sem).at[i]) for i, (a, b) in enumerate(zip(late_in, late_mem))]
        loads.append(pltpu.make_async_copy(get(h_w).at[layer], get(h_wm), get(l_sem).at[len(late)]))
        for chain in chains + born:
            chain.bind(get)

        @pl.when(g == 0)
        def _():
            if far:
                greet(greeted)
            for copy in loads:
                copy.start()

        @pl.when(g < last)
        def _():
            lanes = pl.ds(pl.multiple_of(pair_of(g) * 128, 128), 128)
            attn_bwd_step(
                2 - layer, seq_of(g), lanes, get(h_p), get(h_inv), get(h_qw), get(h_qr), get(h_k), get(h_v), get(h_tab), get(h_dm),
                dq, dk, dv, dtab, dbias,
            )

        for point in range(last):
            acts = [(c, k) for c, (_, _, _, when) in zip(chains, plan) for k, w in when.items() if w == point]
            if acts:

                @pl.when(g == point)
                def _():
                    for chain, k in acts:
                        chain.go(k)

        def swap_lout():
            other = 1 - lax.axis_index("seq")
            half_of = get(h_lout).at[:, pl.ds(other * (queries // 2), queries // 2)]
            return remote(half_of, get(h_lgot), get(l_swap), 0, ALONG_Y)

        if swaps:

            @pl.when(g == SWAP_POINT)
            def _():
                swap_lout().start()

        dres_ref, xq_ref, enc_ref = (get(h) for h in late_mem[:3])
        xk_ref = get(late_mem[3]) if layer == 0 or xk is not xq else xq_ref
        for group in groups:
            group.bind(get)
        per = last // BLOCKS

        def swap_piece(i):
            return remote(get(h_piece).at[i], get(h_got).at[i], get(h_swap), i, ALONG_Y)

        def make(t):
            cols = slice(2 * t * BLOCK, 2 * (t + 1) * BLOCK)
            return (
                (1, 0, lambda: mm_tn(xk_ref[...], dv[:, cols])),
                (0, 0, lambda: mm_tn(xq_ref[...], dq[:, cols])),
                (1, 1, lambda: mm_tn(enc_ref[...], dtab[:, cols].astype(BF))),
                (0, 1, lambda: mm_tn(xk_ref[...], dk[:, cols])),
            )

        def gradients(t):
            for group in groups:
                group.locate()
            base = places(BORN_ORDERS[t], ROW, far) if tail and far else None
            for which, mat, tile in make(t):
                if tail and far:
                    put(get(born[t].total), 2 * which + mat, base, tile(), range(SHARDS), ROW, 0, ROW)
                else:
                    groups[which].put(2 * t + mat, tile(), range(SHARDS))
                    groups[which].leave(2 * t + mat)
            if tail and far:
                born[t].core().start()

        def settled(t):
            if tail and far:
                born[t].first()
                return
            for which, mat, _ in make(t):
                groups[which].settle(2 * t + mat)

        for t in range(BLOCKS):

            @pl.when(g == (t + 1) * per - 1)
            def _():
                if t == 0:
                    for copy in loads:
                        copy.wait()
                gradients(t)

            if t < BLOCKS - 1:

                @pl.when(g == (t + 1) * per)
                def _():
                    settled(t)

                for chain in born[t : t + 1]:
                    for k, point in BORN_POINTS[t].items():

                        @pl.when(g == point)
                        def _():
                            chain.go(k)

        @pl.when(g == last)
        def _():
            w = get(h_wm)
            dx_ref = get(h_dx)

            def at(point):
                for chain, (_, _, _, when) in zip(chains, plan):
                    for step, due in when.items():
                        if due == point:
                            chain.go(step)

            if tail and far:
                small_start(get, dbias)
            settled(BLOCKS - 1)
            if tail and far:
                small_round(get, 0)
            at(last)
            if layer == 1:
                dx_ref[...] = dres_ref[...] + (mm_nt(dq[...], w[0]) + mm_nt(dk[...], w[1]) + mm_nt(dv[...], w[2]))
            else:
                spread = pool_matrix_t(keys, queries)
                side = lax.axis_index("seq") if far else 0
                for i in range(s):
                    q_at, k_at = slice(i * queries, (i + 1) * queries), slice(i * keys, (i + 1) * keys)
                    hi, lo = split_hi_lo(dres_ref[q_at, :] + mm_nt(dq[q_at, :], w[0]))
                    dtok = mm_nt(dk[k_at, :], w[1]) + mm_nt(dv[k_at, :], w[2]) + (mm(spread, hi) + mm(spread, lo))
                    if tail and far:
                        low_half, high_half = dtok[:half], dtok[half:]
                        is_low = side == 0
                        dx_ref[i] = jnp.where(is_low, low_half, high_half)
                        get(h_piece)[i] = jnp.where(is_low, high_half, low_half).astype(BF)
                        if i < s - 1:
                            swap_piece(i).start()
                    else:
                        dx_ref[k_at, :] = dtok
            at(last + 1)
            if tail and far:
                finish_tail(get, swap_piece)
                return
            get(h_bias)[...] = dbias[...]
            for chain in chains:
                chain.go(chain.j)
            for group in groups:
                group.end()
            for chain in chains:
                chain.end()
            if swaps:
                swap_lout().wait()

    def small_copies(get, k):
        top = sum(len(step) for step in SMALL_STEPS[:k])
        came = [get(h) for h in sm_in]
        return [
            (came[top + i], remote(get(sm[k]), came[top + i], get(sm_sem), top + i, one))
            for i, one in enumerate(SMALL_STEPS[k])
        ]

    def small_start(get, dbias):
        own = get(sm[0])
        small0, upg0, small1, upg1, bias1 = (get(h) for h in h_small)
        for top, small, upg, bias in ((0, small0, upg0, dbias), (SMALL_ROWS, small1, upg1, bias1)):
            own[top : top + 6, :] = small[0:6, :]
            own[top + 6 : top + 8, :] = bias[0:2, :]
            for p in range(PANELS):
                own[top + 8 + p : top + 9 + p, :] = upg[0:1, p * D : (p + 1) * D]
        for _, copy in small_copies(get, 0):
            copy.start()

    def small_round(get, k):
        pieces = small_copies(get, k)
        for _, copy in pieces:
            copy.wait()
        own = get(sm[k])
        dst = get(sm[k + 1]) if k + 1 < len(SMALL_STEPS) else get(h_sum)
        if len(pieces) == 1:
            dst[...] = own[...] + pieces[0][0][...]
        else:
            a, b, c = (ref[...] for ref, _ in pieces)
            dst[...] = (own[...] + a) + (b + c)
        if k + 1 < len(SMALL_STEPS):
            for _, copy in small_copies(get, k + 1):
                copy.start()

    def finish_tail(get, swap_piece):
        pending = {c: max(when) + 1 for c, (_, _, _, when) in zip(chains, plan)}
        for t, chain in enumerate(born):
            pending[chain] = max([0, *BORN_POINTS[t]]) + 1 if t < BLOCKS - 1 else 1
        order = [chains[1], born[0], born[1], chains[0], chains[2], born[2], *chains[3:]]
        for r in range(5):
            for chain in order:
                k = pending[chain]
                if k <= chain.j:
                    chain.go(k)
                    pending[chain] = k + 1
            if r == 0:
                swap_piece(s - 1).start()
            if r + 1 < len(SMALL_STEPS):
                small_round(get, r + 1)
        for chain in order:
            chain.end()
        for i in range(s):
            swap_piece(i).wait()

    flops = 2 * s * HEADS * queries * keys * 64 * 9 + 2 * D * D * (4 * nq + 4 * nk + table)
    res = kn.run(
        body, "back_layer_%d" % layer, cost(flops, 40 * MIB), grid=(last + 1,), cid=cid if far else None, limit=62
    )
    moved = [chain.result(res) for chain in chains]
    if tail and far:
        return res[h_dx[1]], res[h_got[1]], res[h_sum[1]], moved, [chain.result(res) for chain in born]
    got = res[h_lgot[1]] if swaps else None
    return res[h_dx[1]], res[h_bias[1]], moved, [group.result(res) for group in groups], got


def steps_of(distances):
    half_width = D // 2
    frequency = 10000.0 ** (-jnp.arange(half_width, dtype=F32) / half_width)
    angles = distances.astype(F32)[:, None] * frequency[None, :]
    return jnp.stack([jnp.sin(angles), jnp.cos(angles)])


FINE = 32


def prologue(far, cid, tokens, w_qkv, w_pos, attn_bias):
    parts = 2 if far else 1
    s, part_len = tokens.shape[0] // parts, tokens.shape[1]
    length = part_len * parts
    queries = length // 2
    table = 2 * length
    coarse = steps_of(2 * (queries - 1) - FINE * jnp.arange(table // FINE, dtype=jnp.int32))
    fine = steps_of(-jnp.arange(FINE, dtype=jnp.int32))
    fine2 = steps_of(-2 * jnp.arange(FINE // 2, dtype=jnp.int32))
    kn = Kernel()
    h_tok, h_w, h_wp = (kn.inp(x) for x in (tokens, w_qkv, w_pos))
    h_coarse, h_fine, h_fine2, h_bias = (kn.inp(x, VM) for x in (coarse, fine, fine2, attn_bias))
    names = {}

    def result(name, shape, dtype=BF):
        names[name] = (kn.out(shape, dtype), kn.mem(shape, dtype))

    result("tok", (s, length, D))
    result("enc0", (table, D))
    result("enc1", (table // 2, D))
    result("tab0", (table, D))
    result("tab1", (table // 2, D))
    result("pooled", (s * queries, D), F32)
    for name in ("low", "qw", "qr"):
        result(name, (s * queries, D))
    for name in ("k", "v"):
        result(name, (s, length, D))
    h_wm, h_wpm = kn.mem((3, D, D)), kn.mem((2, D, D))
    o_sem, l_sem, r_sem = kn.sems(len(names)), kn.sems(3), kn.sems(s, 2)
    order = list(names)

    def body(get):
        mem = lambda name: get(names[name][1])

        def store(name):
            return pltpu.make_async_copy(mem(name), get(names[name][0]), get(o_sem).at[order.index(name)])

        ls = get(l_sem)
        tok = mem("tok")
        if far:
            side = lax.axis_index("seq")
            mine = pl.ds(side * s, s)
            greet([ALONG_Y])
            here = pl.ds(side * part_len, part_len)
            sends = [
                remote(get(h_tok).at[pl.ds((1 - side) * s + i, 1)], tok.at[pl.ds(i, 1), here], get(r_sem), i, ALONG_Y)
                for i in range(s)
            ]
            loads = [pltpu.make_async_copy(get(h_tok).at[mine], tok.at[:, here], ls.at[0])]
        else:
            sends = []
            loads = [pltpu.make_async_copy(get(h_tok), tok, ls.at[0])]
        loads += [
            pltpu.make_async_copy(get(h_wp), get(h_wpm), ls.at[1]),
            pltpu.make_async_copy(get(h_w).at[0], get(h_wm), ls.at[2]),
        ]
        for copy in sends + loads:
            copy.start()
        w = get(h_wm)

        def encode(dst, table_rows, fine_ref):
            n = fine_ref.shape[1]
            fs, fc = fine_ref[0], fine_ref[1]
            for a in range(table_rows // n):
                cs, cc = get(h_coarse)[0, a : a + 1, :], get(h_coarse)[1, a : a + 1, :]
                dst[a * n : (a + 1) * n, :HALF] = (cs * fc + cc * fs).astype(BF)
                dst[a * n : (a + 1) * n, HALF:] = (cc * fc - cs * fs).astype(BF)

        encode(mem("enc0"), table, get(h_fine))
        store("enc0").start()
        encode(mem("enc1"), table // 2, get(h_fine2))
        store("enc1").start()
        loads[1].wait()
        wp = get(h_wpm)
        mem("tab0")[...] = mm(mem("enc0")[...], wp[0]).astype(BF)
        store("tab0").start()
        mem("tab1")[...] = mm(mem("enc1")[...], wp[1]).astype(BF)
        store("tab1").start()
        for i in (0, 2):
            loads[i].wait()

        def keys_of(i, part):
            x = tok[i, part, :]
            mem("k")[i, part, :] = mm(x, w[1]).astype(BF)
            mem("v")[i, part, :] = mm(x, w[2]).astype(BF)

        if far:
            for i in range(s):
                keys_of(i, pl.ds(pl.multiple_of(side * part_len, part_len), part_len))
        gather = pool_matrix(queries, length)
        for i in range(s):
            if far:
                sends[i].wait()
                keys_of(i, pl.ds(pl.multiple_of((1 - side) * part_len, part_len), part_len))
            else:
                keys_of(i, pl.ds(0, length))
            at = slice(i * queries, (i + 1) * queries)
            pooled = mm(gather, tok[i])
            mem("pooled")[at, :] = pooled
            low = pooled.astype(BF)
            mem("low")[at, :] = low
            q = mm(low, w[0])
            mem("qw")[at, :] = (q + get(h_bias)[0, 0:1, :]).astype(BF)
            mem("qr")[at, :] = (q + get(h_bias)[0, 1:2, :]).astype(BF)
        for name in ("tok", "k", "v"):
            store(name).start()
        for name in ("pooled", "low", "qw", "qr"):
            store(name).start()
        for name in order:
            store(name).wait()

    res = kn.run(
        body, "prologue", cost(2 * D * D * (3 * s * length + 2 * table), 30 * MIB), cid=cid if far else None
    )
    found = {name: res[h[0][1]] for name, h in names.items()}
    return found


def finish(done, sums, dtok, got, lout, lout_got):
    s, half, _ = dtok.shape
    q = lout_got.shape[1]
    names = ["b00", "b01", "b02", "g00", "g10", "g20", "qk1", "vp1", "g01", "g11", "g21"]
    kn = Kernel()
    hs = {n: (kn.inp(m, VM), kn.inp(o, VM)) for n, (m, o) in zip(names, done)}
    h_sum, h_dtok, h_got, h_lgot = (kn.inp(x, VM) for x in (sums, dtok, got, lout_got))
    h_lout = kn.inp(lout)
    o_lout = kn.out((2 * s, q, D), BF, VM)
    o_tok = kn.out((2 * s, half, D), F32, VM)
    o_qkv = kn.out((2, 3, ROW, D), F32, VM)
    o_out, o_pos = (kn.out((2, ROW, D), F32, VM) for _ in range(2))
    o_up = kn.out((2, ROW, FF), F32, VM)
    o_down = kn.out((2, UP_ROWS, D), F32, VM)
    o_attn = kn.out((2, 2, ROW), F32, VM)
    o_upb = kn.out((2, FF // SHARDS), F32, VM)
    o_gain, o_nb, o_ob = (kn.out((2, 2, ROW), F32, VM) for _ in range(3))
    h_lmem, h_sem = kn.mem((s, q, D)), kn.sems(1)

    def body(get):
        side, me = lax.axis_index("seq"), lax.axis_index("rows")
        copy = pltpu.make_async_copy(
            get(h_lout).at[:, pl.ds(pl.multiple_of(side * q, q), q)], get(h_lmem), get(h_sem).at[0]
        )
        copy.start()
        mine, other = pl.ds(side * s, s), pl.ds((1 - side) * s, s)
        get(o_tok)[mine] = get(h_dtok)[...]
        get(o_tok)[other] = get(h_got)[...].astype(F32)
        get(o_lout)[other] = get(h_lgot)[...]

        def halves(name, mat, dst, lead, base=0, rows=slice(None)):
            for h, which in zip(hs[name], (side, 1 - side)):
                width = get(h).shape[2]
                lanes = pl.ds(pl.multiple_of(base + which * width, 128), width)
                dst[(*lead, rows, lanes)] = get(h)[mat].astype(F32)

        for l in range(2):
            ffn = lambda at: ("g%d%d" % (at[0], l), at[1])
            for t in range(BLOCKS):
                for i, dst, lead in ((0, o_qkv, (l, 0)), (1, o_qkv, (l, 1)), (2, o_qkv, (l, 2)), (3, o_pos, (l,))):
                    name, mat = ("b0%d" % t, i) if l == 0 else (("qk1", "vp1")[i // 2], 2 * t + i % 2)
                    halves(name, mat, get(dst), lead, 2 * t * BLOCK)
            halves(*ffn(OUT_AT), get(o_out), (l,))
            for p in range(PANELS):
                halves(*ffn(UP_AT[p]), get(o_up), (l,), p * D)
                halves(*ffn(DOWN_AT[p]), get(o_down), (l,), rows=slice(p * ROW, (p + 1) * ROW))
        both = get(h_sum)[...]
        turned = pltpu.roll(both, lax.rem(D - me * ROW, D), 1)
        for l in range(2):
            r = 12 * l
            for o, row in ((o_gain, 0), (o_nb, 2), (o_ob, 4), (o_attn, 6)):
                get(o)[l] = turned[r + row : r + row + 2, :ROW]
        wide = FF // SHARDS
        per = D // wide
        shifted = pltpu.roll(both, lax.rem(D - lax.rem(me, per) * wide, D), 1)
        for l in range(2):
            picked = jnp.zeros((1, D), F32)
            for p in range(PANELS):
                picked = picked + jnp.where(lax.div(me, per) == p, shifted[12 * l + 8 + p : 12 * l + 9 + p, :], 0.0)
            get(o_upb)[l : l + 1, :] = picked[:, :wide]
        copy.wait()
        get(o_lout)[mine] = get(h_lmem)[...]

    return tuple(kn.run(body, "finish", cost(1e6, 16 * MIB)))


def swap(x, axis, b):
    n = lax.axis_size(axis)
    return lax.ppermute(x, axis, [(i, i ^ b) for i in range(n)])


def natural(both, order, rows_each):
    mats = both.shape[0]
    both = both.reshape(mats, 2, 2, 2, 2, 2, rows_each, both.shape[-1])
    at = {step: 1 + i for i, step in enumerate(bits_of(order))}
    return both.transpose(0, at[Z_FAR], at[Z_NEAR], at[ALONG_X], at[CORE], 6, at[ALONG_Y], 7)


def to_sequences(x, side, parts):
    own = x.shape[0] // parts
    mine = lax.dynamic_slice_in_dim(x, side * own, own, 0)
    other = swap(lax.dynamic_slice_in_dim(x, (1 - side) * own, own, 0), "seq", 1)
    return jnp.where(
        side == 0, jnp.concatenate([mine, other], axis=1), jnp.concatenate([other, mine], axis=1)
    )


def to_positions(x, side, parts, wire):
    own = x.shape[1] // parts
    mine = lax.dynamic_slice_in_dim(x, side * own, own, 1)
    other = swap(lax.dynamic_slice_in_dim(x, (1 - side) * own, own, 1).astype(wire), "seq", 1).astype(x.dtype)
    return jnp.where(
        side == 0, jnp.concatenate([mine, other], axis=0), jnp.concatenate([other, mine], axis=0)
    )


def elsewhere(att0, ffn0, att1, ffn1, smalls, n_rows, me):
    flat = lambda x: x.reshape(x.shape[0], -1, x.shape[-1] * x.shape[-2])
    rows = lambda x, order: flat(natural(x, order, ROW))
    total = lambda x: lax.psum(lax.psum_scatter(x, "rows", scatter_dimension=1, tiled=True).astype(F32), "seq")

    def quarter(f, at):
        return natural(f[at[0]], FFN_ORDERS[at[0]], ROW)[at[1] : at[1] + 1]

    def att(x, orders):
        qk, vp = (rows(b, o) for b, o in zip(x, orders))
        both = [jnp.concatenate([qk[2 * t : 2 * t + 2], vp[2 * t : 2 * t + 2]]) for t in range(BLOCKS)]
        return total(jnp.concatenate(both, axis=2))

    att0, att1 = att(att0, ATT_ORDERS[0]), att(att1, ATT_ORDERS[1])
    outs = [total(flat(quarter(f, OUT_AT))) for f in (ffn0, ffn1)]
    ups = [total(flat(jnp.concatenate([quarter(f, at) for at in UP_AT]))) for f in (ffn0, ffn1)]
    downs = [total(flat(jnp.concatenate([quarter(f, at) for at in DOWN_AT], axis=5))) for f in (ffn0, ffn1)]
    sums = lax.psum(smalls, ("rows", "seq")).reshape(2, -1, D)
    own = D // n_rows
    cut = lambda x: lax.dynamic_slice_in_dim(x, me * own, own, 2)
    upb = lax.dynamic_slice_in_dim(sums[:, 8:].reshape(2, FF), me * (FF // n_rows), FF // n_rows, 1)
    panels = lambda x: jnp.concatenate(list(x), axis=1)
    return (
        jnp.stack([att0[:3], att1[:3]]),
        jnp.concatenate(outs),
        jnp.stack([att0[3], att1[3]]),
        jnp.stack([panels(x) for x in ups]),
        jnp.concatenate(downs),
        cut(sums[:, 6:8]),
        upb,
        cut(sums[:, 0:2]),
        cut(sums[:, 2:4]),
        cut(sums[:, 4:6]),
    )


def on_device(
    tokens, lengths, key_mask, cotangent, w_qkv, w_out, w_pos, w_up, w_down, attn_bias, up_bias, norm_gain,
    norm_bias, out_bias,
):
    side = lax.axis_index("seq")
    parts = lax.axis_size("seq")
    n_rows = lax.axis_size("rows")
    me = lax.axis_index("rows")
    far = n_rows == SHARDS and parts == 2
    seqs = tokens.shape[0] // parts
    length = tokens.shape[1] * parts
    queries = length // 2
    flat = lambda x: x.reshape(-1, x.shape[-1])
    sets = lambda x: x.reshape(seqs, -1, D)

    if not far:
        tokens, cotangent = to_sequences(tokens, side, parts), to_sequences(cotangent, side, parts)
    start = prologue(far, 1, tokens, w_qkv, w_pos, attn_bias)
    tab0, tab1, enc0, enc1 = (start[n] for n in ("tab0", "tab1", "enc0", "enc1"))
    qw0, qr0, k0, v0 = sets(start["qw"]), sets(start["qr"]), start["k"], start["v"]
    mixed0, inv0, p0, *swapped = attn_fwd(2, lengths, key_mask, qw0, qr0, k0, v0, tab0, far, 6, cotangent)
    cot = swapped[0] if far else cotangent
    mixed0 = flat(mixed0)
    hid, x1, r1, act, slope, x2, r2, first, first_low, qw1, qr1, k1, v1 = ffn_fwd(
        mixed0, start["pooled"], w_out, w_up, w_down, w_qkv, attn_bias, up_bias, norm_gain, norm_bias, out_bias
    )
    qw1, qr1, k1, v1 = sets(qw1), sets(qr1), sets(k1), sets(v1)
    mixed1, inv1, p1 = attn_fwd(1, lengths, key_mask, qw1, qr1, k1, v1, tab1)
    mixed1 = flat(mixed1)
    lout, (dmixed1, dbranch1, dres1, small1, upg1), ffn1 = ffn_last(
        far, 2, mixed1, first, flat(cot), w_out, w_up, w_down, up_bias, norm_gain, norm_bias, out_bias
    )
    lout = sets(lout)
    plan = []
    if far:
        plan = [(x, order[1:3], False, {0: 0, 1: 8}) for x, order in zip(ffn1, FFN_ORDERS)]
    dfirst, dbias1, moved, att1, lout_got = back_layer(
        far, 3, 1, plan, p1, inv1, qw1, qr1, k1, v1, tab1, sets(dmixed1), dres1, w_qkv, first_low, first_low, enc1,
        lout=lout,
    )
    chains = []
    if far:
        for x, order in zip(moved, FFN_ORDERS):
            steps = order[3:]
            chains.append((x, steps, True, {k: k for k in range(1, len(steps) + 1)}))
        chains += [(x, order[1:3], False, {2: 1}) for x, order in zip(att1, ATT_ORDERS[1])]
    (dmixed0, dbranch0, dres0, small0, upg0), ffn0, moved = ffn_bwd(
        far, 4, chains, dfirst, x2, r2, hid, mixed0, x1, r1, norm_gain, w_out, w_up, w_down, act, slope
    )
    plan = []
    if far:
        when = ({0: 0, 1: 7, 2: 11}, {0: 0, 1: 7}, {0: 0, 1: 7, 2: 11})
        plan = [(x, order[1:], True, due) for x, order, due in zip(ffn0, FFN_ORDERS, when)]
        plan += [(x, order[3:], True, {0: 1, 1: 9}) for x, order in zip(moved[3:], ATT_ORDERS[1])]
    args = (p0, inv0, qw0, qr0, k0, v0, tab0, sets(dmixed0), dres0, w_qkv, start["low"], flat(start["tok"]), enc0)
    if far:
        dtok, got, sums, ended, att0 = back_layer(far, 5, 0, plan, *args, smalls=(small0, upg0, small1, upg1, dbias1))
        done = att0 + ended + moved[:3]
        return finish(done, sums, dtok, got, lout, lout_got)
    dtok, dbias0, _, att0, _ = back_layer(far, 5, 0, plan, *args)
    small = lambda s, u, b: jnp.concatenate([s[:6], b[:2], u[0].reshape(PANELS, D)], axis=0)
    smalls = jnp.concatenate([small(small0, upg0, dbias0), small(small1, upg1, dbias1)], axis=0)
    return (
        to_positions(lout, side, parts, BF),
        to_positions(sets(dtok), side, parts, BF),
        *elsewhere(att0, ffn0, att1, ffn1, smalls, n_rows, me),
    )


def solution(mesh):
    seq3 = P("rows", "seq", None)
    in_specs = (seq3, P("rows"), P("rows", None), seq3) + (P(),) * 10
    mat = P(None, "rows", None)
    vec = P(None, None, "rows")
    out_specs = (seq3, seq3, P(None, None, "rows", None), mat, mat, mat, mat, vec, P(None, "rows"), vec, vec, vec)
    return jax.shard_map(on_device, mesh=mesh, in_specs=in_specs, out_specs=out_specs, check_vma=False)
```

```python
import functools

import jax
import jax.numpy as jnp
from jax import lax
from jax.experimental import pallas as pl
from jax.experimental.pallas import tpu as pltpu
from jax.sharding import PartitionSpec as P

D = 768
HEADS = 12
HEAD_DIM = 64
FF = 3072
PANELS = FF // D
HALF = D // 2
EPS = 1e-06
MASKED = -1000000000.0
SCALE = HEAD_DIM ** (-0.5)
BF = jnp.bfloat16
F32 = jnp.float32
MIB = 1 << 20

SHARDS = 16
MESH = pl.DeviceIdType.MESH
UP_ROWS = PANELS * D // SHARDS
ROW = D // SHARDS
WIDE = 2
SMALL_ROWS = 12


def mm(a, b):
    return lax.dot_general(a, b, (((1,), (0,)), ((), ())), preferred_element_type=F32)


def mm_nt(a, b):
    return lax.dot_general(a, b, (((1,), (1,)), ((), ())), preferred_element_type=F32)


def mm_tn(a, b):
    return lax.dot_general(a, b, (((0,), (0,)), ((), ())), preferred_element_type=F32)


def ln_fwd(z):
    center = z - jnp.mean(z, axis=-1, keepdims=True)
    var = jnp.mean(center * center, axis=-1, keepdims=True)
    rstd = lax.rsqrt(var + EPS)
    return center * rstd, rstd


def ln_bwd(dy, xhat, rstd, gain):
    dx = dy * gain
    m1 = jnp.mean(dx, axis=-1, keepdims=True)
    m2 = jnp.mean(dx * xhat, axis=-1, keepdims=True)
    return rstd * (dx - m1 - xhat * m2)


GELU_K = 0.7978845608028654
GELU_C = 0.044715


def gelu_and_slope(z):
    z2 = z * z
    t = jnp.tanh(GELU_K * z * (1.0 + GELU_C * z2))
    half = 0.5 * (1.0 + t)
    slope = half + 0.5 * z * (1.0 - t * t) * (GELU_K * (1.0 + 3.0 * GELU_C * z2))
    return z * half, slope


def split_hi_lo(x):
    hi = x.astype(BF)
    return hi, (x - hi.astype(F32)).astype(BF)


def cost(flops, nbytes, trans=0):
    return pl.CostEstimate(flops=int(flops), bytes_accessed=int(nbytes), transcendentals=int(trans))


def params(limit=56, **kw):
    return pltpu.CompilerParams(vmem_limit_bytes=limit * MIB, **kw)


def full_spec(shape, memory_space=pltpu.VMEM):
    return pl.BlockSpec(memory_space=memory_space)


ANY = pl.BlockSpec(memory_space=pl.ANY)
VM = pl.BlockSpec(memory_space=pltpu.VMEM)
SM = pl.BlockSpec(memory_space=pltpu.SMEM)


def sds(shape, dtype):
    return jax.ShapeDtypeStruct(shape, dtype)


CORE = ("rows", 1)
ALONG_X = ("rows", 2)
ALONG_Y = ("seq", 1)
Z_NEAR = ("rows", 4)
Z_FAR = ("rows", 8)
Z_DIAG = ("rows", 12)
Z_ALL = ("rows", 0)
XZY = (CORE, ALONG_X, Z_NEAR, ALONG_Y, Z_FAR)
ZYX = (CORE, Z_NEAR, ALONG_Y, ALONG_X, Z_FAR)
XY = (CORE, ALONG_X, ALONG_Y, Z_ALL)
YX = (CORE, ALONG_Y, ALONG_X, Z_ALL)
BLOCK = 128
BLOCKS = D // (2 * BLOCK)


def bit(v, b):
    return lax.rem(lax.div(v, b), 2)


def partner(step):
    if isinstance(step[0], tuple):
        return {axis: spot for one in step for axis, spot in partner(one).items()}
    axis, b = step
    me = lax.axis_index(axis)
    spot = me
    for k in (1, 2, 4, 8):
        if b & k:
            spot = spot + k - 2 * k * bit(me, k)
    return {axis: spot}


def singles(step):
    return (Z_FAR, Z_NEAR, Z_DIAG) if step == Z_ALL else (step,)


def bits_of(order):
    return [one for step in order for one in ((Z_NEAR, Z_FAR) if step == Z_ALL else (step,))]


def greet(steps):
    steps = list(dict.fromkeys(one for step in steps for one in singles(step)))
    sem = pltpu.get_barrier_semaphore()
    for step in steps:
        pl.semaphore_signal(sem, inc=1, device_id=partner(step), device_id_type=MESH)
    pl.semaphore_wait(sem, len(steps))


def remote(src, dst, sems, i, step):
    return pltpu.make_async_remote_copy(
        src_ref=src,
        dst_ref=dst,
        send_sem=sems.at[i, 0],
        recv_sem=sems.at[i, 1],
        device_id=partner(step),
        device_id_type=MESH,
    )


def add_to(dst, first, b, b_first, mats, rows):
    blk = rows
    while blk * dst.shape[2] > 96 * HALF:
        blk //= 2
    per = rows // blk

    def one(i, _):
        m = lax.div(i, per)
        at = pl.ds(pl.multiple_of(lax.rem(i, per) * blk, 16), blk)
        dst[first + m, at, :] = dst[first + m, at, :] + b[b_first + m, at, :]
        return 0

    lax.fori_loop(0, mats * per, one, 0)


class Kernel:
    def __init__(self):
        self.args, self.in_specs, self.out_specs, self.out_shape, self.scr = [], [], [], [], []

    def inp(self, x, spec=ANY):
        self.args.append(x)
        self.in_specs.append(spec)
        return ("i", len(self.args) - 1)

    def out(self, shape, dtype, spec=ANY):
        self.out_shape.append(sds(shape, dtype))
        self.out_specs.append(spec)
        return ("o", len(self.out_shape) - 1)

    def mem(self, shape, dtype=BF):
        self.scr.append(pltpu.VMEM(shape, dtype))
        return ("s", len(self.scr) - 1)

    def sems(self, *shape):
        self.scr.append(pltpu.SemaphoreType.DMA(shape))
        return ("s", len(self.scr) - 1)

    def run(self, body, name, cost_estimate, grid=(), cid=None, limit=56):
        n, m = len(self.args), len(self.out_shape)

        def kernel(*refs):
            groups = {"i": refs[:n], "o": refs[n : n + m], "s": refs[n + m :]}
            body(lambda handle: groups[handle[0]][handle[1]])

        kw = {} if cid is None else dict(collective_id=cid, has_side_effects=True)
        return pl.pallas_call(
            kernel,
            grid=grid,
            in_specs=self.in_specs,
            out_specs=self.out_specs,
            out_shape=self.out_shape,
            scratch_shapes=self.scr,
            compiler_params=params(limit, **kw),
            cost_estimate=cost_estimate,
            name=name,
        )(*self.args)


class Chain:
    def __init__(self, kn, whole, steps, close=False, born=None):
        self.steps, self.close, self.born, self.whole = steps, close, born is not None, whole
        j = len(steps)
        self.j = j
        if self.born:
            self.total, self.m, self.n, width = born
            self.arr = kn.mem((self.m, self.n, width))
        else:
            self.m, self.n, width = whole.shape
            self.src = kn.inp(whole)
            if j:
                self.total = kn.mem((self.m, self.n // (1 + len(singles(steps[0]))), width))
        m = self.m
        self.size = [self.n]
        for step in steps:
            self.size.append(self.size[-1] // (1 + len(singles(step))))
        self.land = [kn.mem((m * len(singles(s)), self.size[k + 1], width)) for k, s in enumerate(steps)]
        self.nf = self.size[-1]
        self.out = kn.out((m, self.nf, width), BF) if j else None
        self.other = kn.out((m, self.nf, width), BF) if close else None
        self.sem = kn.sems(2 * m + 3 * j + 3, 2)

    def bind(self, get):
        self.ref = get
        return self

    def core(self):
        g = self.ref
        return remote(g(self.total).at[:, pl.ds(self.n, self.n)], g(self.arr), g(self.sem), 0, CORE)

    def sends(self, k):
        g, m, j = self.ref, self.m, self.j
        sem = g(self.sem)
        if k == j:
            mine = g(self.total).at[:, pl.ds(0, self.nf)] if j else g(self.src)
            return [remote(mine, g(self.other), sem, 2 * m + 3 * j, ALONG_Y)]
        n = self.size[k + 1]
        source = g(self.total) if k or self.born else g(self.src)
        return [
            remote(
                source.at[:, pl.ds((i + 1) * n, n)], g(self.land[k]).at[pl.ds(i * m, m)], sem, 2 * m + 3 * k + i, one
            )
            for i, one in enumerate(singles(self.steps[k]))
        ]

    def fetch(self):
        g = self.ref
        return pltpu.make_async_copy(
            g(self.src).at[:, pl.ds(0, self.size[1])], g(self.total), g(self.sem).at[2 * self.m + 3 * self.j + 1, 0]
        )

    def keep(self):
        g = self.ref
        return pltpu.make_async_copy(
            g(self.total).at[:, pl.ds(0, self.nf)], g(self.out), g(self.sem).at[2 * self.m + 3 * self.j + 2, 0]
        )

    def first(self):
        g = self.ref
        self.core().wait()
        add_to(g(self.total), 0, g(self.arr), 0, self.m, self.n)
        for copy in self.sends(0):
            copy.start()

    def go(self, k):
        g = self.ref
        if k == 0 and self.j:
            self.fetch().start()
        if k > 0:
            if k == 1 and not self.born:
                self.fetch().wait()
            for copy in self.sends(k - 1):
                copy.wait()
            for b in range(len(singles(self.steps[k - 1]))):
                add_to(g(self.total), 0, g(self.land[k - 1]), b * self.m, self.m, self.size[k])
        if k < self.j or self.close:
            for copy in self.sends(k):
                copy.start()
        if k == self.j and self.j:
            self.keep().start()

    def end(self):
        if self.close:
            for copy in self.sends(self.j):
                copy.wait()
        if self.j:
            self.keep().wait()

    def result(self, res):
        mine = res[self.out[1]] if self.j else self.whole
        return (mine, res[self.other[1]]) if self.close else mine


class Group:
    def __init__(self, kn, far, order, mats, rows_each, width=HALF):
        self.far, self.order, self.mats, self.rows = far, order, mats, rows_each
        self.n = SHARDS * rows_each
        self.buf = kn.mem((mats, 2 * self.n, width))
        if far:
            self.arr = kn.mem((mats, self.n, width))
        self.out = kn.out((mats, self.n if far else 2 * self.n, width), BF)
        self.sem = kn.sems(mats * SHARDS, 2)
        self.done = kn.sems(mats)

    def bind(self, get):
        self.ref = get
        self.sent = {i: [] for i in range(self.mats)}

    def locate(self):
        self.base = places(self.order, self.rows, self.far)

    def put(self, mat, tile, shards, first=0, pitch=None):
        put(self.ref(self.buf), mat, self.base, tile, shards, self.rows, first, pitch or self.rows)

    def leave(self, mat, start=0, n=None):
        if not self.far:
            return
        n = n or self.n
        self.sent[mat].append((start, n))
        self.copy(mat, len(self.sent[mat]) - 1).start()

    def copy(self, mat, i):
        g = self.ref
        start, n = self.sent[mat][i]
        source = g(self.buf).at[mat, pl.ds(self.n + start, n)]
        return remote(source, g(self.arr).at[mat, pl.ds(start, n)], g(self.sem), mat * SHARDS + i, CORE)

    def settle(self, mat):
        g = self.ref
        if self.far:
            for i in range(len(self.sent[mat])):
                self.copy(mat, i).wait()
            add_to(g(self.buf), mat, g(self.arr), mat, 1, self.n)
        self.store(mat).start()

    def store(self, mat):
        g = self.ref
        n = self.n if self.far else 2 * self.n
        return pltpu.make_async_copy(g(self.buf).at[mat, pl.ds(0, n)], g(self.out).at[mat], g(self.done).at[mat])

    def end(self):
        for mat in range(self.mats):
            self.store(mat).wait()

    def result(self, res):
        return res[self.out[1]]


def pool_matrix(rows, cols):
    k = lax.broadcasted_iota(jnp.int32, (rows, cols), 0)
    t = lax.broadcasted_iota(jnp.int32, (rows, cols), 1)
    both = jnp.where((t == 2 * k) | (t == 2 * k - 1), 0.5, 0.0)
    return jnp.where((k == 0) & (t == 0), 1.0, both).astype(BF)


def pool_matrix_t(rows, cols):
    t = lax.broadcasted_iota(jnp.int32, (rows, cols), 0)
    k = lax.broadcasted_iota(jnp.int32, (rows, cols), 1)
    both = jnp.where((t == 2 * k) | (t == 2 * k - 1), 0.5, 0.0)
    return jnp.where((k == 0) & (t == 0), 1.0, both).astype(BF)


def head_masks():
    lane = lax.broadcasted_iota(jnp.int32, (1, 128), 1)
    first = jnp.where(lane < HEAD_DIM, 1.0, 0.0)
    return first.astype(BF), (1.0 - first).astype(BF)


def both_heads(x, masks):
    return jnp.concatenate([x * masks[0], x * masks[1]], axis=0)


QB = 128


def attn_fwd_step(stride, pairs, valid, qw_ref, qr_ref, k_ref, v_ref, tab_ref, mixed_ref, inv_ref, p_ref):
    masks = head_masks()
    lane = lax.broadcasted_iota(jnp.int32, (1, 128), 1)
    keys = k_ref.shape[1]
    queries = qw_ref.shape[1]
    width = stride * QB + keys
    for pr in range(pairs):
        lanes = slice(pr * 128, (pr + 1) * 128)
        k = k_ref[0, :, lanes]
        v = jnp.concatenate([v_ref[0, :, lanes], jnp.ones((keys, 128), BF)], axis=1)
        outs = []
        for h in range(2):
            content = mm_nt(qw_ref[0, :, lanes] * (masks[h] * SCALE).astype(BF), k)
            relative = mm_nt(qr_ref[0, :, lanes] * (masks[h] * SCALE).astype(BF), tab_ref[:, lanes])
            parts = []
            for b in range(queries // QB):
                rows = slice(b * QB, (b + 1) * QB)
                t0 = stride * (queries - QB - b * QB)
                rolled = pltpu.roll(
                    relative[rows, t0 : t0 + width], width - stride * (QB - 1), 1, stride=stride, stride_axis=0
                )
                scores = jnp.where(valid, content[rows] + rolled[:, :keys], MASKED)
                terms = jnp.exp(scores - jnp.max(scores, axis=-1, keepdims=True)).astype(BF)
                p_ref[0, 2 * pr + h, rows, :] = terms
                parts.append(terms)
            outs.append(mm(jnp.concatenate(parts, axis=0), v))
        inv = 1.0 / jnp.where(lane < HEAD_DIM, outs[0][:, 128:], outs[1][:, 128:])
        inv_ref[0, :, lanes] = inv
        mixed_ref[0, :, lanes] = (jnp.where(lane < HEAD_DIM, outs[0][:, :128], outs[1][:, :128]) * inv).astype(BF)


def attn_fwd(stride, lengths, key_mask, qw, qr, k, v, tab, far=False, cid=None, extra=None):
    s, queries, _ = qw.shape
    keys = k.shape[1]
    table = tab.shape[0]
    pairs = 2
    steps = HEADS // 2 // pairs
    kn = Kernel()
    block = lambda n: pl.BlockSpec((1, n, 128 * pairs), lambda i, j: (i, 0, j))
    h_len, h_mask = kn.inp(lengths, SM), kn.inp(key_mask, VM)
    handles = [
        kn.inp(qw, block(queries)),
        kn.inp(qr, block(queries)),
        kn.inp(k, block(keys)),
        kn.inp(v, block(keys)),
        kn.inp(tab, pl.BlockSpec((table, 128 * pairs), lambda i, j: (0, j))),
        kn.out((s, queries, D), BF, block(queries)),
        kn.out((s, queries, D), F32, block(queries)),
        kn.out((s, HEADS, queries, keys), BF, pl.BlockSpec((1, 2 * pairs, queries, keys), lambda i, j: (i, j, 0, 0))),
    ]
    if extra is not None and far:
        part = extra.shape[1]
        h_ex, h_full, r_sem, l_sem = kn.inp(extra), kn.out((s, 2 * part, D), BF), kn.sems(1, 2), kn.sems(1)

    def body(get):
        if extra is not None and far:
            side = lax.axis_index("seq")
            here = get(h_full).at[:, pl.ds(side * part, part)]
            copies = lambda: (
                remote(get(h_ex).at[pl.ds((1 - side) * s, s)], here, get(r_sem), 0, ALONG_Y),
                pltpu.make_async_copy(get(h_ex).at[pl.ds(side * s, s)], here, get(l_sem).at[0]),
            )
            first = jnp.logical_and(pl.program_id(0) == 0, pl.program_id(1) == 0)
            end = jnp.logical_and(pl.program_id(0) == s - 1, pl.program_id(1) == steps - 1)

            @pl.when(first)
            def _():
                greet([ALONG_Y])
                for copy in copies():
                    copy.start()

        own = lax.axis_index("seq") * s + pl.program_id(0)
        kept = get(h_mask)[pl.ds(own, 1), :]
        spots = lax.broadcasted_iota(jnp.int32, kept.shape, 1)
        valid = jnp.where((kept > 0) & (spots < get(h_len)[own]), 1.0, 0.0)
        if stride == 1:
            rows = jnp.broadcast_to(valid, (8, valid.shape[1])).astype(BF)
            valid = mm_nt(rows, pool_matrix(keys, valid.shape[1]))[0:1]
        attn_fwd_step(stride, pairs, valid > 0.0, *[get(h) for h in handles])
        if extra is not None and far:

            @pl.when(end)
            def _():
                for copy in copies():
                    copy.wait()

    return kn.run(
        body,
        "attn_fwd_%d" % stride,
        cost(2 * s * HEADS * queries * keys * 64 * 4, 12 * MIB, s * HEADS * queries * keys),
        grid=(s, steps),
        cid=cid if extra is not None and far else None,
    )


def ffn_fwd(mixed, resid, w_out, w_up, w_down, w_qkv, attn_bias, up_bias, gain, nbias, obias):
    rows = mixed.shape[0]
    kn = Kernel()
    h_mixed, h_resid = kn.inp(mixed, VM), kn.inp(resid, VM)
    h_wout, h_up, h_down, h_qkv = (kn.inp(x) for x in (w_out, w_up, w_down, w_qkv))
    h_ab, h_upb, h_gain, h_nb, h_ob = (kn.inp(x, VM) for x in (attn_bias, up_bias, gain, nbias, obias))
    wout, wup, wdown, wqkv = kn.mem((D, D)), kn.mem((D, FF)), kn.mem((FF, D)), kn.mem((3, D, D))
    shapes = {"hid": (D, BF), "x1": (D, F32), "r1": (128, F32), "act": (FF, BF), "slope": (FF, BF), "x2": (D, F32)}
    shapes.update({"r2": (128, F32), "out": (D, F32), "low": (D, BF), "qw": (D, BF), "qr": (D, BF), "k": (D, BF), "v": (D, BF)})
    order = list(shapes)
    outs = {n: (kn.out((rows, c), t), kn.mem((rows, c), t)) for n, (c, t) in shapes.items()}
    l_sem, o_sem = kn.sems(4), kn.sems(len(order))
    h_total = kn.mem((rows, D), F32)

    def body(get):
        mem = lambda n: get(outs[n][1])
        store = lambda n: pltpu.make_async_copy(mem(n), get(outs[n][0]), get(o_sem).at[order.index(n)])
        pairs = ((get(h_wout).at[0], wout), (get(h_up).at[0], wup), (get(h_down).at[0], wdown), (get(h_qkv).at[1], wqkv))
        loads = [pltpu.make_async_copy(src, get(dst), get(l_sem).at[i]) for i, (src, dst) in enumerate(pairs)]
        for copy in loads:
            copy.start()
        gain_ref, nb_ref, ob_ref, ab_ref = get(h_gain), get(h_nb), get(h_ob), get(h_ab)
        loads[0].wait()
        x1, r1 = ln_fwd(get(h_resid)[...] + (mm(get(h_mixed)[...], get(wout)[...]) + ob_ref[0, 0:1, :]))
        mem("x1")[...] = x1
        mem("r1")[...] = jnp.broadcast_to(r1, (rows, 128))
        hidden = x1 * gain_ref[0, 0:1, :] + nb_ref[0, 0:1, :]
        mem("hid")[...] = hidden.astype(BF)
        for n in ("x1", "r1", "hid"):
            store(n).start()
        total = get(h_total)
        total[...] = hidden + ob_ref[0, 1:2, :]
        loads[1].wait()
        for c in range(0, PANELS, WIDE):
            cols = slice(c * D, (c + WIDE) * D)
            act, slope = gelu_and_slope(mm(mem("hid")[...], get(wup)[:, cols]) + get(h_upb)[0:1, cols])
            act = act.astype(BF)
            mem("act")[:, cols] = act
            mem("slope")[:, cols] = slope.astype(BF)
            if c == 0:
                loads[2].wait()
            total[...] += mm(act, get(wdown)[cols, :])
        store("act").start()
        store("slope").start()
        x2, r2 = ln_fwd(total[...])
        mem("x2")[...] = x2
        mem("r2")[...] = jnp.broadcast_to(r2, (rows, 128))
        out = x2 * gain_ref[0, 1:2, :] + nb_ref[0, 1:2, :]
        mem("out")[...] = out
        low = out.astype(BF)
        mem("low")[...] = low
        for n in ("x2", "r2", "out", "low"):
            store(n).start()
        loads[3].wait()
        q = mm(low, get(wqkv)[0])
        mem("qw")[...] = (q + ab_ref[1, 0:1, :]).astype(BF)
        mem("qr")[...] = (q + ab_ref[1, 1:2, :]).astype(BF)
        store("qw").start()
        store("qr").start()
        mem("k")[...] = mm(low, get(wqkv)[1]).astype(BF)
        store("k").start()
        mem("v")[...] = mm(low, get(wqkv)[2]).astype(BF)
        store("v").start()
        for n in order:
            store(n).wait()

    return kn.run(body, "ffn_fwd", cost(2 * rows * D * D * 12, 34 * MIB, rows * FF), limit=60)


def places(order, rows_each, far):
    me = lax.axis_index("rows") if far else 0
    side = lax.axis_index("seq") if far else 0
    base = {}
    for r in range(SHARDS):
        for half in range(2):
            spot = 0
            for axis, b in bits_of(order):
                c = half if axis == "seq" else (r // b) % 2
                mine = side if axis == "seq" else me
                spot = spot * 2 + (lax.rem(bit(mine, b) + c, 2) if far else c)
            base[r, half] = spot * rows_each
    return base


def put(buf_ref, mat, base, tile, shards, rows, first=0, pitch=None):
    low = tile.astype(BF)
    width = buf_ref.shape[2]
    for n, r in enumerate(shards):
        for half in range(2):
            start = base[r, half]
            if not isinstance(start, int):
                start = pl.multiple_of(start, 16)
            top = n * pitch + first
            buf_ref[mat, pl.ds(start, rows), :] = low[top : top + rows, half * width : (half + 1) * width]


NA = SHARDS * ROW
BORN_ORDERS = (XY, XY, XY)
SWAP_POINT = 1
BORN_POINTS = ({1: 11}, {})
SMALL_STEPS = (
    (CORE,),
    (ALONG_X, ALONG_Y, (ALONG_X, ALONG_Y)),
    (Z_NEAR, Z_FAR, Z_DIAG),
)
UP_AT = ((0, 0), (0, 1), (0, 2), (1, 0))
DOWN_AT = ((1, 1), (1, 2), (2, 0), (2, 1))
OUT_AT = (2, 2)
FFN_ORDERS = (XZY, YX, ZYX)
FFN_MATS = (3, 3, 3)
ATT_ORDERS = ((XY, YX), (XZY, YX))


class FfnGrads:
    def __init__(self, kn, far, rows):
        full = lambda shape: pl.BlockSpec(shape, lambda *g: (0,) * len(shape))
        self.dmixed = kn.out((rows, D), BF, full((rows, D)))
        self.dbranch = kn.out((rows, D), BF, full((rows, D)))
        self.dres = kn.out((rows, D), F32, full((rows, D)))
        self.small = kn.out((8, D), F32, full((8, D)))
        self.upg = kn.out((8, FF), F32, full((8, FF)))
        self.groups = [Group(kn, far, order, mats, ROW) for order, mats in zip(FFN_ORDERS, FFN_MATS)]
        self.wup, self.wdown = kn.mem((D, FF)), kn.mem((FF, D))
        self.act, self.slope = kn.mem((rows, FF)), kn.mem((rows, FF))
        self.dffn, self.dhid = kn.mem((rows, D)), kn.mem((rows, D), F32)
        self.near = kn.sems(4)

    def run(self, get, dy, x2, r2, gain2, gain1, wout_ref, hid_ref, mixed_ref, x1, r1, at):
        small_ref, upg_ref, dffn_ref, dhid_ref = get(self.small), get(self.upg), get(self.dffn), get(self.dhid)
        act, slope, wup, wdown = get(self.act), get(self.slope), get(self.wup), get(self.wdown)
        for group in self.groups:
            group.bind(get)
            group.locate()
        small_ref[...] = jnp.zeros_like(small_ref)
        dpost = ln_bwd(dy, x2, r2, gain2)
        small_ref[1:2, :] = jnp.sum(dy * x2, axis=0, keepdims=True)
        small_ref[3:4, :] = jnp.sum(dy, axis=0, keepdims=True)
        dffn = dpost.astype(BF)
        small_ref[5:6, :] = jnp.sum(dffn.astype(F32), axis=0, keepdims=True)
        dffn_ref[...] = dffn
        dhid_ref[...] = dpost
        at(0)
        each = SHARDS // PANELS
        groups = self.groups
        for w in range(0, PANELS, WIDE):
            ddown = mm_tn(act[:, w * D : (w + WIDE) * D], dffn_ref[...])
            shards = range(w * each, (w + WIDE) * each)
            for i, (group, mat) in enumerate(DOWN_AT):
                groups[group].put(mat, ddown, shards, i * ROW, UP_ROWS)
        for group, mat in DOWN_AT:
            groups[group].leave(mat)
        for w in range(0, PANELS, WIDE):
            cols = slice(w * D, (w + WIDE) * D)
            dact = mm_nt(dffn_ref[...], wdown[cols, :])
            dpre = (dact * slope[:, cols].astype(F32)).astype(BF)
            upg_ref[:, cols] = jnp.broadcast_to(jnp.sum(dpre.astype(F32), axis=0, keepdims=True), (8, WIDE * D))
            dup = mm_tn(hid_ref[...], dpre)
            for i in range(WIDE):
                group, mat = UP_AT[w + i]
                groups[group].put(mat, dup[:, i * D : (i + 1) * D], range(SHARDS))
                groups[group].leave(mat)
            dhid_ref[...] += mm_nt(dpre, wup[:, cols])
            at(w // WIDE + 1)
        for group, mat in DOWN_AT + UP_AT[:WIDE]:
            groups[group].settle(mat)
        dhid = dhid_ref[...]
        xh = x1()
        small_ref[0:1, :] = jnp.sum(dhid * xh, axis=0, keepdims=True)
        small_ref[2:3, :] = jnp.sum(dhid, axis=0, keepdims=True)
        dres = ln_bwd(dhid, xh, r1(), gain1)
        get(self.dres)[...] = dres
        dbranch = dres.astype(BF)
        get(self.dbranch)[...] = dbranch
        small_ref[4:5, :] = jnp.sum(dbranch.astype(F32), axis=0, keepdims=True)
        group, mat = OUT_AT
        groups[group].put(mat, mm_tn(mixed_ref[...], dbranch), range(SHARDS))
        groups[group].leave(mat)
        get(self.dmixed)[...] = mm_nt(dbranch, wout_ref[0]).astype(BF)
        for group, mat in UP_AT[WIDE:] + (OUT_AT,):
            groups[group].settle(mat)
        for group in groups:
            group.end()

    def results(self, res):
        own = [res[h[1]] for h in (self.dmixed, self.dbranch, self.dres, self.small, self.upg)]
        return own, [group.result(res) for group in self.groups]


def ffn_last(far, cid, mixed, resid, cot, w_out, w_up, w_down, up_bias, gain, nbias, obias):
    rows = mixed.shape[0]
    kn = Kernel()
    whole = pl.BlockSpec((rows, D), lambda i: (0, 0))
    layer = pl.BlockSpec((1, 2, D), lambda i: (1, 0, 0))
    h_mixed, h_resid, h_cot = (kn.inp(x, whole) for x in (mixed, resid, cot))
    h_wout = kn.inp(w_out, pl.BlockSpec((1, D, D), lambda i: (1, 0, 0)))
    h_up, h_down = kn.inp(w_up), kn.inp(w_down)
    h_upb = kn.inp(up_bias, pl.BlockSpec((2, FF), lambda i: (0, 0)))
    h_gain, h_nbias, h_obias = (kn.inp(x, layer) for x in (gain, nbias, obias))
    h_lout = kn.out((rows, D), BF, whole)
    grads = FfnGrads(kn, far, rows)
    h_hid, h_x1 = kn.mem((rows, D)), kn.mem((rows, D), F32)

    def body(get):
        if far:
            greet([CORE])
        near = get(grads.near)
        wup, wdown, act, slope, hid, x1s = (
            get(h) for h in (grads.wup, grads.wdown, grads.act, grads.slope, h_hid, h_x1)
        )
        dhid_s = get(grads.dhid)
        gain_ref, nbias_ref, obias_ref, upb_ref, wout_ref = (
            get(h) for h in (h_gain, h_nbias, h_obias, h_upb, h_wout)
        )
        cp_up = pltpu.make_async_copy(get(h_up).at[1], wup, near.at[0])
        cp_down = pltpu.make_async_copy(get(h_down).at[1], wdown, near.at[1])
        cp_up.start()
        cp_down.start()
        pre_norm = get(h_resid)[...] + (mm(get(h_mixed)[...], wout_ref[0]) + obias_ref[0, 0:1, :])
        x1, r1 = ln_fwd(pre_norm)
        x1s[...] = x1
        hidden = x1 * gain_ref[0, 0:1, :] + nbias_ref[0, 0:1, :]
        hid[...] = hidden.astype(BF)
        dhid_s[...] = hidden + obias_ref[0, 1:2, :]
        cp_up.wait()
        cp_down.wait()
        for c in range(0, PANELS, WIDE):
            cols = slice(c * D, (c + WIDE) * D)
            a, s = gelu_and_slope(mm(hid[...], wup[:, cols]) + upb_ref[1:2, cols])
            a = a.astype(BF)
            act[:, cols] = a
            slope[:, cols] = s.astype(BF)
            dhid_s[...] += mm(a, wdown[cols, :])
        x2, r2 = ln_fwd(dhid_s[...])
        get(h_lout)[...] = (x2 * gain_ref[0, 1:2, :] + nbias_ref[0, 1:2, :]).astype(BF)
        grads.run(
            get, get(h_cot)[...].astype(F32), x2, r2, gain_ref[0, 1:2, :], gain_ref[0, 0:1, :], wout_ref, hid,
            get(h_mixed), lambda: x1s[...], lambda: r1, lambda point: None,
        )

    res = kn.run(
        body, "ffn_last", cost(2 * rows * D * D * 26, 30 * MIB, rows * FF), grid=(1,), cid=cid if far else None, limit=63
    )
    return res[h_lout[1]], *grads.results(res)


def ffn_bwd(far, cid, chains, dy, x2, r2, hid, mixed, x1, r1, gain, w_out, w_up, w_down, act, slope):
    rows = hid.shape[0]
    kn = Kernel()
    whole = pl.BlockSpec((rows, D), lambda i: (0, 0))
    thin = pl.BlockSpec((rows, 128), lambda i: (0, 0))
    h_dy, h_x2, h_hid, h_mixed, h_x1 = (kn.inp(x, whole) for x in (dy, x2, hid, mixed, x1))
    h_r2, h_r1 = (kn.inp(x, thin) for x in (r2, r1))
    h_gain = kn.inp(gain, pl.BlockSpec((1, 2, D), lambda i: (0, 0, 0)))
    h_wout = kn.inp(w_out, pl.BlockSpec((1, D, D), lambda i: (0, 0, 0)))
    h_up, h_down, h_act, h_slope = (kn.inp(x) for x in (w_up, w_down, act, slope))
    grads = FfnGrads(kn, far, rows)
    links = [Chain(kn, *c[:3]) for c in chains]
    def body(get):
        near = get(grads.near)
        if far:
            greet([CORE, ALONG_X, ALONG_Y, Z_ALL])
        for link in links:
            link.bind(get)
            link.go(0)
        loads = [
            pltpu.make_async_copy(get(h_act), get(grads.act), near.at[0]),
            pltpu.make_async_copy(get(h_down).at[0], get(grads.wdown), near.at[1]),
            pltpu.make_async_copy(get(h_slope), get(grads.slope), near.at[2]),
            pltpu.make_async_copy(get(h_up).at[0], get(grads.wup), near.at[3]),
        ]
        for copy in loads:
            copy.start()

        def at(point):
            if point == 0:
                for copy in loads:
                    copy.wait()
            for link, (_, _, _, when) in zip(links, chains):
                if point in when:
                    link.go(when[point])

        gain_ref = get(h_gain)
        grads.run(
            get, get(h_dy)[...], get(h_x2)[...], get(h_r2)[:, 0:1], gain_ref[0, 1:2, :], gain_ref[0, 0:1, :],
            get(h_wout), get(h_hid), get(h_mixed), lambda: get(h_x1)[...], lambda: get(h_r1)[:, 0:1], at,
        )
        for link, (_, _, close, _) in zip(links, chains):
            if not close:
                link.go(link.j)
        for link in links:
            link.end()

    res = kn.run(
        body, "ffn_bwd", cost(2 * rows * D * D * 18, 40 * MIB), grid=(1,), cid=cid if far else None, limit=63
    )
    return *grads.results(res), [link.result(res) for link in links]


def attn_bwd_step(
    stride, seq, lanes, p_ref, inv_ref, qw_ref, qr_ref, k_ref, v_ref, tab_ref, dm_ref, dq, dk_out, dv_out, dtab, dbias
):
    masks = head_masks()
    lane = lax.broadcasted_iota(jnp.int32, (1, 128), 1)
    first = lane < HEAD_DIM
    keys = k_ref.shape[1]
    queries = qw_ref.shape[1]
    blocks = queries // QB
    width = stride * QB + keys
    flip_i = lax.broadcasted_iota(jnp.int32, (queries, queries), 0)
    flip_j = lax.broadcasted_iota(jnp.int32, (queries, queries), 1)
    flip = jnp.where(flip_i + flip_j == queries - 1, 1.0, 0.0).astype(BF)

    @pl.when(seq == 0)
    def _():
        dtab[:, lanes] = jnp.zeros((dtab.shape[0], 128), F32)
        dbias[:, lanes] = jnp.zeros((dbias.shape[0], 128), F32)

    k = k_ref[0]
    v = v_ref[0]
    inv = inv_ref[0]
    scaled = (dm_ref[0].astype(F32) * inv).astype(BF)
    qr_rev = mm(flip, qr_ref[0]).astype(BF)
    dk = jnp.zeros((keys, 128), F32)
    dv = jnp.zeros((keys, 128), F32)
    dqws, dqrs = [], []
    for h in range(2):
        dmh = scaled * masks[h]
        terms = p_ref[0, h]
        dprob = mm_nt(dmh, v)
        wide = terms.astype(F32)
        inner = jnp.sum(dprob * wide, axis=-1, keepdims=True) * inv[:, h * HEAD_DIM : h * HEAD_DIM + 1]
        ds = (wide * (dprob - inner)).astype(BF)
        dv = dv + mm_tn(terms, dmh)
        dk = dk + mm_tn(ds, qw_ref[0] * masks[h])
        dqws.append(mm(ds, k))
        rev = mm(flip, ds)
        back = []
        for b in range(blocks):
            rows = slice(b * QB, (b + 1) * QB)
            t0 = stride * b * QB
            padded = jnp.concatenate([rev[rows], jnp.zeros((QB, width - keys), F32)], axis=1)
            rel = pltpu.roll(padded, 0, 1, stride=stride, stride_axis=0).astype(BF)
            dtab[t0 : t0 + width, lanes] += mm_tn(rel, qr_rev[rows] * masks[h]) * SCALE
            back.append(mm(rel, tab_ref[t0 : t0 + width, :]))
        dqrs.append(jnp.concatenate(back, axis=0))
    dqw = jnp.where(first, dqws[0], dqws[1]) * SCALE
    hi, lo = split_hi_lo(jnp.where(first, dqrs[0], dqrs[1]))
    dqr = (mm(flip, hi) + mm(flip, lo)) * SCALE
    dq[pl.ds(pl.multiple_of(seq * queries, QB), queries), lanes] = (dqw + dqr).astype(BF)
    at = pl.ds(pl.multiple_of(seq * keys, QB), keys)
    dk_out[at, lanes] = (dk * SCALE).astype(BF)
    dv_out[at, lanes] = dv.astype(BF)
    dbias[0:1, lanes] += jnp.sum(dqw, axis=0, keepdims=True)
    dbias[1:2, lanes] += jnp.sum(dqr, axis=0, keepdims=True)


def back_layer(
    far, cid, layer, plan, p, inv, qw, qr, k, v, tab, dmixed, dres, w_qkv, xq, xk, enc, smalls=None, lout=None
):
    s, queries, _ = qw.shape
    keys = k.shape[1]
    table = tab.shape[0]
    last = s * (HEADS // 2)
    nq, nk = s * queries, s * keys
    tail = smalls is not None
    kn = Kernel()
    seq_of = lambda g: lax.rem(jnp.minimum(g, last - 1), s)
    pair_of = lambda g: lax.div(jnp.minimum(g, last - 1), s)
    pair_block = lambda n: pl.BlockSpec((1, n, 128), lambda g: (seq_of(g), 0, pair_of(g)))
    h_p = kn.inp(p, pl.BlockSpec((1, 2, queries, keys), lambda g: (seq_of(g), pair_of(g), 0, 0)))
    h_inv, h_qw, h_qr, h_dm = (kn.inp(x, pair_block(queries)) for x in (inv, qw, qr, dmixed))
    h_k, h_v = (kn.inp(x, pair_block(keys)) for x in (k, v))
    h_tab = kn.inp(tab, pl.BlockSpec((table, 128), lambda g: (0, pair_of(g))))
    dq_s, dk_s, dv_s = kn.mem((nq, D)), kn.mem((nk, D)), kn.mem((nk, D))
    dtab_s, dbias_s = kn.mem((table, D), F32), kn.mem((8, D), F32)
    late = [(dres, F32), (xq, BF), (enc, BF)]
    if layer == 0 or xk is not xq:
        late.append((xk, BF))
    late_in = [kn.inp(x) for x, _ in late]
    late_mem = [kn.mem(x.shape, t) for x, t in late]
    h_w, h_wm = kn.inp(w_qkv), kn.mem((3, D, D))
    l_sem = kn.sems(len(late) + 1)
    chains = [Chain(kn, so_far, steps, close) for so_far, steps, close, _ in plan]
    whole = lambda shape: pl.BlockSpec(shape, lambda g: (0,) * len(shape))
    half = keys // 2
    born, groups = [], []
    if tail and far:
        for order in BORN_ORDERS:
            born.append(Chain(kn, None, order[1:], True, (kn.mem((4, 2 * NA, BLOCK)), 4, NA, BLOCK)))
    else:
        groups = [Group(kn, far, order, 2 * BLOCKS, ROW, BLOCK) for order in ATT_ORDERS[layer]]
    if tail and far:
        h_small = [kn.inp(x, whole(x.shape)) for x in smalls]
        sum_shape = (2 * SMALL_ROWS, D)
        h_sum = kn.out(sum_shape, F32, whole(sum_shape))
        sm = [kn.mem(sum_shape, F32) for _ in range(len(SMALL_STEPS))]
        sm_in = [kn.mem(sum_shape, F32) for step in SMALL_STEPS for _ in step]
        sm_sem = kn.sems(len(sm_in), 2)
        h_dx = kn.out((s, half, D), F32, whole((s, half, D)))
        h_piece, h_got, h_swap = kn.mem((s, half, D)), kn.out((s, half, D), BF), kn.sems(s, 2)
    else:
        h_dx = kn.out((nk, D), F32, whole((nk, D)))
        h_bias = kn.out((8, D), F32, whole((8, D)))
    swaps = lout is not None and far
    if swaps:
        h_lout, h_lgot, l_swap = kn.inp(lout), kn.out((s, queries // 2, D), BF), kn.sems(1, 2)
    greeted = [step for _, steps, _, _ in plan for step in steps] + [CORE]
    if tail:
        greeted = [CORE, ALONG_X, ALONG_Y, (ALONG_X, ALONG_Y), Z_ALL]

    def body(get):
        g = pl.program_id(0)
        dq, dk, dv, dtab, dbias = (get(h) for h in (dq_s, dk_s, dv_s, dtab_s, dbias_s))
        loads = [pltpu.make_async_copy(get(a), get(b), get(l_sem).at[i]) for i, (a, b) in enumerate(zip(late_in, late_mem))]
        loads.append(pltpu.make_async_copy(get(h_w).at[layer], get(h_wm), get(l_sem).at[len(late)]))
        for chain in chains + born:
            chain.bind(get)

        @pl.when(g == 0)
        def _():
            if far:
                greet(greeted)
            for copy in loads:
                copy.start()

        @pl.when(g < last)
        def _():
            lanes = pl.ds(pl.multiple_of(pair_of(g) * 128, 128), 128)
            attn_bwd_step(
                2 - layer, seq_of(g), lanes, get(h_p), get(h_inv), get(h_qw), get(h_qr), get(h_k), get(h_v), get(h_tab), get(h_dm),
                dq, dk, dv, dtab, dbias,
            )

        for point in range(last):
            acts = [(c, k) for c, (_, _, _, when) in zip(chains, plan) for k, w in when.items() if w == point]
            if acts:

                @pl.when(g == point)
                def _():
                    for chain, k in acts:
                        chain.go(k)

        def swap_lout():
            other = 1 - lax.axis_index("seq")
            half_of = get(h_lout).at[:, pl.ds(other * (queries // 2), queries // 2)]
            return remote(half_of, get(h_lgot), get(l_swap), 0, ALONG_Y)

        if swaps:

            @pl.when(g == SWAP_POINT)
            def _():
                swap_lout().start()

        dres_ref, xq_ref, enc_ref = (get(h) for h in late_mem[:3])
        xk_ref = get(late_mem[3]) if layer == 0 or xk is not xq else xq_ref
        for group in groups:
            group.bind(get)
        per = last // BLOCKS

        def swap_piece(i):
            return remote(get(h_piece).at[i], get(h_got).at[i], get(h_swap), i, ALONG_Y)

        def make(t):
            cols = slice(2 * t * BLOCK, 2 * (t + 1) * BLOCK)
            return (
                (1, 0, lambda: mm_tn(xk_ref[...], dv[:, cols])),
                (0, 0, lambda: mm_tn(xq_ref[...], dq[:, cols])),
                (1, 1, lambda: mm_tn(enc_ref[...], dtab[:, cols].astype(BF))),
                (0, 1, lambda: mm_tn(xk_ref[...], dk[:, cols])),
            )

        def gradients(t):
            for group in groups:
                group.locate()
            base = places(BORN_ORDERS[t], ROW, far) if tail and far else None
            for which, mat, tile in make(t):
                if tail and far:
                    put(get(born[t].total), 2 * which + mat, base, tile(), range(SHARDS), ROW, 0, ROW)
                else:
                    groups[which].put(2 * t + mat, tile(), range(SHARDS))
                    groups[which].leave(2 * t + mat)
            if tail and far:
                born[t].core().start()

        def settled(t):
            if tail and far:
                born[t].first()
                return
            for which, mat, _ in make(t):
                groups[which].settle(2 * t + mat)

        for t in range(BLOCKS):

            @pl.when(g == (t + 1) * per - 1)
            def _():
                if t == 0:
                    for copy in loads:
                        copy.wait()
                gradients(t)

            if t < BLOCKS - 1:

                @pl.when(g == (t + 1) * per)
                def _():
                    settled(t)

                for chain in born[t : t + 1]:
                    for k, point in BORN_POINTS[t].items():

                        @pl.when(g == point)
                        def _():
                            chain.go(k)

        @pl.when(g == last)
        def _():
            w = get(h_wm)
            dx_ref = get(h_dx)

            def at(point):
                for chain, (_, _, _, when) in zip(chains, plan):
                    for step, due in when.items():
                        if due == point:
                            chain.go(step)

            if tail and far:
                small_start(get, dbias)
            settled(BLOCKS - 1)
            if tail and far:
                small_round(get, 0)
            at(last)
            if layer == 1:
                dx_ref[...] = dres_ref[...] + (mm_nt(dq[...], w[0]) + mm_nt(dk[...], w[1]) + mm_nt(dv[...], w[2]))
            else:
                spread = pool_matrix_t(keys, queries)
                side = lax.axis_index("seq") if far else 0
                for i in range(s):
                    q_at, k_at = slice(i * queries, (i + 1) * queries), slice(i * keys, (i + 1) * keys)
                    hi, lo = split_hi_lo(dres_ref[q_at, :] + mm_nt(dq[q_at, :], w[0]))
                    dtok = mm_nt(dk[k_at, :], w[1]) + mm_nt(dv[k_at, :], w[2]) + (mm(spread, hi) + mm(spread, lo))
                    if tail and far:
                        low_half, high_half = dtok[:half], dtok[half:]
                        is_low = side == 0
                        dx_ref[i] = jnp.where(is_low, low_half, high_half)
                        get(h_piece)[i] = jnp.where(is_low, high_half, low_half).astype(BF)
                        if i < s - 1:
                            swap_piece(i).start()
                    else:
                        dx_ref[k_at, :] = dtok
            at(last + 1)
            if tail and far:
                finish_tail(get, swap_piece)
                return
            get(h_bias)[...] = dbias[...]
            for chain in chains:
                chain.go(chain.j)
            for group in groups:
                group.end()
            for chain in chains:
                chain.end()
            if swaps:
                swap_lout().wait()

    def small_copies(get, k):
        top = sum(len(step) for step in SMALL_STEPS[:k])
        came = [get(h) for h in sm_in]
        return [
            (came[top + i], remote(get(sm[k]), came[top + i], get(sm_sem), top + i, one))
            for i, one in enumerate(SMALL_STEPS[k])
        ]

    def small_start(get, dbias):
        own = get(sm[0])
        small0, upg0, small1, upg1, bias1 = (get(h) for h in h_small)
        for top, small, upg, bias in ((0, small0, upg0, dbias), (SMALL_ROWS, small1, upg1, bias1)):
            own[top : top + 6, :] = small[0:6, :]
            own[top + 6 : top + 8, :] = bias[0:2, :]
            for p in range(PANELS):
                own[top + 8 + p : top + 9 + p, :] = upg[0:1, p * D : (p + 1) * D]
        for _, copy in small_copies(get, 0):
            copy.start()

    def small_round(get, k):
        pieces = small_copies(get, k)
        for _, copy in pieces:
            copy.wait()
        own = get(sm[k])
        dst = get(sm[k + 1]) if k + 1 < len(SMALL_STEPS) else get(h_sum)
        if len(pieces) == 1:
            dst[...] = own[...] + pieces[0][0][...]
        else:
            a, b, c = (ref[...] for ref, _ in pieces)
            dst[...] = (own[...] + a) + (b + c)
        if k + 1 < len(SMALL_STEPS):
            for _, copy in small_copies(get, k + 1):
                copy.start()

    def finish_tail(get, swap_piece):
        pending = {c: max(when) + 1 for c, (_, _, _, when) in zip(chains, plan)}
        for t, chain in enumerate(born):
            pending[chain] = max([0, *BORN_POINTS[t]]) + 1 if t < BLOCKS - 1 else 1
        order = [chains[1], born[0], born[1], chains[0], chains[2], born[2], *chains[3:]]
        for r in range(5):
            for chain in order:
                k = pending[chain]
                if k <= chain.j:
                    chain.go(k)
                    pending[chain] = k + 1
            if r == 0:
                swap_piece(s - 1).start()
            if r + 1 < len(SMALL_STEPS):
                small_round(get, r + 1)
        for chain in order:
            chain.end()
        for i in range(s):
            swap_piece(i).wait()

    flops = 2 * s * HEADS * queries * keys * 64 * 9 + 2 * D * D * (4 * nq + 4 * nk + table)
    res = kn.run(
        body, "back_layer_%d" % layer, cost(flops, 40 * MIB), grid=(last + 1,), cid=cid if far else None, limit=62
    )
    moved = [chain.result(res) for chain in chains]
    if tail and far:
        return res[h_dx[1]], res[h_got[1]], res[h_sum[1]], moved, [chain.result(res) for chain in born]
    got = res[h_lgot[1]] if swaps else None
    return res[h_dx[1]], res[h_bias[1]], moved, [group.result(res) for group in groups], got


def steps_of(distances):
    half_width = D // 2
    frequency = 10000.0 ** (-jnp.arange(half_width, dtype=F32) / half_width)
    angles = distances.astype(F32)[:, None] * frequency[None, :]
    return jnp.stack([jnp.sin(angles), jnp.cos(angles)])


FINE = 32


def prologue(far, cid, tokens, w_qkv, w_pos, attn_bias):
    parts = 2 if far else 1
    s, part_len = tokens.shape[0] // parts, tokens.shape[1]
    length = part_len * parts
    queries = length // 2
    table = 2 * length
    coarse = steps_of(2 * (queries - 1) - FINE * jnp.arange(table // FINE, dtype=jnp.int32))
    fine = steps_of(-jnp.arange(FINE, dtype=jnp.int32))
    fine2 = steps_of(-2 * jnp.arange(FINE // 2, dtype=jnp.int32))
    kn = Kernel()
    h_tok, h_w, h_wp = (kn.inp(x) for x in (tokens, w_qkv, w_pos))
    h_coarse, h_fine, h_fine2, h_bias = (kn.inp(x, VM) for x in (coarse, fine, fine2, attn_bias))
    names = {}

    def result(name, shape, dtype=BF):
        names[name] = (kn.out(shape, dtype), kn.mem(shape, dtype))

    result("tok", (s, length, D))
    result("enc0", (table, D))
    result("enc1", (table // 2, D))
    result("tab0", (table, D))
    result("tab1", (table // 2, D))
    result("pooled", (s * queries, D), F32)
    for name in ("low", "qw", "qr"):
        result(name, (s * queries, D))
    for name in ("k", "v"):
        result(name, (s, length, D))
    h_wm, h_wpm = kn.mem((3, D, D)), kn.mem((2, D, D))
    o_sem, l_sem, r_sem = kn.sems(len(names)), kn.sems(3), kn.sems(s, 2)
    order = list(names)

    def body(get):
        mem = lambda name: get(names[name][1])

        def store(name):
            return pltpu.make_async_copy(mem(name), get(names[name][0]), get(o_sem).at[order.index(name)])

        ls = get(l_sem)
        tok = mem("tok")
        if far:
            side = lax.axis_index("seq")
            mine = pl.ds(side * s, s)
            greet([ALONG_Y])
            here = pl.ds(side * part_len, part_len)
            sends = [
                remote(get(h_tok).at[pl.ds((1 - side) * s + i, 1)], tok.at[pl.ds(i, 1), here], get(r_sem), i, ALONG_Y)
                for i in range(s)
            ]
            loads = [pltpu.make_async_copy(get(h_tok).at[mine], tok.at[:, here], ls.at[0])]
        else:
            sends = []
            loads = [pltpu.make_async_copy(get(h_tok), tok, ls.at[0])]
        loads += [
            pltpu.make_async_copy(get(h_wp), get(h_wpm), ls.at[1]),
            pltpu.make_async_copy(get(h_w).at[0], get(h_wm), ls.at[2]),
        ]
        for copy in sends + loads:
            copy.start()
        w = get(h_wm)

        def encode(dst, table_rows, fine_ref):
            n = fine_ref.shape[1]
            fs, fc = fine_ref[0], fine_ref[1]
            for a in range(table_rows // n):
                cs, cc = get(h_coarse)[0, a : a + 1, :], get(h_coarse)[1, a : a + 1, :]
                dst[a * n : (a + 1) * n, :HALF] = (cs * fc + cc * fs).astype(BF)
                dst[a * n : (a + 1) * n, HALF:] = (cc * fc - cs * fs).astype(BF)

        encode(mem("enc0"), table, get(h_fine))
        store("enc0").start()
        encode(mem("enc1"), table // 2, get(h_fine2))
        store("enc1").start()
        loads[1].wait()
        wp = get(h_wpm)
        mem("tab0")[...] = mm(mem("enc0")[...], wp[0]).astype(BF)
        store("tab0").start()
        mem("tab1")[...] = mm(mem("enc1")[...], wp[1]).astype(BF)
        store("tab1").start()
        for i in (0, 2):
            loads[i].wait()

        def keys_of(i, part):
            x = tok[i, part, :]
            mem("k")[i, part, :] = mm(x, w[1]).astype(BF)
            mem("v")[i, part, :] = mm(x, w[2]).astype(BF)

        if far:
            for i in range(s):
                keys_of(i, pl.ds(pl.multiple_of(side * part_len, part_len), part_len))
        gather = pool_matrix(queries, length)
        for i in range(s):
            if far:
                sends[i].wait()
                keys_of(i, pl.ds(pl.multiple_of((1 - side) * part_len, part_len), part_len))
            else:
                keys_of(i, pl.ds(0, length))
            at = slice(i * queries, (i + 1) * queries)
            pooled = mm(gather, tok[i])
            mem("pooled")[at, :] = pooled
            low = pooled.astype(BF)
            mem("low")[at, :] = low
            q = mm(low, w[0])
            mem("qw")[at, :] = (q + get(h_bias)[0, 0:1, :]).astype(BF)
            mem("qr")[at, :] = (q + get(h_bias)[0, 1:2, :]).astype(BF)
        for name in ("tok", "k", "v"):
            store(name).start()
        for name in ("pooled", "low", "qw", "qr"):
            store(name).start()
        for name in order:
            store(name).wait()

    res = kn.run(
        body, "prologue", cost(2 * D * D * (3 * s * length + 2 * table), 30 * MIB), cid=cid if far else None
    )
    found = {name: res[h[0][1]] for name, h in names.items()}
    return found


def finish(done, sums, dtok, got, lout, lout_got):
    s, half, _ = dtok.shape
    q = lout_got.shape[1]
    names = ["b00", "b01", "b02", "g00", "g10", "g20", "qk1", "vp1", "g01", "g11", "g21"]
    kn = Kernel()
    hs = {n: (kn.inp(m, VM), kn.inp(o, VM)) for n, (m, o) in zip(names, done)}
    h_sum, h_dtok, h_got, h_lgot = (kn.inp(x, VM) for x in (sums, dtok, got, lout_got))
    h_lout = kn.inp(lout)
    o_lout = kn.out((2 * s, q, D), BF, VM)
    o_tok = kn.out((2 * s, half, D), F32, VM)
    o_qkv = kn.out((2, 3, ROW, D), F32, VM)
    o_out, o_pos = (kn.out((2, ROW, D), F32, VM) for _ in range(2))
    o_up = kn.out((2, ROW, FF), F32, VM)
    o_down = kn.out((2, UP_ROWS, D), F32, VM)
    o_attn = kn.out((2, 2, ROW), F32, VM)
    o_upb = kn.out((2, FF // SHARDS), F32, VM)
    o_gain, o_nb, o_ob = (kn.out((2, 2, ROW), F32, VM) for _ in range(3))
    h_lmem, h_sem = kn.mem((s, q, D)), kn.sems(1)

    def body(get):
        side, me = lax.axis_index("seq"), lax.axis_index("rows")
        copy = pltpu.make_async_copy(
            get(h_lout).at[:, pl.ds(pl.multiple_of(side * q, q), q)], get(h_lmem), get(h_sem).at[0]
        )
        copy.start()
        mine, other = pl.ds(side * s, s), pl.ds((1 - side) * s, s)
        get(o_tok)[mine] = get(h_dtok)[...]
        get(o_tok)[other] = get(h_got)[...].astype(F32)
        get(o_lout)[other] = get(h_lgot)[...]

        def halves(name, mat, dst, lead, base=0, rows=slice(None)):
            for h, which in zip(hs[name], (side, 1 - side)):
                width = get(h).shape[2]
                lanes = pl.ds(pl.multiple_of(base + which * width, 128), width)
                dst[(*lead, rows, lanes)] = get(h)[mat].astype(F32)

        for l in range(2):
            ffn = lambda at: ("g%d%d" % (at[0], l), at[1])
            for t in range(BLOCKS):
                for i, dst, lead in ((0, o_qkv, (l, 0)), (1, o_qkv, (l, 1)), (2, o_qkv, (l, 2)), (3, o_pos, (l,))):
                    name, mat = ("b0%d" % t, i) if l == 0 else (("qk1", "vp1")[i // 2], 2 * t + i % 2)
                    halves(name, mat, get(dst), lead, 2 * t * BLOCK)
            halves(*ffn(OUT_AT), get(o_out), (l,))
            for p in range(PANELS):
                halves(*ffn(UP_AT[p]), get(o_up), (l,), p * D)
                halves(*ffn(DOWN_AT[p]), get(o_down), (l,), rows=slice(p * ROW, (p + 1) * ROW))
        both = get(h_sum)[...]
        turned = pltpu.roll(both, lax.rem(D - me * ROW, D), 1)
        for l in range(2):
            r = 12 * l
            for o, row in ((o_gain, 0), (o_nb, 2), (o_ob, 4), (o_attn, 6)):
                get(o)[l] = turned[r + row : r + row + 2, :ROW]
        wide = FF // SHARDS
        per = D // wide
        shifted = pltpu.roll(both, lax.rem(D - lax.rem(me, per) * wide, D), 1)
        for l in range(2):
            picked = jnp.zeros((1, D), F32)
            for p in range(PANELS):
                picked = picked + jnp.where(lax.div(me, per) == p, shifted[12 * l + 8 + p : 12 * l + 9 + p, :], 0.0)
            get(o_upb)[l : l + 1, :] = picked[:, :wide]
        copy.wait()
        get(o_lout)[mine] = get(h_lmem)[...]

    return tuple(kn.run(body, "finish", cost(1e6, 16 * MIB)))


def swap(x, axis, b):
    n = lax.axis_size(axis)
    return lax.ppermute(x, axis, [(i, i ^ b) for i in range(n)])


def natural(both, order, rows_each):
    mats = both.shape[0]
    both = both.reshape(mats, 2, 2, 2, 2, 2, rows_each, both.shape[-1])
    at = {step: 1 + i for i, step in enumerate(bits_of(order))}
    return both.transpose(0, at[Z_FAR], at[Z_NEAR], at[ALONG_X], at[CORE], 6, at[ALONG_Y], 7)


def to_sequences(x, side, parts):
    own = x.shape[0] // parts
    mine = lax.dynamic_slice_in_dim(x, side * own, own, 0)
    other = swap(lax.dynamic_slice_in_dim(x, (1 - side) * own, own, 0), "seq", 1)
    return jnp.where(
        side == 0, jnp.concatenate([mine, other], axis=1), jnp.concatenate([other, mine], axis=1)
    )


def to_positions(x, side, parts, wire):
    own = x.shape[1] // parts
    mine = lax.dynamic_slice_in_dim(x, side * own, own, 1)
    other = swap(lax.dynamic_slice_in_dim(x, (1 - side) * own, own, 1).astype(wire), "seq", 1).astype(x.dtype)
    return jnp.where(
        side == 0, jnp.concatenate([mine, other], axis=0), jnp.concatenate([other, mine], axis=0)
    )


def elsewhere(att0, ffn0, att1, ffn1, smalls, n_rows, me):
    flat = lambda x: x.reshape(x.shape[0], -1, x.shape[-1] * x.shape[-2])
    rows = lambda x, order: flat(natural(x, order, ROW))
    total = lambda x: lax.psum(lax.psum_scatter(x, "rows", scatter_dimension=1, tiled=True).astype(F32), "seq")

    def quarter(f, at):
        return natural(f[at[0]], FFN_ORDERS[at[0]], ROW)[at[1] : at[1] + 1]

    def att(x, orders):
        qk, vp = (rows(b, o) for b, o in zip(x, orders))
        both = [jnp.concatenate([qk[2 * t : 2 * t + 2], vp[2 * t : 2 * t + 2]]) for t in range(BLOCKS)]
        return total(jnp.concatenate(both, axis=2))

    att0, att1 = att(att0, ATT_ORDERS[0]), att(att1, ATT_ORDERS[1])
    outs = [total(flat(quarter(f, OUT_AT))) for f in (ffn0, ffn1)]
    ups = [total(flat(jnp.concatenate([quarter(f, at) for at in UP_AT]))) for f in (ffn0, ffn1)]
    downs = [total(flat(jnp.concatenate([quarter(f, at) for at in DOWN_AT], axis=5))) for f in (ffn0, ffn1)]
    sums = lax.psum(smalls, ("rows", "seq")).reshape(2, -1, D)
    own = D // n_rows
    cut = lambda x: lax.dynamic_slice_in_dim(x, me * own, own, 2)
    upb = lax.dynamic_slice_in_dim(sums[:, 8:].reshape(2, FF), me * (FF // n_rows), FF // n_rows, 1)
    panels = lambda x: jnp.concatenate(list(x), axis=1)
    return (
        jnp.stack([att0[:3], att1[:3]]),
        jnp.concatenate(outs),
        jnp.stack([att0[3], att1[3]]),
        jnp.stack([panels(x) for x in ups]),
        jnp.concatenate(downs),
        cut(sums[:, 6:8]),
        upb,
        cut(sums[:, 0:2]),
        cut(sums[:, 2:4]),
        cut(sums[:, 4:6]),
    )


def on_device(
    tokens, lengths, key_mask, cotangent, w_qkv, w_out, w_pos, w_up, w_down, attn_bias, up_bias, norm_gain,
    norm_bias, out_bias,
):
    side = lax.axis_index("seq")
    parts = lax.axis_size("seq")
    n_rows = lax.axis_size("rows")
    me = lax.axis_index("rows")
    far = n_rows == SHARDS and parts == 2
    seqs = tokens.shape[0] // parts
    length = tokens.shape[1] * parts
    queries = length // 2
    flat = lambda x: x.reshape(-1, x.shape[-1])
    sets = lambda x: x.reshape(seqs, -1, D)

    if not far:
        tokens, cotangent = to_sequences(tokens, side, parts), to_sequences(cotangent, side, parts)
    start = prologue(far, 1, tokens, w_qkv, w_pos, attn_bias)
    tab0, tab1, enc0, enc1 = (start[n] for n in ("tab0", "tab1", "enc0", "enc1"))
    qw0, qr0, k0, v0 = sets(start["qw"]), sets(start["qr"]), start["k"], start["v"]
    mixed0, inv0, p0, *swapped = attn_fwd(2, lengths, key_mask, qw0, qr0, k0, v0, tab0, far, 6, cotangent)
    cot = swapped[0] if far else cotangent
    mixed0 = flat(mixed0)
    hid, x1, r1, act, slope, x2, r2, first, first_low, qw1, qr1, k1, v1 = ffn_fwd(
        mixed0, start["pooled"], w_out, w_up, w_down, w_qkv, attn_bias, up_bias, norm_gain, norm_bias, out_bias
    )
    qw1, qr1, k1, v1 = sets(qw1), sets(qr1), sets(k1), sets(v1)
    mixed1, inv1, p1 = attn_fwd(1, lengths, key_mask, qw1, qr1, k1, v1, tab1)
    mixed1 = flat(mixed1)
    lout, (dmixed1, dbranch1, dres1, small1, upg1), ffn1 = ffn_last(
        far, 2, mixed1, first, flat(cot), w_out, w_up, w_down, up_bias, norm_gain, norm_bias, out_bias
    )
    lout = sets(lout)
    plan = []
    if far:
        plan = [(x, order[1:3], False, {0: 0, 1: 8}) for x, order in zip(ffn1, FFN_ORDERS)]
    dfirst, dbias1, moved, att1, lout_got = back_layer(
        far, 3, 1, plan, p1, inv1, qw1, qr1, k1, v1, tab1, sets(dmixed1), dres1, w_qkv, first_low, first_low, enc1,
        lout=lout,
    )
    chains = []
    if far:
        for x, order in zip(moved, FFN_ORDERS):
            steps = order[3:]
            chains.append((x, steps, True, {k: k for k in range(1, len(steps) + 1)}))
        chains += [(x, order[1:3], False, {2: 1}) for x, order in zip(att1, ATT_ORDERS[1])]
    (dmixed0, dbranch0, dres0, small0, upg0), ffn0, moved = ffn_bwd(
        far, 4, chains, dfirst, x2, r2, hid, mixed0, x1, r1, norm_gain, w_out, w_up, w_down, act, slope
    )
    plan = []
    if far:
        when = ({0: 0, 1: 7, 2: 11}, {0: 0, 1: 7}, {0: 0, 1: 7, 2: 11})
        plan = [(x, order[1:], True, due) for x, order, due in zip(ffn0, FFN_ORDERS, when)]
        plan += [(x, order[3:], True, {0: 1, 1: 9}) for x, order in zip(moved[3:], ATT_ORDERS[1])]
    args = (p0, inv0, qw0, qr0, k0, v0, tab0, sets(dmixed0), dres0, w_qkv, start["low"], flat(start["tok"]), enc0)
    if far:
        dtok, got, sums, ended, att0 = back_layer(far, 5, 0, plan, *args, smalls=(small0, upg0, small1, upg1, dbias1))
        done = att0 + ended + moved[:3]
        return finish(done, sums, dtok, got, lout, lout_got)
    dtok, dbias0, _, att0, _ = back_layer(far, 5, 0, plan, *args)
    small = lambda s, u, b: jnp.concatenate([s[:6], b[:2], u[0].reshape(PANELS, D)], axis=0)
    smalls = jnp.concatenate([small(small0, upg0, dbias0), small(small1, upg1, dbias1)], axis=0)
    return (
        to_positions(lout, side, parts, BF),
        to_positions(sets(dtok), side, parts, BF),
        *elsewhere(att0, ffn0, att1, ffn1, smalls, n_rows, me),
    )


def solution(mesh):
    seq3 = P("rows", "seq", None)
    in_specs = (seq3, P("rows"), P("rows", None), seq3) + (P(),) * 10
    mat = P(None, "rows", None)
    vec = P(None, None, "rows")
    out_specs = (seq3, seq3, P(None, None, "rows", None), mat, mat, mat, mat, vec, P(None, "rows"), vec, vec, vec)
    return jax.shard_map(on_device, mesh=mesh, in_specs=in_specs, out_specs=out_specs, check_vma=False)
```
